32 devices in a mesh: dp: 8 (over z, x), expert: 4 (over y, core).
Axes of the slice: x: 2, y: 2, z: 4, core: 2. Of those that a mesh axis runs over, the one named last changes fastest.
Arguments:
- tokens_in: bfloat16 [2, 2048, 2048], P(None, 'dp', 'expert'), may hold values from -6 to 6
- teacher: bfloat16 [2, 2048, 2048], P(None, 'dp', 'expert'), may hold values from -6 to 6
- valid: int32 [2, 2048], P(None, 'dp'), may hold values from 0 to 1, as said below
- attn_routes: int32 [2, 2048, 2], P(None, 'dp'), may hold values from 0 to 3, all different within a row; in each aligned block of 256 rows (0 to 255, 256 to 511, ..., all dimensions but the last counted through in order) at most 144 rows name the same one
- attn_share: int32 [2, 2048, 2], P(None, 'dp'), may hold values from 1 to 7
- mlp_routes: int32 [2, 2048, 2], P(None, 'dp'), may hold values from 0 to 3, all different within a row; in each aligned block of 256 rows (0 to 255, 256 to 511, ..., all dimensions but the last counted through in order) at most 144 rows name the same one
- mlp_share: int32 [2, 2048, 2], P(None, 'dp'), may hold values from 1 to 7
- gains: float32 [2, 2048], replicated, may hold values from 0.5 to 1.5
- w_query: bfloat16 [4, 2048, 2048], P(None, 'dp', 'expert'), may hold values from -0.1875 to 0.1875
- w_out: bfloat16 [4, 2048, 2048], P(None, 'expert', 'dp'), may hold values from -0.875 to 0.875
- w_keyval: bfloat16 [2048, 2, 2048], P('dp', None, 'expert'), may hold values from -0.1875 to 0.1875
- w_gate: bfloat16 [4, 2048, 5632], P('expert', 'dp'), may hold values from -0.125 to 0.125
- w_up: bfloat16 [4, 2048, 5632], P('expert', 'dp'), may hold values from -0.125 to 0.125
- w_down: bfloat16 [4, 5632, 2048], P('expert', 'dp'), may hold values from -0.15625 to 0.15625
Outputs:
- layer_out: bfloat16 [2, 2048, 2048], P(None, 'dp', 'expert')
- loss: float32 [], replicated
- input_grad: float32 [2, 2048, 2048], P(None, 'dp', 'expert')
- gains_grad: float32 [2, 2048], replicated
- query_grad: float32 [4, 2048, 2048], P(None, 'dp', 'expert')
- out_grad: float32 [4, 2048, 2048], P(None, 'expert', 'dp')
- keyval_grad: float32 [2048, 2, 2048], P('dp', None, 'expert')
- gate_grad: float32 [4, 2048, 5632], P('expert', 'dp')
- up_grad: float32 [4, 2048, 5632], P('expert', 'dp')
- down_grad: float32 [4, 5632, 2048], P('expert', 'dp')
The draws below stay inside these ranges and needn't reach their ends.
Inputs may be any that keep to these rules, and one draw needn't show every extreme that they name: `attn_routes`: in every aligned block of 256 tokens (one index of dp in one micro-batch) no expert is named by more than 144 tokens; a token names 2 different experts. `mlp_routes`: in every aligned block of 256 tokens (one index of dp in one micro-batch) no expert is named by more than 144 tokens; a token names 2 different experts. `valid`: the last token of every block of 256 tokens counts.
All inputs are finite; a program needn't handle non-finite values.
Results may differ from the reference program's by a relative error of at most 0.018.
Values may be sent and summed in bfloat16 or wider, within the bound.
No kernel may reach another device: no remote copies, remote signals or barrier semaphores. Data moves between devices by JAX's collectives and lax.ppermute only.
A program may use at most 640 MiB of HBM per device.

```python
import math
import jax
import jax.numpy as jnp
import numpy as np
from jax import lax

D = 2048
QH = 16
KVH = 16
HEAD = 128
FF = 5632
TOPK = 2
MB = 2
PROMPT_DEV = 128
CLEN = 128
EXPERTS = 4
ROWS = 256
PLEN = 1024
TOKENS = 2048
CAP = 144
N_DP = 8


def draw_valid(key, part):
    whole = MB * TOKENS
    index = jnp.arange(whole, dtype=jnp.int32)
    blocks = TOKENS // ROWS
    block_of = index % TOKENS // ROWS
    limit = 250 + 650 * block_of // max(blocks - 1, 1)
    throw = jax.random.randint(key, (whole,), 0, 1000, dtype=jnp.int32)
    keep = (throw < limit) | (index % ROWS == ROWS - 1)
    return keep.astype(jnp.int32).reshape(MB, TOKENS)


def with_ends(entries, key, least, largest):
    index_at = [jax.random.randint(jax.random.fold_in(key, axis), (), 0, length) for axis, length in enumerate(entries.shape)]
    longest = entries.shape.index(max(entries.shape))
    neighbour = index_at[:longest] + [(index_at[longest] + 1) % entries.shape[longest]] + index_at[longest + 1:]
    return entries.at[tuple(index_at)].set(least).at[tuple(neighbour)].set(largest)


def shard_levels(stream_key, extent, split, least, high):
    factor_of = 1.0
    for position, shards_of in split:
        heights = jax.random.uniform(jax.random.fold_in(jax.random.fold_in(stream_key, 6), position), (shards_of,), jnp.float32, least / len(split), high / len(split))
        factor_of = factor_of * jnp.repeat(jnp.exp(heights), extent[position] // shards_of).reshape((-1,) + (1,) * (len(extent) - 1 - position))
    return factor_of


def routed_block(own_key, own, number, rows, amount, top, most, skew):
    order = jax.random.permutation(own_key, amount)
    crowded, common = load_shares(amount, rows * top, most, skew, True), load_shares(amount, rows * top, most, skew, False)
    places = jnp.arange(amount)

    def named(lengths, turn):
        used = int((lengths > 0).sum())
        fixed = max(1, used // 4)
        moved = fixed + (places - fixed + turn * (used - fixed)) % max(1, amount - fixed)
        return jnp.zeros((amount,), jnp.int32).at[order[jnp.where(places < fixed, places, moved)]].set(jnp.asarray(lengths, jnp.int32))

    lengths = jnp.where(number % 4 == 0, named(crowded, number // 4), named(common, number - number // 4 - 1))
    mixed = jax.random.permutation(jax.random.fold_in(own, 3), amount)
    donor, taker = mixed[0:amount // 2 * 2:2], mixed[1:amount // 2 * 2:2]
    slack = jnp.minimum(lengths[donor] - 1, most - lengths[taker]) // 2
    slack = jnp.where((donor == order[0]) | (taker == order[0]) | (lengths[taker] == 0), 0, jnp.maximum(slack, 0))
    moved = jax.random.randint(jax.random.fold_in(own, 4), (amount // 2,), 0, 1 << 20) % (slack + 1)
    lengths = lengths.at[donor].add(-moved).at[taker].add(moved)
    members = jnp.searchsorted(jnp.cumsum(lengths), jnp.arange(rows * top), side="right").astype(jnp.int32)
    grid = members.reshape(top, rows).T
    grid = grid[jax.random.permutation(jax.random.fold_in(own, 1), rows)]
    turn = jax.random.randint(jax.random.fold_in(own, 2), (rows, 1), 0, top)
    return jnp.take_along_axis(grid, (jnp.arange(top)[None, :] + turn) % top, axis=1)


def load_shares(number_of, total, reach, lean, full):
    portions = [(1 << 20) // math.isqrt(grade ** lean) + 1 for grade in range(1, number_of + 1)]
    largest = reach if full else min(reach, max(-(-total // number_of), total * portions[0] // sum(portions)))
    least = 1 if total - largest >= number_of - 1 else 0
    counts, spare = [largest] + [least] * (number_of - 1), total - largest - least * (number_of - 1)
    while spare > 0:
        movable = [i for i in range(1, number_of) if counts[i] < largest] or [i for i in range(1, number_of) if counts[i] < reach]
        whole, budget = sum([portions[i] for i in movable]), spare
        for i in movable:
            addition = min(reach - counts[i], max(1, budget * portions[i] // whole), spare)
            counts[i] = counts[i] + addition
            spare = spare - addition
    return np.array(counts)


def bell_draw(stream_key, dims, deviation, reach, split=(), kind=jnp.bfloat16):
    values = jax.random.normal(stream_key, dims, jnp.float32) * deviation
    if len(split) > 0:
        values = shard_levels(stream_key, dims, split, -0.22, 0.18) * values
    return jnp.clip(values, min=-reach, max=reach).astype(kind)


def setup_inputs(seed: int = 0) -> dict:
    splits = jax.random.split(jax.random.key(seed), 15)
    tokens_in = bell_draw(splits[0], (MB, TOKENS, D), 1.0, 6.0, ((1, 8), (2, 4)))
    teacher = bell_draw(splits[1], (MB, TOKENS, D), 1.0, 6.0, ((1, 8), (2, 4)))
    valid = draw_valid(jax.random.fold_in(splits[14], 71), 0)
    attn_routes_keys = jax.random.split(jax.random.fold_in(splits[3], 1), MB * TOKENS // ROWS)
    attn_routes_turns = jax.random.permutation(jax.random.fold_in(splits[3], 3), MB * TOKENS // ROWS)
    attn_routes = jax.vmap(lambda own, number: routed_block(jax.random.fold_in(splits[3], 2), own, number, ROWS, EXPERTS, TOPK, CAP, 2))(attn_routes_keys, attn_routes_turns).reshape((MB, TOKENS, TOPK))
    attn_share = with_ends(jax.random.randint(splits[4], (MB, TOKENS, TOPK), 1, 8), jax.random.fold_in(splits[4], 1), 1, 7).astype(jnp.int32)
    mlp_routes_keys = jax.random.split(jax.random.fold_in(splits[5], 1), MB * TOKENS // ROWS)
    mlp_routes_turns = jax.random.permutation(jax.random.fold_in(splits[5], 3), MB * TOKENS // ROWS)
    mlp_routes = jax.vmap(lambda own, number: routed_block(jax.random.fold_in(splits[5], 2), own, number, ROWS, EXPERTS, TOPK, CAP, 2))(mlp_routes_keys, mlp_routes_turns).reshape((MB, TOKENS, TOPK))
    mlp_share = with_ends(jax.random.randint(splits[6], (MB, TOKENS, TOPK), 1, 8), jax.random.fold_in(splits[6], 1), 1, 7).astype(jnp.int32)
    gains = jnp.clip(1.0 + 0.1 * jax.random.normal(splits[7], (2, D), jnp.float32), 0.5, 1.5)
    w_query = bell_draw(splits[8], (EXPERTS, D, QH * HEAD), (D // 2) ** -0.5, 0.1875, ((1, 8), (2, 4)))
    w_out = bell_draw(splits[9], (EXPERTS, QH * HEAD, D), (max(QH * HEAD // 40, 16)) ** -0.5, 0.875, ((1, 4), (2, 8)))
    w_keyval = bell_draw(splits[10], (D, 2, KVH * HEAD), (D // 2) ** -0.5, 0.1875, ((0, 8), (2, 4)))
    w_gate = bell_draw(splits[11], (EXPERTS, D, FF), D ** -0.5, 0.125, ((0, 4), (1, 8)))
    w_up = bell_draw(splits[12], (EXPERTS, D, FF), D ** -0.5, 0.125, ((0, 4), (1, 8)))
    w_down = bell_draw(splits[13], (EXPERTS, FF, D), (FF // 4) ** -0.5, 0.15625, ((0, 4), (1, 8)))
    return dict(tokens_in=tokens_in, teacher=teacher, valid=valid, attn_routes=attn_routes, attn_share=attn_share, mlp_routes=mlp_routes, mlp_share=mlp_share, gains=gains, w_query=w_query, w_out=w_out, w_keyval=w_keyval, w_gate=w_gate, w_up=w_up, w_down=w_down)


EPS = 1e-06
THETA = 10000.0
HIGH = lax.Precision.HIGHEST

@jax.custom_vjp
def low(v):
    return lax.optimization_barrier(v.astype(jnp.bfloat16)).astype(jnp.float32)

@jax.custom_vjp
def low_back(v):
    return v

def low_keep(v):
    return (low(v), None)

def low_pass(kept, grad):
    return (grad,)

def back_keep(v):
    return (v, None)

def back_low(kept, grad):
    return (low(grad),)
low.defvjp(low_keep, low_pass)
low_back.defvjp(back_keep, back_low)

def rotate(value, places):
    half = value.shape[-1] // 2
    kind = value.dtype
    ladder = jnp.arange(half).astype(kind) * (2.0 / value.shape[-1])
    freqs = jnp.power(jnp.asarray(THETA, kind), -ladder)
    angle = places.astype(kind)[:, None] * freqs[None, :]
    cosine = jnp.cos(angle)[:, None, :]
    sine = jnp.sin(angle)[:, None, :]
    first = value[..., :half]
    second = value[..., half:]
    return jnp.concatenate([first * cosine - second * sine, second * cosine + first * sine], axis=-1)

def rms_scale(field, gain):
    return field * lax.rsqrt(lax.optimization_barrier(jnp.mean(field * field, axis=-1, keepdims=True)) + EPS) * gain

def gate_table(route, share):
    shares = share.astype(jnp.float32)
    weight = shares / lax.optimization_barrier(jnp.sum(shares, axis=-1, keepdims=True))
    labels = jnp.arange(EXPERTS, dtype=jnp.int32)
    match = route[:, :, None] == labels[None, None, :]
    return lax.optimization_barrier(jnp.sum(jnp.where(match, weight[:, :, None], 0.0), axis=1))

def token_places():
    within = jnp.arange(ROWS, dtype=jnp.int32)
    blocks = jnp.arange(N_DP, dtype=jnp.int32)
    prompt_place = blocks[:, None] * PROMPT_DEV + within[None, :]
    cont_place = jnp.zeros((N_DP, 1), jnp.int32) + PLEN + within[None, :] - PROMPT_DEV
    return jnp.where(within[None, :] < PROMPT_DEV, prompt_place, cont_place).reshape(TOKENS)

def micro_forward(field, gain_pair, wq, wo, wkv, wg, wu, wd, attn_gate, mlp_gate):
    places = token_places()
    normed = low(rms_scale(field, gain_pair[0]))
    keyval = jnp.dot(normed, wkv.reshape(D, 2 * KVH * HEAD), precision=HIGH).reshape(TOKENS, 2, KVH, HEAD)
    keys = low(rotate(low_back(keyval[:, 0]), places))
    values = low_back(low(keyval[:, 1]))
    query_pre = jnp.einsum('td,edf->etf', normed, wq, precision=HIGH).reshape(EXPERTS, TOKENS, QH, HEAD)
    queries = low(jax.vmap(lambda v: rotate(v, places))(low_back(query_pre)))
    key_blocks = keys.reshape(N_DP, ROWS, KVH, HEAD)
    value_blocks = values.reshape(N_DP, ROWS, KVH, HEAD)
    prompt_keys = key_blocks[:, :PROMPT_DEV].reshape(PLEN, KVH, HEAD)
    prompt_values = value_blocks[:, :PROMPT_DEV].reshape(PLEN, KVH, HEAD)
    query_blocks = jnp.moveaxis(queries.reshape(EXPERTS, N_DP, ROWS, QH, HEAD), 1, 0)
    place_blocks = places.reshape(N_DP, ROWS)
    key_index = jnp.arange(PLEN + CLEN, dtype=jnp.int32)

    def one_block(pack):
        query_here, key_cont, value_cont, place_here = pack
        key_all = jnp.concatenate([prompt_keys, key_cont], axis=0)
        value_all = jnp.concatenate([prompt_values, value_cont], axis=0)
        scores = jnp.einsum('erhd,khd->ehrk', query_here, key_all, precision=HIGH) * HEAD ** (-0.5)
        seen = key_index[None, :] <= place_here[:, None]
        scores = low_back(jnp.where(seen[None, None], scores, -1e+30))
        attend = jax.nn.softmax(scores, axis=-1)
        mixed = jnp.einsum('ehrk,khd->erhd', low(attend), value_all, precision=HIGH)
        return low_back(low(mixed))
    mixed = lax.map(jax.checkpoint(one_block), (query_blocks, key_blocks[:, PROMPT_DEV:], value_blocks[:, PROMPT_DEV:], place_blocks))
    mixed = jnp.moveaxis(mixed, 0, 1).reshape(EXPERTS, TOKENS, QH * HEAD)
    project = low_back(jnp.einsum('etf,efd->etd', mixed, wo, precision=HIGH))
    hidden1 = field + lax.optimization_barrier(jnp.sum(attn_gate.T[:, :, None] * project, axis=0))
    normed2 = low(rms_scale(hidden1, gain_pair[1]))

    def expert_step(running, pack):
        gate_w, up_w, down_w, gate_col = pack
        gate_pre = low_back(jnp.dot(normed2, gate_w, precision=HIGH))
        up_pre = low_back(jnp.dot(normed2, up_w, precision=HIGH))
        inner = low(jax.nn.silu(gate_pre) * up_pre)
        result = low_back(jnp.dot(inner, down_w, precision=HIGH))
        return (running + gate_col[:, None] * result, None)
    feed, _ = lax.scan(jax.checkpoint(expert_step), jnp.zeros_like(hidden1), (wg, wu, wd, mlp_gate.T))
    return hidden1 + feed

def reference(tokens_in, teacher, valid, attn_routes, attn_share, mlp_routes, mlp_share, gains, w_query, w_out, w_keyval, w_gate, w_up, w_down):
    count = jnp.sum(valid).astype(jnp.float32)
    attn_gates = [gate_table(attn_routes[index], attn_share[index]) for index in range(MB)]
    mlp_gates = [gate_table(mlp_routes[index], mlp_share[index]) for index in range(MB)]

    def objective(field_all, gain_pair, wq, wo, wkv, wg, wu, wd):
        squared = jnp.zeros((), jnp.float32)
        results = []
        for index in range(MB):
            result = micro_forward(field_all[index], gain_pair, wq, wo, wkv, wg, wu, wd, attn_gates[index], mlp_gates[index])
            differ = result - teacher[index].astype(jnp.float32)
            squared = squared + jnp.sum(valid[index].astype(jnp.float32)[:, None] * differ * differ)
            results.append(result)
        return (squared / (count * D), jnp.stack(results))
    primals = (tokens_in.astype(jnp.float32), gains.astype(jnp.float32), w_query.astype(jnp.float32), w_out.astype(jnp.float32), w_keyval.astype(jnp.float32), w_gate.astype(jnp.float32), w_up.astype(jnp.float32), w_down.astype(jnp.float32))
    loss, pullback, results = jax.vjp(objective, *primals, has_aux=True)
    grads = pullback(jnp.asarray(D * MB * TOKENS / 2.0, jnp.float32))
    return (results.astype(jnp.bfloat16), loss, grads[0], grads[1], grads[2], grads[3], grads[4], grads[5], grads[6], grads[7])
```

```python
import jax
import jax.numpy as jnp
from jax import lax
from jax.sharding import Mesh
from jax.sharding import PartitionSpec as P

HEAD = 128
PROMPT_DEV = 128
CLEN = 128
CAP = 144


EPS = 1e-06
THETA = 10000.0
TRANS_DIMS = (((1,), (1,)), ((), ()))
ROWS_DIMS = (((0,), (0,)), ((), ()))


def rotate(value, places):
    half = value.shape[-1] // 2
    kind = value.dtype
    ladder = jnp.arange(half).astype(kind) * (2.0 / value.shape[-1])
    freqs = jnp.power(jnp.asarray(THETA, kind), -ladder)
    angle = places.astype(kind)[:, None] * freqs[None, :]
    cosine = jnp.cos(angle)[:, None, :]
    sine = jnp.sin(angle)[:, None, :]
    first = value[..., :half]
    second = value[..., half:]
    return jnp.concatenate(
        [first * cosine - second * sine, second * cosine + first * sine], axis=-1
    )


def rms_scale(field, gain):
    return field * lax.rsqrt(jnp.mean(field * field, axis=-1, keepdims=True) + EPS) * gain


def times_trans(left, right):
    return lax.dot_general(left, right, TRANS_DIMS, preferred_element_type=jnp.float32)


def times_rows(left, right):
    return lax.dot_general(left, right, ROWS_DIMS, preferred_element_type=jnp.float32)


def slot_plan(route, share, expert_id, slots):
    shares = share.astype(jnp.float32)
    weight = shares / jnp.sum(shares, axis=-1, keepdims=True)
    match = route == expert_id
    taken = jnp.any(match, axis=-1)
    gate_row = jnp.sum(jnp.where(match, weight, 0.0), axis=-1)
    order = jnp.cumsum(taken.astype(jnp.int32)) - 1
    placed = (order[None, :] == jnp.arange(slots, dtype=jnp.int32)[:, None]) & taken[None, :]
    row_index = jnp.arange(route.shape[0], dtype=jnp.int32)
    row_ids = jnp.sum(jnp.where(placed, row_index[None, :], 0), axis=1)
    filled = jnp.any(placed, axis=1)
    slot_gate = jnp.where(filled, gate_row[row_ids], 0.0)
    return (row_ids, slot_gate)


def per_device(
    tokens_in,
    teacher,
    valid,
    attn_routes,
    attn_share,
    mlp_routes,
    mlp_share,
    gains,
    w_query,
    w_out,
    w_keyval,
    w_gate,
    w_up,
    w_down,
):
    dp_count = lax.axis_size("dp")
    unit_index = lax.axis_index("dp")
    expert_index = lax.axis_index("expert")
    micro_count, row_count, local_width = tokens_in.shape
    full_width = local_width * lax.axis_size("expert")
    expert_count = w_query.shape[0]
    head_cols = w_query.shape[2]
    local_heads = head_cols // HEAD
    prompt_total = PROMPT_DEV * dp_count
    key_count = prompt_total + CLEN
    loss_scale = full_width * micro_count * row_count * dp_count / 2.0
    scale_root = HEAD ** (-0.5)
    within = jnp.arange(row_count, dtype=jnp.int32)
    places = jnp.where(
        within < PROMPT_DEV, unit_index * PROMPT_DEV + within, prompt_total + within - PROMPT_DEV
    )
    key_index = jnp.arange(key_count, dtype=jnp.int32)
    own_columns = jnp.arange(full_width, dtype=jnp.int32) // local_width == expert_index
    col_start = expert_index * local_width
    count = lax.psum(jnp.sum(valid).astype(jnp.float32), "dp")
    query_full, out_full, keyval_full = (
        lax.all_gather(w_query, "dp", axis=1, tiled=True),
        lax.all_gather(w_out, "dp", axis=2, tiled=True),
        lax.all_gather(w_keyval, "dp", axis=0, tiled=True),
    )
    keyval_flat = keyval_full.reshape(full_width, 2 * head_cols)
    held_query = jnp.zeros(query_full.shape, jnp.float32)
    held_out = jnp.zeros(out_full.shape, jnp.float32)
    held_keyval = jnp.zeros(keyval_full.shape, jnp.float32)
    held_gate = jnp.zeros((full_width, w_gate.shape[2]), jnp.float32)
    held_up = jnp.zeros((full_width, w_up.shape[2]), jnp.float32)
    held_down = jnp.zeros((w_down.shape[1] * dp_count, w_down.shape[2]), jnp.float32)
    gain_sum = jnp.zeros((2, full_width), jnp.float32)
    squared = jnp.zeros((), jnp.float32)
    results = []
    input_grads = []
    for micro_id in range(micro_count):
        field_low = lax.all_gather(tokens_in[micro_id], "expert", axis=1, tiled=True)
        field = field_low.astype(jnp.float32)
        normed1 = rms_scale(field, gains[0]).astype(jnp.bfloat16)
        keyval_pre = jnp.dot(normed1, keyval_flat, preferred_element_type=jnp.float32).reshape(
            row_count, 2, local_heads, HEAD
        )
        keys_here = rotate(keyval_pre[:, 0], places).astype(jnp.bfloat16)
        values_here = keyval_pre[:, 1].astype(jnp.bfloat16)
        pair_here = jnp.stack([keys_here, values_here], axis=1).reshape(row_count, 2, head_cols)
        prompt_pair = lax.all_gather(pair_here[:PROMPT_DEV], "dp", axis=0, tiled=True)
        pair_all = jnp.concatenate([prompt_pair, pair_here[PROMPT_DEV:]], axis=0).reshape(
            key_count, 2, local_heads, HEAD
        )
        keys_all = pair_all[:, 0]
        values_all = pair_all[:, 1]

        def score_block(query_rot, slot_places):
            raw = (
                jnp.einsum("chd,khd->hck", query_rot, keys_all, preferred_element_type=jnp.float32)
                * scale_root
            )
            seen = key_index[None, :] <= slot_places[:, None]
            return jnp.where(seen[None], raw, -1e30)

        attn_part = jnp.zeros((row_count, full_width), jnp.float32)
        kept = []
        for expert_id in range(expert_count):
            row_ids, slot_gate = slot_plan(
                attn_routes[micro_id], attn_share[micro_id], expert_id, CAP
            )
            chosen = jnp.take(normed1, row_ids, axis=0)
            slot_places = places[row_ids]
            query_pre = jnp.dot(
                chosen, query_full[expert_id], preferred_element_type=jnp.float32
            ).reshape(CAP, local_heads, HEAD)
            query_rot = rotate(query_pre, slot_places).astype(jnp.bfloat16)
            scores = score_block(query_rot, slot_places)
            peak = jnp.max(scores, axis=-1, keepdims=True)
            raised = jnp.exp(scores - peak)
            denom_sum = jnp.sum(raised, axis=-1, keepdims=True)
            attend = raised / denom_sum
            log_total = peak + jnp.log(denom_sum)
            mixed = jnp.einsum(
                "hck,khd->chd",
                attend.astype(jnp.bfloat16),
                values_all,
                preferred_element_type=jnp.float32,
            )
            mixed_low = mixed.reshape(CAP, head_cols).astype(jnp.bfloat16)
            project = jnp.dot(mixed_low, out_full[expert_id], preferred_element_type=jnp.float32)
            attn_part = attn_part.at[row_ids].add(project * slot_gate[:, None])
            kept.append(
                (
                    row_ids,
                    slot_gate,
                    chosen,
                    slot_places,
                    query_pre,
                    query_rot,
                    log_total,
                    mixed_low,
                )
            )
        attn_total = lax.psum(attn_part, "expert")
        hidden1 = field + attn_total
        normed2 = rms_scale(hidden1, gains[1]).astype(jnp.bfloat16)
        gate_full, up_full, down_full = (
            lax.all_gather(w_gate[0], "dp", axis=0, tiled=True),
            lax.all_gather(w_up[0], "dp", axis=0, tiled=True),
            lax.all_gather(w_down[0], "dp", axis=0, tiled=True),
        )
        feed_rows, feed_gate = slot_plan(
            mlp_routes[micro_id], mlp_share[micro_id], expert_index, CAP
        )
        feed_in = jnp.take(normed2, feed_rows, axis=0)
        gate_pre = jnp.dot(feed_in, gate_full, preferred_element_type=jnp.float32)
        up_pre = jnp.dot(feed_in, up_full, preferred_element_type=jnp.float32)
        inner = (jax.nn.silu(gate_pre) * up_pre).astype(jnp.bfloat16)
        feed_out = jnp.dot(inner, down_full, preferred_element_type=jnp.float32)
        feed_part = (
            jnp.zeros((row_count, full_width), jnp.float32)
            .at[feed_rows]
            .add(feed_out * feed_gate[:, None])
        )
        feed_shard = lax.psum_scatter(feed_part, "expert", scatter_dimension=1, tiled=True)
        hidden1_shard = lax.dynamic_slice_in_dim(hidden1, col_start, local_width, 1)
        result = hidden1_shard + feed_shard
        results.append(result.astype(jnp.bfloat16))
        differ = result - teacher[micro_id].astype(jnp.float32)
        counted = valid[micro_id].astype(jnp.float32)[:, None]
        squared = squared + jnp.sum(counted * differ * differ)
        grad_result = counted * differ * (2.0 * (loss_scale / (count * full_width)))
        grad_rows = lax.all_gather(grad_result, "expert", axis=1, tiled=True)
        gate_back, up_back, down_back = (
            lax.all_gather(w_gate[0], "dp", axis=0, tiled=True),
            lax.all_gather(w_up[0], "dp", axis=0, tiled=True),
            lax.all_gather(w_down[0], "dp", axis=0, tiled=True),
        )
        grad_feed = (jnp.take(grad_rows, feed_rows, axis=0) * feed_gate[:, None]).astype(
            jnp.bfloat16
        )
        grad_inner = times_trans(grad_feed, down_back)
        _, silu_back = jax.vjp(lambda left, right: jax.nn.silu(left) * right, gate_pre, up_pre)
        grad_gate_pre, grad_up_pre = silu_back(grad_inner)
        grad_gate_low = grad_gate_pre.astype(jnp.bfloat16)
        grad_up_low = grad_up_pre.astype(jnp.bfloat16)
        grad_feed_in = times_trans(grad_gate_low, gate_back) + times_trans(grad_up_low, up_back)
        held_gate = held_gate + times_rows(feed_in, grad_gate_low)
        held_up = held_up + times_rows(feed_in, grad_up_low)
        held_down = held_down + times_rows(inner, grad_feed)
        grad_norm2_part = (
            jnp.zeros((row_count, full_width), jnp.float32).at[feed_rows].add(grad_feed_in)
        )
        grad_norm2 = lax.psum(grad_norm2_part, "expert")
        _, norm2_back = jax.vjp(rms_scale, hidden1, gains[1])
        grad_hidden_norm, grad_gain2 = norm2_back(grad_norm2)
        grad_hidden1 = grad_rows + grad_hidden_norm
        grad_norm1_part = jnp.zeros((row_count, full_width), jnp.float32)
        grad_pair = jnp.zeros((key_count, 2, local_heads, HEAD), jnp.float32)
        term_query = []
        term_out = []
        for expert_id in range(expert_count):
            row_ids, slot_gate, chosen, slot_places, query_pre, query_rot, log_total, mixed_low = (
                kept[expert_id]
            )
            grad_project = (jnp.take(grad_hidden1, row_ids, axis=0) * slot_gate[:, None]).astype(
                jnp.bfloat16
            )
            grad_mixed = times_trans(grad_project, out_full[expert_id]).astype(jnp.bfloat16)
            term_out.append(times_rows(mixed_low, grad_project))
            grad_mixed = grad_mixed.reshape(CAP, local_heads, HEAD)
            scores = score_block(query_rot, slot_places)
            attend = jnp.exp(scores - log_total)
            attend_low = attend.astype(jnp.bfloat16)
            grad_attend = jnp.einsum(
                "chd,khd->hck", grad_mixed, values_all, preferred_element_type=jnp.float32
            )
            inner_sum = jnp.sum(attend * grad_attend, axis=-1, keepdims=True)
            grad_scores = (attend * (grad_attend - inner_sum)).astype(jnp.bfloat16)
            grad_query_rot = (
                jnp.einsum(
                    "hck,khd->chd", grad_scores, keys_all, preferred_element_type=jnp.float32
                )
                * scale_root
            )
            grad_keys = (
                jnp.einsum(
                    "hck,chd->khd", grad_scores, query_rot, preferred_element_type=jnp.float32
                )
                * scale_root
            )
            grad_values = jnp.einsum(
                "hck,chd->khd", attend_low, grad_mixed, preferred_element_type=jnp.float32
            )
            grad_pair = grad_pair + jnp.stack([grad_keys, grad_values], axis=1)
            _, query_back = jax.vjp(lambda value: rotate(value, slot_places), query_pre)
            grad_query_pre = (
                query_back(grad_query_rot)[0].astype(jnp.bfloat16).reshape(CAP, head_cols)
            )
            grad_norm1_part = grad_norm1_part.at[row_ids].add(
                times_trans(grad_query_pre, query_full[expert_id])
            )
            term_query.append(times_rows(chosen, grad_query_pre))
        grad_pair_flat = grad_pair.reshape(key_count, 2, head_cols)
        prompt_grad = lax.psum_scatter(
            grad_pair_flat[:prompt_total], "dp", scatter_dimension=0, tiled=True
        )
        pair_grad = jnp.concatenate([prompt_grad, grad_pair_flat[prompt_total:]], axis=0)
        _, key_back = jax.vjp(lambda value: rotate(value, places), keyval_pre[:, 0])
        grad_key_pre = key_back(pair_grad[:, 0].reshape(row_count, local_heads, HEAD))[0].reshape(
            row_count, head_cols
        )
        grad_pair_low = (
            jnp.stack([grad_key_pre, pair_grad[:, 1]], axis=1)
            .astype(jnp.bfloat16)
            .reshape(row_count, 2 * head_cols)
        )
        grad_norm1_part = grad_norm1_part + times_trans(grad_pair_low, keyval_flat)
        term_keyval = times_rows(normed1, grad_pair_low).reshape(full_width, 2, head_cols)
        grad_norm1 = lax.psum(grad_norm1_part.astype(jnp.bfloat16), "expert").astype(jnp.float32)
        _, norm1_back = jax.vjp(rms_scale, field, gains[0])
        grad_field_norm, grad_gain1 = norm1_back(grad_norm1)
        grad_field = grad_hidden1 + grad_field_norm
        input_grads.append(lax.dynamic_slice_in_dim(grad_field, col_start, local_width, 1))
        gain_sum = gain_sum + jnp.stack(
            [jnp.where(own_columns, grad_gain1, 0.0), jnp.where(own_columns, grad_gain2, 0.0)]
        )
        held_query = held_query + jnp.stack(term_query)
        held_out = held_out + jnp.stack(term_out)
        held_keyval = held_keyval + term_keyval
    grad_query, grad_out, grad_keyval, grad_gate, grad_up, grad_down = (
        lax.psum_scatter(
            held_query.astype(jnp.bfloat16), "dp", scatter_dimension=1, tiled=True
        ).astype(jnp.float32),
        lax.psum_scatter(
            held_out.astype(jnp.bfloat16), "dp", scatter_dimension=2, tiled=True
        ).astype(jnp.float32),
        lax.psum_scatter(
            held_keyval.astype(jnp.bfloat16), "dp", scatter_dimension=0, tiled=True
        ).astype(jnp.float32),
        lax.psum_scatter(
            held_gate.astype(jnp.bfloat16), "dp", scatter_dimension=0, tiled=True
        ).astype(jnp.float32),
        lax.psum_scatter(
            held_up.astype(jnp.bfloat16), "dp", scatter_dimension=0, tiled=True
        ).astype(jnp.float32),
        lax.psum_scatter(
            held_down.astype(jnp.bfloat16), "dp", scatter_dimension=0, tiled=True
        ).astype(jnp.float32),
    )
    gain_total, squared_total = lax.psum((gain_sum, squared), ("dp", "expert"))
    loss = squared_total / (count * full_width)
    return (
        jnp.stack(results),
        loss,
        jnp.stack(input_grads),
        gain_total,
        grad_query,
        grad_out,
        grad_keyval,
        grad_gate[None],
        grad_up[None],
        grad_down[None],
    )


def swap_pairs(size):
    return [(i, i ^ 1) for i in range(size)]


DEAL_FIRST = [(0, 0), (1, 2), (2, 1), (3, 3)]
DEAL_SECOND = [(0, 2), (1, 0), (2, 3), (3, 1)]
BACK_FIRST = [(b, a) for a, b in DEAL_FIRST]
BACK_SECOND = [(b, a) for a, b in DEAL_SECOND]
QUAD = ("y", "c")
TEAM = ("c", "dp")


def rope_tables(places):
    half = HEAD // 2
    ladder = jnp.arange(half).astype(jnp.float32) * (2.0 / HEAD)
    freqs = jnp.power(jnp.asarray(THETA, jnp.float32), -ladder)
    angle = places.astype(jnp.float32)[:, None] * freqs[None, :]
    return jnp.cos(angle), jnp.sin(angle)


def turn(value, cosine, sine):
    half = value.shape[-1] // 2
    first = value[..., :half]
    second = value[..., half:]
    return jnp.concatenate(
        [first * cosine - second * sine, second * cosine + first * sine], axis=-1
    )


def root_of(field):
    return lax.rsqrt(jnp.mean(field * field, axis=-1, keepdims=True) + EPS)


def norm_back(field, gain, grad):
    root = root_of(field)
    scaled = grad * gain
    along = jnp.sum(scaled * field, axis=-1, keepdims=True) / field.shape[-1]
    return root * scaled - field * (root * root * root) * along, jnp.sum(grad * field * root, axis=0)


def gate_rows(route, share, expert_count):
    shares = share.astype(jnp.float32)
    weight = shares / jnp.sum(shares, axis=-1, keepdims=True)
    labels = jnp.arange(expert_count, dtype=jnp.int32)
    match = route[None, :, :] == labels[:, None, None]
    return jnp.sum(jnp.where(match, weight[None], 0.0), axis=-1)


def dot(left, right):
    return jnp.dot(left, right, preferred_element_type=jnp.float32)


def team_device(
    tokens_in,
    teacher,
    valid,
    attn_routes,
    attn_share,
    mlp_routes,
    mlp_share,
    gains,
    w_query,
    w_out,
    w_keyval,
    w_gate,
    w_up,
    w_down,
):
    low = jnp.bfloat16
    units = lax.axis_size("dp")
    plane = lax.axis_index("y")
    core = lax.axis_index("c")
    micro_count, row_count, local_width = tokens_in.shape
    half = row_count // 2
    width = local_width * 4
    team_rows = 2 * units * half
    prompt_total = units * half
    expert_count = w_query.shape[0]
    local_heads = w_query.shape[2] // HEAD
    depth = w_query.shape[1]
    hidden = w_down.shape[1]
    loss_scale = width * micro_count * row_count * units / 2.0
    scale_root = HEAD ** (-0.5)

    def to_rows(value):
        parts = value.reshape(4, half, local_width)
        got = lax.all_to_all(parts, QUAD, 0, 0, tiled=True)
        return got.transpose(1, 0, 2).reshape(half, width)

    def from_rows(value):
        parts = value.reshape(half, 4, local_width).transpose(1, 0, 2)
        got = lax.all_to_all(parts, QUAD, 0, 0, tiled=True)
        return got.reshape(micro_count, row_count, local_width)

    def collect(value):
        return lax.all_gather(value, TEAM, axis=0, tiled=True)

    def deliver(value):
        return lax.psum_scatter(value.astype(low), TEAM, scatter_dimension=0, tiled=True).astype(
            jnp.float32
        )

    def mine(value):
        return lax.dynamic_index_in_dim(value, plane, 0, keepdims=False)

    field = to_rows(tokens_in).astype(jnp.float32)
    goal = to_rows(teacher).astype(jnp.float32)
    normed1 = collect((field * root_of(field) * gains[0]).astype(low))

    query_part = w_query.reshape(expert_count, depth, local_heads, HEAD).transpose(1, 2, 0, 3)
    out_part = w_out.reshape(expert_count, local_heads, HEAD, depth).transpose(3, 1, 0, 2)
    pair_part = w_keyval.reshape(depth, 2, local_heads, HEAD).transpose(0, 2, 1, 3)
    wide = expert_count * HEAD
    packed = jnp.concatenate(
        [
            query_part.reshape(depth, local_heads, wide),
            pair_part.reshape(depth, local_heads, 2 * HEAD),
            out_part.reshape(depth, local_heads, wide),
        ],
        axis=2,
    )
    lanes = packed.shape[2]
    packed = packed.reshape(2, depth // 2, local_heads, lanes).transpose(0, 2, 1, 3)
    kept_half = lax.dynamic_index_in_dim(packed, core, 0, keepdims=False)
    sent_half = lax.dynamic_index_in_dim(packed, 1 - core, 0, keepdims=False)
    got_half = lax.ppermute(sent_half, "c", swap_pairs(2))
    heads = jnp.concatenate(
        [
            jnp.where(core == 0, kept_half, got_half),
            jnp.where(core == 0, got_half, kept_half),
        ],
        axis=0,
    )
    heads = lax.all_to_all(heads, "dp", 0, 0, tiled=True)
    dealt_first = lax.ppermute(heads, QUAD, DEAL_FIRST)
    dealt_second = lax.ppermute(heads, QUAD, DEAL_SECOND)
    head_weights = jnp.stack(
        [
            jnp.where(plane == 0, dealt_first, dealt_second),
            jnp.where(plane == 0, dealt_second, dealt_first),
        ],
        axis=1,
    ).reshape(width, lanes)
    front_weights = head_weights[:, : wide + 2 * HEAD]
    out_weights = head_weights[:, wide + 2 * HEAD :]

    def spread(value):
        slabs = value.reshape(depth, units, hidden).transpose(1, 0, 2)
        return lax.all_to_all(slabs, "dp", 0, 0, tiled=True).reshape(width, hidden)

    def across(value):
        return lax.ppermute(value, "y", swap_pairs(2))

    down_own = w_down[0]
    down_far = across(down_own)
    gate_own = spread(w_gate[0])
    gate_far = across(gate_own)
    up_own = spread(w_up[0])
    up_far = across(up_own)

    gate_here = jnp.concatenate(
        [
            gate_rows(mine(attn_routes), mine(attn_share), expert_count),
            gate_rows(mine(mlp_routes), mine(mlp_share), expert_count),
        ],
        axis=0,
    )
    gate_all = lax.all_gather(gate_here, "dp", axis=0, tiled=False)
    gate_all = (
        gate_all.reshape(units, 2 * expert_count, 2, half)
        .transpose(1, 2, 0, 3)
        .reshape(2 * expert_count, team_rows)
    )
    attn_gate = gate_all[:expert_count].T
    feed_gate_own = lax.dynamic_index_in_dim(gate_all, expert_count + 2 * plane + core, 0, False)[:, None]
    feed_gate_far = lax.dynamic_index_in_dim(
        gate_all, expert_count + 2 * (1 - plane) + core, 0, False
    )[:, None]
    count = lax.psum(jnp.sum(valid).astype(jnp.float32), "dp")
    counted = lax.dynamic_slice_in_dim(mine(valid), core * half, half, 0).astype(jnp.float32)[:, None]

    index = jnp.arange(team_rows, dtype=jnp.int32)
    places = jnp.where(index < prompt_total, index, prompt_total + index % half)
    cosine, sine = rope_tables(places)

    front = dot(normed1, front_weights)
    query_rot = turn(
        front[:, :wide].reshape(team_rows, expert_count, HEAD), cosine[:, None], sine[:, None]
    ).astype(low)
    keys = turn(front[:, wide : wide + HEAD], cosine, sine).astype(low)
    values = front[:, wide + HEAD :].astype(low)
    prompt_keys, prompt_values = keys[:prompt_total], values[:prompt_total]
    tail_keys = keys[prompt_total:].reshape(units, half, HEAD)
    tail_values = values[prompt_total:].reshape(units, half, HEAD)
    prompt_query = query_rot[:prompt_total].transpose(1, 0, 2)
    tail_query = query_rot[prompt_total:].reshape(units, half, expert_count, HEAD).transpose(2, 0, 1, 3)

    def product(kind, left, right):
        return jnp.einsum(kind, left, right, preferred_element_type=jnp.float32)

    seen = index[None, :prompt_total] <= index[:prompt_total, None]
    prompt_score = jnp.where(
        seen, product("etd,kd->etk", prompt_query, prompt_keys) * scale_root, -1e30
    )
    tail_far = product("ejtd,kd->ejtk", tail_query, prompt_keys) * scale_root
    tail_near = jnp.where(
        seen[:half, :half], product("ejtd,jkd->ejtk", tail_query, tail_keys) * scale_root, -1e30
    )

    prompt_share = jax.nn.softmax(prompt_score, axis=-1)
    peak = jnp.maximum(
        jnp.max(tail_far, axis=-1, keepdims=True), jnp.max(tail_near, axis=-1, keepdims=True)
    )
    far_raised = jnp.exp(tail_far - peak)
    near_raised = jnp.exp(tail_near - peak)
    total = jnp.sum(far_raised, axis=-1, keepdims=True) + jnp.sum(near_raised, axis=-1, keepdims=True)
    far_share = far_raised / total
    near_share = near_raised / total
    prompt_mix = product("etk,kd->etd", prompt_share.astype(low), prompt_values)
    tail_mix = product("ejtk,kd->ejtd", far_share.astype(low), prompt_values) + product(
        "ejtk,jkd->ejtd", near_share.astype(low), tail_values
    )
    mixed = jnp.concatenate(
        [prompt_mix.transpose(1, 0, 2), tail_mix.transpose(1, 2, 0, 3).reshape(prompt_total, expert_count, HEAD)],
        axis=0,
    )
    mixed_low = (mixed * attn_gate[:, :, None]).astype(low).reshape(team_rows, wide)
    hidden1 = field + deliver(times_trans(mixed_low, out_weights))
    normed2 = collect((hidden1 * root_of(hidden1) * gains[1]).astype(low))

    sides = ((gate_own, up_own, down_own, feed_gate_own), (gate_far, up_far, down_far, feed_gate_far))
    feed_part = jnp.zeros((team_rows, width), jnp.float32)
    kept = []
    for gate_w, up_w, down_w, share_col in sides:
        gate_pre = dot(normed2, gate_w)
        up_pre = dot(normed2, up_w)
        inner = (jax.nn.silu(gate_pre) * up_pre * share_col).astype(low)
        feed_part = feed_part + dot(inner, down_w)
        kept.append((gate_pre, up_pre, inner))
    result = hidden1 + deliver(feed_part)
    layer_out = from_rows(result.astype(low))
    differ = result - goal
    squared = jnp.sum(counted * differ * differ)
    grad_result = counted * differ * (2.0 * (loss_scale / (count * width)))
    grad_rows = collect(grad_result.astype(low))

    grad_norm2_part = jnp.zeros((team_rows, width), jnp.float32)
    feed_grads = []
    for (gate_w, up_w, down_w, share_col), (gate_pre, up_pre, inner) in zip(sides, kept):
        grad_inner = times_trans(grad_rows, down_w) * share_col
        sigma = jax.nn.sigmoid(gate_pre)
        grad_gate = (grad_inner * up_pre * sigma * (1.0 + gate_pre * (1.0 - sigma))).astype(low)
        grad_up = (grad_inner * gate_pre * sigma).astype(low)
        grad_norm2_part = grad_norm2_part + times_trans(grad_gate, gate_w) + times_trans(grad_up, up_w)
        feed_grads.append((grad_gate, grad_up, inner))
    grad_norm2 = deliver(grad_norm2_part)
    grad_hidden_norm, grad_gain2 = norm_back(hidden1, gains[1], grad_norm2)
    grad_hidden1 = grad_result + grad_hidden_norm
    grad_hidden_rows = collect(grad_hidden1.astype(low))

    (grad_gate_own, grad_up_own, inner_own), (grad_gate_far, grad_up_far, inner_far) = feed_grads
    down_sum = times_rows(inner_own, grad_rows) + across(
        times_rows(inner_far, grad_rows).astype(low)
    ).astype(jnp.float32)
    gate_sum = times_rows(normed2, grad_gate_own) + across(
        times_rows(normed2, grad_gate_far).astype(low)
    ).astype(jnp.float32)
    up_sum = times_rows(normed2, grad_up_own) + across(
        times_rows(normed2, grad_up_far).astype(low)
    ).astype(jnp.float32)

    def gather_back(value):
        slabs = value.astype(low).reshape(units, depth, hidden)
        got = lax.all_to_all(slabs, "dp", 0, 0, tiled=True)
        return got.transpose(1, 0, 2).reshape(depth, units * hidden).astype(jnp.float32)

    grad_gate_out = gather_back(gate_sum)
    grad_up_out = gather_back(up_sum)

    grad_mixed = (
        dot(grad_hidden_rows, out_weights).reshape(team_rows, expert_count, HEAD) * attn_gate[:, :, None]
    ).astype(low)
    out_grad = times_rows(grad_hidden_rows, mixed_low)
    prompt_back = grad_mixed[:prompt_total].transpose(1, 0, 2)
    tail_back = grad_mixed[prompt_total:].reshape(units, half, expert_count, HEAD).transpose(2, 0, 1, 3)
    prompt_pull = product("etd,kd->etk", prompt_back, prompt_values)
    prompt_ds = (
        prompt_share * (prompt_pull - jnp.sum(prompt_share * prompt_pull, axis=-1, keepdims=True))
    ).astype(low)
    far_pull = product("ejtd,kd->ejtk", tail_back, prompt_values)
    near_pull = product("ejtd,jkd->ejtk", tail_back, tail_values)
    along = jnp.sum(far_share * far_pull, axis=-1, keepdims=True) + jnp.sum(
        near_share * near_pull, axis=-1, keepdims=True
    )
    far_ds = (far_share * (far_pull - along)).astype(low)
    near_ds = (near_share * (near_pull - along)).astype(low)
    prompt_dq = product("etk,kd->etd", prompt_ds, prompt_keys)
    tail_dq = product("ejtk,kd->ejtd", far_ds, prompt_keys) + product("ejtk,jkd->ejtd", near_ds, tail_keys)
    prompt_dk = product("etk,etd->kd", prompt_ds, prompt_query) + product(
        "ejtk,ejtd->kd", far_ds, tail_query
    )
    tail_dk = product("ejtk,ejtd->jkd", near_ds, tail_query)
    prompt_dv = product("etk,etd->kd", prompt_share.astype(low), prompt_back) + product(
        "ejtk,ejtd->kd", far_share.astype(low), tail_back
    )
    tail_dv = product("ejtk,ejtd->jkd", near_share.astype(low), tail_back)
    grad_query = (
        jnp.concatenate(
            [prompt_dq.transpose(1, 0, 2), tail_dq.transpose(1, 2, 0, 3).reshape(prompt_total, expert_count, HEAD)],
            axis=0,
        )
        * scale_root
    )
    grad_keys = jnp.concatenate([prompt_dk, tail_dk.reshape(prompt_total, HEAD)], axis=0) * scale_root
    grad_values = jnp.concatenate([prompt_dv, tail_dv.reshape(prompt_total, HEAD)], axis=0)
    front_back = jnp.concatenate(
        [
            turn(grad_query, cosine[:, None], -sine[:, None]).reshape(team_rows, wide),
            turn(grad_keys, cosine, -sine),
            grad_values,
        ],
        axis=1,
    ).astype(low)
    grad_norm1 = deliver(times_trans(front_back, front_weights))
    front_grad = times_rows(normed1, front_back)
    grad_field_norm, grad_gain1 = norm_back(field, gains[0], grad_norm1)
    input_grad = from_rows(grad_hidden1 + grad_field_norm)

    def send_back(value):
        columns = value.shape[1]
        halves = value.astype(low).reshape(units, 2, depth // 2, columns)
        first = lax.dynamic_index_in_dim(halves, plane, 1, keepdims=False)
        second = lax.dynamic_index_in_dim(halves, 1 - plane, 1, keepdims=False)
        both = lax.ppermute(first, QUAD, BACK_FIRST).astype(jnp.float32) + lax.ppermute(
            second, QUAD, BACK_SECOND
        ).astype(jnp.float32)
        got = lax.all_to_all(both.astype(low), "dp", 0, 0, tiled=True)
        got = got.reshape(2, local_heads, depth // 2, columns)
        own = lax.dynamic_index_in_dim(got, core, 0, keepdims=False)
        swapped = lax.ppermute(
            lax.dynamic_index_in_dim(got, 1 - core, 0, keepdims=False), "c", swap_pairs(2)
        )
        rows = jnp.concatenate(
            [jnp.where(core == 0, own, swapped), jnp.where(core == 0, swapped, own)], axis=1
        )
        return rows.astype(jnp.float32)

    out_back = send_back(out_grad)
    front_out = send_back(front_grad)
    grad_out = out_back.reshape(local_heads, depth, expert_count, HEAD).transpose(2, 0, 3, 1)
    grad_query_out = front_out[:, :, :wide].reshape(local_heads, depth, expert_count, HEAD).transpose(2, 1, 0, 3)
    grad_pair = front_out[:, :, wide:].reshape(local_heads, depth, 2, HEAD).transpose(1, 2, 0, 3)
    gain_total, squared_total = lax.psum(
        (jnp.stack([grad_gain1, grad_gain2]), squared), ("dp", "y", "c")
    )
    return (
        layer_out,
        squared_total / (count * width),
        input_grad,
        gain_total,
        grad_query_out.reshape(w_query.shape),
        grad_out.reshape(w_out.shape),
        grad_pair.reshape(w_keyval.shape),
        grad_gate_out[None],
        grad_up_out[None],
        down_sum[None],
    )


def solution(mesh):
    units, experts = mesh.shape["dp"], mesh.shape["expert"]

    def specs(quad):
        return (
            (
                P(None, "dp", quad),
                P(None, "dp", quad),
                P(None, "dp"),
                P(None, "dp", None),
                P(None, "dp", None),
                P(None, "dp", None),
                P(None, "dp", None),
                P(),
                P(None, "dp", quad),
                P(None, quad, "dp"),
                P("dp", None, quad),
                P(quad, "dp", None),
                P(quad, "dp", None),
                P(quad, "dp", None),
            ),
            (
                P(None, "dp", quad),
                P(),
                P(None, "dp", quad),
                P(),
                P(None, "dp", quad),
                P(None, quad, "dp"),
                P("dp", None, quad),
                P(quad, "dp", None),
                P(quad, "dp", None),
                P(quad, "dp", None),
            ),
        )

    def step(*arguments):
        tokens_in, w_query = arguments[0], arguments[8]
        team = (
            experts == 4
            and tokens_in.shape[0] == 2
            and w_query.shape[2] // HEAD == 2 * units
            and w_query.shape[0] == 4
            and tokens_in.shape[1] == units * 2 * PROMPT_DEV
            and PROMPT_DEV == CLEN
        )
        if team:
            grid = Mesh(mesh.devices.reshape(units, 2, 2), ("dp", "y", "c"))
            ins, outs = specs(QUAD)
            body = team_device
        else:
            grid = mesh
            ins, outs = specs("expert")
            body = per_device
        return jax.shard_map(body, mesh=grid, in_specs=ins, out_specs=outs, check_vma=False)(*arguments)

    return step
```

```python
import functools

import jax
import jax.numpy as jnp
from jax import lax
from jax.experimental import pallas as pl
from jax.experimental.pallas import tpu as pltpu
from jax.sharding import Mesh
from jax.sharding import PartitionSpec as P

HEAD = 128
PROMPT_DEV = 128
CLEN = 128
CAP = 144


EPS = 1e-06
THETA = 10000.0
TRANS_DIMS = (((1,), (1,)), ((), ()))
ROWS_DIMS = (((0,), (0,)), ((), ()))


def rotate(value, places):
    half = value.shape[-1] // 2
    kind = value.dtype
    ladder = jnp.arange(half).astype(kind) * (2.0 / value.shape[-1])
    freqs = jnp.power(jnp.asarray(THETA, kind), -ladder)
    angle = places.astype(kind)[:, None] * freqs[None, :]
    cosine = jnp.cos(angle)[:, None, :]
    sine = jnp.sin(angle)[:, None, :]
    first = value[..., :half]
    second = value[..., half:]
    return jnp.concatenate(
        [first * cosine - second * sine, second * cosine + first * sine], axis=-1
    )


def rms_scale(field, gain):
    return field * lax.rsqrt(jnp.mean(field * field, axis=-1, keepdims=True) + EPS) * gain


def times_trans(left, right):
    return lax.dot_general(left, right, TRANS_DIMS, preferred_element_type=jnp.float32)


def times_rows(left, right):
    return lax.dot_general(left, right, ROWS_DIMS, preferred_element_type=jnp.float32)


def slot_plan(route, share, expert_id, slots):
    shares = share.astype(jnp.float32)
    weight = shares / jnp.sum(shares, axis=-1, keepdims=True)
    match = route == expert_id
    taken = jnp.any(match, axis=-1)
    gate_row = jnp.sum(jnp.where(match, weight, 0.0), axis=-1)
    order = jnp.cumsum(taken.astype(jnp.int32)) - 1
    placed = (order[None, :] == jnp.arange(slots, dtype=jnp.int32)[:, None]) & taken[None, :]
    row_index = jnp.arange(route.shape[0], dtype=jnp.int32)
    row_ids = jnp.sum(jnp.where(placed, row_index[None, :], 0), axis=1)
    filled = jnp.any(placed, axis=1)
    slot_gate = jnp.where(filled, gate_row[row_ids], 0.0)
    return (row_ids, slot_gate)


def per_device(
    tokens_in,
    teacher,
    valid,
    attn_routes,
    attn_share,
    mlp_routes,
    mlp_share,
    gains,
    w_query,
    w_out,
    w_keyval,
    w_gate,
    w_up,
    w_down,
):
    dp_count = lax.axis_size("dp")
    unit_index = lax.axis_index("dp")
    expert_index = lax.axis_index("expert")
    micro_count, row_count, local_width = tokens_in.shape
    full_width = local_width * lax.axis_size("expert")
    expert_count = w_query.shape[0]
    head_cols = w_query.shape[2]
    local_heads = head_cols // HEAD
    prompt_total = PROMPT_DEV * dp_count
    key_count = prompt_total + CLEN
    loss_scale = full_width * micro_count * row_count * dp_count / 2.0
    scale_root = HEAD ** (-0.5)
    within = jnp.arange(row_count, dtype=jnp.int32)
    places = jnp.where(
        within < PROMPT_DEV, unit_index * PROMPT_DEV + within, prompt_total + within - PROMPT_DEV
    )
    key_index = jnp.arange(key_count, dtype=jnp.int32)
    own_columns = jnp.arange(full_width, dtype=jnp.int32) // local_width == expert_index
    col_start = expert_index * local_width
    count = lax.psum(jnp.sum(valid).astype(jnp.float32), "dp")
    query_full, out_full, keyval_full = (
        lax.all_gather(w_query, "dp", axis=1, tiled=True),
        lax.all_gather(w_out, "dp", axis=2, tiled=True),
        lax.all_gather(w_keyval, "dp", axis=0, tiled=True),
    )
    keyval_flat = keyval_full.reshape(full_width, 2 * head_cols)
    held_query = jnp.zeros(query_full.shape, jnp.float32)
    held_out = jnp.zeros(out_full.shape, jnp.float32)
    held_keyval = jnp.zeros(keyval_full.shape, jnp.float32)
    held_gate = jnp.zeros((full_width, w_gate.shape[2]), jnp.float32)
    held_up = jnp.zeros((full_width, w_up.shape[2]), jnp.float32)
    held_down = jnp.zeros((w_down.shape[1] * dp_count, w_down.shape[2]), jnp.float32)
    gain_sum = jnp.zeros((2, full_width), jnp.float32)
    squared = jnp.zeros((), jnp.float32)
    results = []
    input_grads = []
    for micro_id in range(micro_count):
        field_low = lax.all_gather(tokens_in[micro_id], "expert", axis=1, tiled=True)
        field = field_low.astype(jnp.float32)
        normed1 = rms_scale(field, gains[0]).astype(jnp.bfloat16)
        keyval_pre = jnp.dot(normed1, keyval_flat, preferred_element_type=jnp.float32).reshape(
            row_count, 2, local_heads, HEAD
        )
        keys_here = rotate(keyval_pre[:, 0], places).astype(jnp.bfloat16)
        values_here = keyval_pre[:, 1].astype(jnp.bfloat16)
        pair_here = jnp.stack([keys_here, values_here], axis=1).reshape(row_count, 2, head_cols)
        prompt_pair = lax.all_gather(pair_here[:PROMPT_DEV], "dp", axis=0, tiled=True)
        pair_all = jnp.concatenate([prompt_pair, pair_here[PROMPT_DEV:]], axis=0).reshape(
            key_count, 2, local_heads, HEAD
        )
        keys_all = pair_all[:, 0]
        values_all = pair_all[:, 1]

        def score_block(query_rot, slot_places):
            raw = (
                jnp.einsum("chd,khd->hck", query_rot, keys_all, preferred_element_type=jnp.float32)
                * scale_root
            )
            seen = key_index[None, :] <= slot_places[:, None]
            return jnp.where(seen[None], raw, -1e30)

        attn_part = jnp.zeros((row_count, full_width), jnp.float32)
        kept = []
        for expert_id in range(expert_count):
            row_ids, slot_gate = slot_plan(
                attn_routes[micro_id], attn_share[micro_id], expert_id, CAP
            )
            chosen = jnp.take(normed1, row_ids, axis=0)
            slot_places = places[row_ids]
            query_pre = jnp.dot(
                chosen, query_full[expert_id], preferred_element_type=jnp.float32
            ).reshape(CAP, local_heads, HEAD)
            query_rot = rotate(query_pre, slot_places).astype(jnp.bfloat16)
            scores = score_block(query_rot, slot_places)
            peak = jnp.max(scores, axis=-1, keepdims=True)
            raised = jnp.exp(scores - peak)
            denom_sum = jnp.sum(raised, axis=-1, keepdims=True)
            attend = raised / denom_sum
            log_total = peak + jnp.log(denom_sum)
            mixed = jnp.einsum(
                "hck,khd->chd",
                attend.astype(jnp.bfloat16),
                values_all,
                preferred_element_type=jnp.float32,
            )
            mixed_low = mixed.reshape(CAP, head_cols).astype(jnp.bfloat16)
            project = jnp.dot(mixed_low, out_full[expert_id], preferred_element_type=jnp.float32)
            attn_part = attn_part.at[row_ids].add(project * slot_gate[:, None])
            kept.append(
                (
                    row_ids,
                    slot_gate,
                    chosen,
                    slot_places,
                    query_pre,
                    query_rot,
                    log_total,
                    mixed_low,
                )
            )
        attn_total = lax.psum(attn_part, "expert")
        hidden1 = field + attn_total
        normed2 = rms_scale(hidden1, gains[1]).astype(jnp.bfloat16)
        gate_full, up_full, down_full = (
            lax.all_gather(w_gate[0], "dp", axis=0, tiled=True),
            lax.all_gather(w_up[0], "dp", axis=0, tiled=True),
            lax.all_gather(w_down[0], "dp", axis=0, tiled=True),
        )
        feed_rows, feed_gate = slot_plan(
            mlp_routes[micro_id], mlp_share[micro_id], expert_index, CAP
        )
        feed_in = jnp.take(normed2, feed_rows, axis=0)
        gate_pre = jnp.dot(feed_in, gate_full, preferred_element_type=jnp.float32)
        up_pre = jnp.dot(feed_in, up_full, preferred_element_type=jnp.float32)
        inner = (jax.nn.silu(gate_pre) * up_pre).astype(jnp.bfloat16)
        feed_out = jnp.dot(inner, down_full, preferred_element_type=jnp.float32)
        feed_part = (
            jnp.zeros((row_count, full_width), jnp.float32)
            .at[feed_rows]
            .add(feed_out * feed_gate[:, None])
        )
        feed_shard = lax.psum_scatter(feed_part, "expert", scatter_dimension=1, tiled=True)
        hidden1_shard = lax.dynamic_slice_in_dim(hidden1, col_start, local_width, 1)
        result = hidden1_shard + feed_shard
        results.append(result.astype(jnp.bfloat16))
        differ = result - teacher[micro_id].astype(jnp.float32)
        counted = valid[micro_id].astype(jnp.float32)[:, None]
        squared = squared + jnp.sum(counted * differ * differ)
        grad_result = counted * differ * (2.0 * (loss_scale / (count * full_width)))
        grad_rows = lax.all_gather(grad_result, "expert", axis=1, tiled=True)
        gate_back, up_back, down_back = (
            lax.all_gather(w_gate[0], "dp", axis=0, tiled=True),
            lax.all_gather(w_up[0], "dp", axis=0, tiled=True),
            lax.all_gather(w_down[0], "dp", axis=0, tiled=True),
        )
        grad_feed = (jnp.take(grad_rows, feed_rows, axis=0) * feed_gate[:, None]).astype(
            jnp.bfloat16
        )
        grad_inner = times_trans(grad_feed, down_back)
        _, silu_back = jax.vjp(lambda left, right: jax.nn.silu(left) * right, gate_pre, up_pre)
        grad_gate_pre, grad_up_pre = silu_back(grad_inner)
        grad_gate_low = grad_gate_pre.astype(jnp.bfloat16)
        grad_up_low = grad_up_pre.astype(jnp.bfloat16)
        grad_feed_in = times_trans(grad_gate_low, gate_back) + times_trans(grad_up_low, up_back)
        held_gate = held_gate + times_rows(feed_in, grad_gate_low)
        held_up = held_up + times_rows(feed_in, grad_up_low)
        held_down = held_down + times_rows(inner, grad_feed)
        grad_norm2_part = (
            jnp.zeros((row_count, full_width), jnp.float32).at[feed_rows].add(grad_feed_in)
        )
        grad_norm2 = lax.psum(grad_norm2_part, "expert")
        _, norm2_back = jax.vjp(rms_scale, hidden1, gains[1])
        grad_hidden_norm, grad_gain2 = norm2_back(grad_norm2)
        grad_hidden1 = grad_rows + grad_hidden_norm
        grad_norm1_part = jnp.zeros((row_count, full_width), jnp.float32)
        grad_pair = jnp.zeros((key_count, 2, local_heads, HEAD), jnp.float32)
        term_query = []
        term_out = []
        for expert_id in range(expert_count):
            row_ids, slot_gate, chosen, slot_places, query_pre, query_rot, log_total, mixed_low = (
                kept[expert_id]
            )
            grad_project = (jnp.take(grad_hidden1, row_ids, axis=0) * slot_gate[:, None]).astype(
                jnp.bfloat16
            )
            grad_mixed = times_trans(grad_project, out_full[expert_id]).astype(jnp.bfloat16)
            term_out.append(times_rows(mixed_low, grad_project))
            grad_mixed = grad_mixed.reshape(CAP, local_heads, HEAD)
            scores = score_block(query_rot, slot_places)
            attend = jnp.exp(scores - log_total)
            attend_low = attend.astype(jnp.bfloat16)
            grad_attend = jnp.einsum(
                "chd,khd->hck", grad_mixed, values_all, preferred_element_type=jnp.float32
            )
            inner_sum = jnp.sum(attend * grad_attend, axis=-1, keepdims=True)
            grad_scores = (attend * (grad_attend - inner_sum)).astype(jnp.bfloat16)
            grad_query_rot = (
                jnp.einsum(
                    "hck,khd->chd", grad_scores, keys_all, preferred_element_type=jnp.float32
                )
                * scale_root
            )
            grad_keys = (
                jnp.einsum(
                    "hck,chd->khd", grad_scores, query_rot, preferred_element_type=jnp.float32
                )
                * scale_root
            )
            grad_values = jnp.einsum(
                "hck,chd->khd", attend_low, grad_mixed, preferred_element_type=jnp.float32
            )
            grad_pair = grad_pair + jnp.stack([grad_keys, grad_values], axis=1)
            _, query_back = jax.vjp(lambda value: rotate(value, slot_places), query_pre)
            grad_query_pre = (
                query_back(grad_query_rot)[0].astype(jnp.bfloat16).reshape(CAP, head_cols)
            )
            grad_norm1_part = grad_norm1_part.at[row_ids].add(
                times_trans(grad_query_pre, query_full[expert_id])
            )
            term_query.append(times_rows(chosen, grad_query_pre))
        grad_pair_flat = grad_pair.reshape(key_count, 2, head_cols)
        prompt_grad = lax.psum_scatter(
            grad_pair_flat[:prompt_total], "dp", scatter_dimension=0, tiled=True
        )
        pair_grad = jnp.concatenate([prompt_grad, grad_pair_flat[prompt_total:]], axis=0)
        _, key_back = jax.vjp(lambda value: rotate(value, places), keyval_pre[:, 0])
        grad_key_pre = key_back(pair_grad[:, 0].reshape(row_count, local_heads, HEAD))[0].reshape(
            row_count, head_cols
        )
        grad_pair_low = (
            jnp.stack([grad_key_pre, pair_grad[:, 1]], axis=1)
            .astype(jnp.bfloat16)
            .reshape(row_count, 2 * head_cols)
        )
        grad_norm1_part = grad_norm1_part + times_trans(grad_pair_low, keyval_flat)
        term_keyval = times_rows(normed1, grad_pair_low).reshape(full_width, 2, head_cols)
        grad_norm1 = lax.psum(grad_norm1_part.astype(jnp.bfloat16), "expert").astype(jnp.float32)
        _, norm1_back = jax.vjp(rms_scale, field, gains[0])
        grad_field_norm, grad_gain1 = norm1_back(grad_norm1)
        grad_field = grad_hidden1 + grad_field_norm
        input_grads.append(lax.dynamic_slice_in_dim(grad_field, col_start, local_width, 1))
        gain_sum = gain_sum + jnp.stack(
            [jnp.where(own_columns, grad_gain1, 0.0), jnp.where(own_columns, grad_gain2, 0.0)]
        )
        held_query = held_query + jnp.stack(term_query)
        held_out = held_out + jnp.stack(term_out)
        held_keyval = held_keyval + term_keyval
    grad_query, grad_out, grad_keyval, grad_gate, grad_up, grad_down = (
        lax.psum_scatter(
            held_query.astype(jnp.bfloat16), "dp", scatter_dimension=1, tiled=True
        ).astype(jnp.float32),
        lax.psum_scatter(
            held_out.astype(jnp.bfloat16), "dp", scatter_dimension=2, tiled=True
        ).astype(jnp.float32),
        lax.psum_scatter(
            held_keyval.astype(jnp.bfloat16), "dp", scatter_dimension=0, tiled=True
        ).astype(jnp.float32),
        lax.psum_scatter(
            held_gate.astype(jnp.bfloat16), "dp", scatter_dimension=0, tiled=True
        ).astype(jnp.float32),
        lax.psum_scatter(
            held_up.astype(jnp.bfloat16), "dp", scatter_dimension=0, tiled=True
        ).astype(jnp.float32),
        lax.psum_scatter(
            held_down.astype(jnp.bfloat16), "dp", scatter_dimension=0, tiled=True
        ).astype(jnp.float32),
    )
    gain_total, squared_total = lax.psum((gain_sum, squared), ("dp", "expert"))
    loss = squared_total / (count * full_width)
    return (
        jnp.stack(results),
        loss,
        jnp.stack(input_grads),
        gain_total,
        grad_query,
        grad_out,
        grad_keyval,
        grad_gate[None],
        grad_up[None],
        grad_down[None],
    )


def swap_pairs(size):
    return [(i, i ^ 1) for i in range(size)]


DEAL_FIRST = [(0, 0), (1, 2), (2, 1), (3, 3)]
DEAL_SECOND = [(0, 2), (1, 0), (2, 3), (3, 1)]
BACK_FIRST = [(b, a) for a, b in DEAL_FIRST]
BACK_SECOND = [(b, a) for a, b in DEAL_SECOND]
QUAD = ("y", "c")
TEAM = ("c", "dp")


def rope_tables(places):
    half = HEAD // 2
    ladder = jnp.arange(half).astype(jnp.float32) * (2.0 / HEAD)
    freqs = jnp.power(jnp.asarray(THETA, jnp.float32), -ladder)
    angle = places.astype(jnp.float32)[:, None] * freqs[None, :]
    return jnp.cos(angle), jnp.sin(angle)


def turn(value, cosine, sine):
    half = value.shape[-1] // 2
    first = value[..., :half]
    second = value[..., half:]
    return jnp.concatenate(
        [first * cosine - second * sine, second * cosine + first * sine], axis=-1
    )


def root_of(field):
    return lax.rsqrt(jnp.mean(field * field, axis=-1, keepdims=True) + EPS)


def norm_back(field, gain, grad):
    root = root_of(field)
    scaled = grad * gain
    along = jnp.sum(scaled * field, axis=-1, keepdims=True) / field.shape[-1]
    return root * scaled - field * (root * root * root) * along, jnp.sum(grad * field * root, axis=0)


def gate_rows(route, share, expert_count):
    shares = share.astype(jnp.float32)
    weight = shares / jnp.sum(shares, axis=-1, keepdims=True)
    labels = jnp.arange(expert_count, dtype=jnp.int32)
    match = route[None, :, :] == labels[:, None, None]
    return jnp.sum(jnp.where(match, weight[None], 0.0), axis=-1)


def dot(left, right):
    return jnp.dot(left, right, preferred_element_type=jnp.float32)


BLOCK = 128
MASKED = -1e30
NT_DIMS = (((1,), (1,)), ((), ()))
ROOM = 56 * 1024 * 1024


def nt(left, right):
    return lax.dot_general(left, right, NT_DIMS, preferred_element_type=jnp.float32)


def spin(value, cosine, sine):
    return value * cosine + pltpu.roll(value, HEAD // 2, 1) * sine


def stack_experts(block, count):
    return jnp.concatenate([block[:, e * HEAD : (e + 1) * HEAD] for e in range(count)], axis=0)


def near_mask(columns):
    key_at = lax.broadcasted_iota(jnp.int32, (BLOCK, columns), 0)
    row_at = lax.broadcasted_iota(jnp.int32, (BLOCK, columns), 1) % BLOCK
    return key_at <= row_at


def attend_kernel(
    prompts, experts, front, cosine, sine, gate, mixed, query_out, pair_out, log_out, key_far, value_far
):
    step = pl.program_id(0)
    wide = experts * HEAD
    scale = HEAD ** (-0.5)

    @pl.when(step == 0)
    def _():
        key_far[...] = jnp.zeros_like(key_far)
        value_far[...] = jnp.zeros_like(value_far)

    cos, sin = cosine[...], sine[...]
    key = spin(front[:, wide : wide + HEAD], cos, sin).astype(jnp.bfloat16)
    value_up = front[:, wide + HEAD : wide + 2 * HEAD].T.astype(jnp.bfloat16)
    pair_out[:, :HEAD] = key
    pair_out[:, HEAD:] = front[:, wide + HEAD : wide + 2 * HEAD].astype(jnp.bfloat16)
    for e in range(experts):
        query_out[:, e * HEAD : (e + 1) * HEAD] = spin(
            front[:, e * HEAD : (e + 1) * HEAD], cos, sin
        ).astype(jnp.bfloat16)
    query = stack_experts(query_out[...], experts)
    near = jnp.where(near_mask(wide), nt(key, query) * scale, MASKED)
    far_tiles = jnp.minimum(step, prompts)

    def finish(width):
        far = nt(key_far[:width, :], query) * scale
        key_at = lax.broadcasted_iota(jnp.int32, far.shape, 0)
        far = jnp.where(key_at < far_tiles * BLOCK, far, MASKED)
        peak = jnp.maximum(
            jnp.max(far, axis=0, keepdims=True), jnp.max(near, axis=0, keepdims=True)
        )
        far = jnp.exp(far - peak)
        close = jnp.exp(near - peak)
        total = jnp.sum(far, axis=0, keepdims=True) + jnp.sum(close, axis=0, keepdims=True)
        mix = jnp.dot(
            value_far[:, :width], far.astype(jnp.bfloat16), preferred_element_type=jnp.float32
        ) + jnp.dot(value_up, close.astype(jnp.bfloat16), preferred_element_type=jnp.float32)
        mix = mix * (gate[0] / total)
        log_out[0] = peak + jnp.log(total)
        for e in range(experts):
            mixed[:, e * HEAD : (e + 1) * HEAD] = mix[:, e * BLOCK : (e + 1) * BLOCK].T.astype(
                jnp.bfloat16
            )

    split = prompts // 2

    @pl.when(step <= split)
    def _():
        finish(split * BLOCK)

    @pl.when(step > split)
    def _():
        finish(prompts * BLOCK)

    @pl.when(step < prompts)
    def _():
        at = pl.multiple_of(step * BLOCK, BLOCK)
        key_far[pl.ds(at, BLOCK), :] = key
        value_far[:, pl.ds(at, BLOCK)] = value_up


def attend(front, cosine, sine, gate, prompts, experts):
    rows, lanes = front.shape
    blocks = rows // BLOCK
    wide = experts * HEAD
    at = lambda i: (i, 0)
    line = pl.BlockSpec((1, 1, experts * BLOCK), lambda i: (i, 0, 0))
    return pl.pallas_call(
        functools.partial(attend_kernel, prompts, experts),
        grid=(blocks,),
        in_specs=[
            pl.BlockSpec((BLOCK, lanes), at),
            pl.BlockSpec((BLOCK, HEAD), at),
            pl.BlockSpec((BLOCK, HEAD), at),
            line,
        ],
        out_specs=[
            pl.BlockSpec((BLOCK, wide), at),
            pl.BlockSpec((BLOCK, wide), at),
            pl.BlockSpec((BLOCK, 2 * HEAD), at),
            line,
        ],
        out_shape=[
            jax.ShapeDtypeStruct((rows, wide), jnp.bfloat16),
            jax.ShapeDtypeStruct((rows, wide), jnp.bfloat16),
            jax.ShapeDtypeStruct((rows, 2 * HEAD), jnp.bfloat16),
            jax.ShapeDtypeStruct((blocks, 1, experts * BLOCK), jnp.float32),
        ],
        scratch_shapes=[
            pltpu.VMEM((prompts * BLOCK, HEAD), jnp.bfloat16),
            pltpu.VMEM((HEAD, prompts * BLOCK), jnp.bfloat16),
        ],
        compiler_params=pltpu.CompilerParams(
            dimension_semantics=("arbitrary",), vmem_limit_bytes=ROOM
        ),
        cost_estimate=pl.CostEstimate(
            flops=4 * rows * experts * HEAD * prompts * BLOCK,
            transcendentals=rows * experts * prompts * BLOCK,
            bytes_accessed=rows * lanes * 8,
        ),
        name="attend",
    )(front, cosine, sine, gate)


def attend_back_kernel(
    prompts, experts, pull, gate, query_in, pair, pair_up, log_in, cosine, sine, back, grad_key, grad_value
):
    step = pl.program_id(0)
    wide = experts * HEAD
    scale = HEAD ** (-0.5)

    @pl.when(step == 0)
    def _():
        grad_key[...] = jnp.zeros_like(grad_key)
        grad_value[...] = jnp.zeros_like(grad_value)

    at = pl.multiple_of(step * BLOCK, BLOCK)
    here = pl.ds(at, BLOCK)
    query = stack_experts(query_in[...], experts)
    grads = jnp.concatenate(
        [
            (pull[:, e * HEAD : (e + 1) * HEAD] * gate[:, e : e + 1]).astype(jnp.bfloat16)
            for e in range(experts)
        ],
        axis=0,
    )
    level = log_in[0]
    near = jnp.where(
        near_mask(wide), jnp.exp(nt(pair[here, :HEAD], query) * scale - level), 0.0
    )
    near_pull = nt(pair[here, HEAD:], grads)
    far_tiles = jnp.minimum(step, prompts)

    def finish(width):
        far = jnp.exp(nt(pair[:width, :HEAD], query) * scale - level)
        key_at = lax.broadcasted_iota(jnp.int32, far.shape, 0)
        far = jnp.where(key_at < far_tiles * BLOCK, far, 0.0)
        far_pull = nt(pair[:width, HEAD:], grads)
        along = jnp.sum(far * far_pull, axis=0, keepdims=True) + jnp.sum(
            near * near_pull, axis=0, keepdims=True
        )
        far_ds = (far * (far_pull - along)).astype(jnp.bfloat16)
        near_ds = (near * (near_pull - along)).astype(jnp.bfloat16)
        turned = (
            jnp.dot(pair_up[:, :width], far_ds, preferred_element_type=jnp.float32)
            + jnp.dot(pair_up[:, here], near_ds, preferred_element_type=jnp.float32)
        ) * scale
        cos, sin = cosine[here, :], sine[here, :]
        for e in range(experts):
            back[here, e * HEAD : (e + 1) * HEAD] = spin(
                turned[:, e * BLOCK : (e + 1) * BLOCK].T, cos, -sin
            ).astype(jnp.bfloat16)
        grad_key[:width, :] += jnp.dot(far_ds, query, preferred_element_type=jnp.float32)
        grad_value[:width, :] += jnp.dot(
            far.astype(jnp.bfloat16), grads, preferred_element_type=jnp.float32
        )
        grad_key[here, :] += jnp.dot(near_ds, query, preferred_element_type=jnp.float32)
        grad_value[here, :] += jnp.dot(
            near.astype(jnp.bfloat16), grads, preferred_element_type=jnp.float32
        )

    split = prompts // 2

    @pl.when(step <= split)
    def _():
        finish(split * BLOCK)

    @pl.when(step > split)
    def _():
        finish(prompts * BLOCK)

    @pl.when(step == pl.num_programs(0) - 1)
    def _():
        back[:, wide : wide + HEAD] = spin(
            grad_key[...] * scale, cosine[...], -sine[...]
        ).astype(jnp.bfloat16)
        back[:, wide + HEAD :] = grad_value[...].astype(jnp.bfloat16)


def attend_back(pull, gate, query, pair, pair_up, log_total, cosine, sine, prompts, experts):
    rows, wide = query.shape
    blocks = rows // BLOCK
    at = lambda i: (i, 0)
    still = lambda i: (0, 0)
    line = pl.BlockSpec((1, 1, experts * BLOCK), lambda i: (i, 0, 0))
    return pl.pallas_call(
        functools.partial(attend_back_kernel, prompts, experts),
        grid=(blocks,),
        in_specs=[
            pl.BlockSpec((BLOCK, wide), at),
            pl.BlockSpec((BLOCK, experts), at),
            pl.BlockSpec((BLOCK, wide), at),
            pl.BlockSpec((rows, 2 * HEAD), still),
            pl.BlockSpec((HEAD, rows), still),
            line,
            pl.BlockSpec((rows, HEAD), still),
            pl.BlockSpec((rows, HEAD), still),
        ],
        out_specs=pl.BlockSpec((rows, wide + 2 * HEAD), still),
        out_shape=jax.ShapeDtypeStruct((rows, wide + 2 * HEAD), jnp.bfloat16),
        scratch_shapes=[
            pltpu.VMEM((rows, HEAD), jnp.float32),
            pltpu.VMEM((rows, HEAD), jnp.float32),
        ],
        compiler_params=pltpu.CompilerParams(
            dimension_semantics=("arbitrary",), vmem_limit_bytes=ROOM
        ),
        cost_estimate=pl.CostEstimate(
            flops=10 * rows * experts * HEAD * prompts * BLOCK,
            transcendentals=rows * experts * prompts * BLOCK,
            bytes_accessed=rows * wide * 12,
        ),
        name="attend_back",
    )(pull, gate, query, pair, pair_up, log_total, cosine, sine)


def team_device(
    tokens_in,
    teacher,
    valid,
    attn_routes,
    attn_share,
    mlp_routes,
    mlp_share,
    gains,
    w_query,
    w_out,
    w_keyval,
    w_gate,
    w_up,
    w_down,
):
    low = jnp.bfloat16
    units = lax.axis_size("dp")
    plane = lax.axis_index("y")
    core = lax.axis_index("c")
    micro_count, row_count, local_width = tokens_in.shape
    half = row_count // 2
    width = local_width * 4
    team_rows = 2 * units * half
    prompt_total = units * half
    expert_count = w_query.shape[0]
    local_heads = w_query.shape[2] // HEAD
    depth = w_query.shape[1]
    hidden = w_down.shape[1]
    loss_scale = width * micro_count * row_count * units / 2.0
    scale_root = HEAD ** (-0.5)

    def exchange(parts):
        spot = 2 * plane + core
        got = [lax.dynamic_index_in_dim(parts, spot, 0, keepdims=False)]
        for step in (1, 2, 3):
            part = lax.dynamic_index_in_dim(parts, spot ^ step, 0, keepdims=False)
            got.append(lax.ppermute(part, QUAD, [(p, p ^ step) for p in range(4)]))
        for step, flag in ((1, core), (2, plane)):
            got = [jnp.where(flag == 0, got[p], got[p ^ step]) for p in range(4)]
        return got

    def to_rows(value):
        return jnp.concatenate(exchange(value.reshape(4, half, local_width)), axis=1)

    def from_rows(value):
        got = exchange(value.reshape(half, 4, local_width).transpose(1, 0, 2))
        return jnp.stack(got).reshape(micro_count, row_count, local_width)

    def collect(value):
        return lax.all_gather(value, TEAM, axis=0, tiled=True)

    def deliver(value):
        return lax.psum_scatter(value.astype(low), TEAM, scatter_dimension=0, tiled=True).astype(
            jnp.float32
        )

    def mine(value):
        return lax.dynamic_index_in_dim(value, plane, 0, keepdims=False)

    field = to_rows(tokens_in).astype(jnp.float32)
    goal = to_rows(teacher).astype(jnp.float32)
    gate_here = jnp.concatenate(
        [
            gate_rows(mine(attn_routes), mine(attn_share), expert_count),
            gate_rows(mine(mlp_routes), mine(mlp_share), expert_count),
        ],
        axis=0,
    )
    tokens_here = jnp.full((1, row_count), jnp.sum(valid).astype(jnp.float32))
    gate_here = jnp.concatenate([gate_here, tokens_here], axis=0)
    slots = jnp.arange(units, dtype=jnp.int32)[:, None, None] == lax.axis_index("dp")
    gate_all = jnp.where(slots, gate_here[None], 0.0)
    reach = 1
    while reach < units:
        gate_all = gate_all + lax.ppermute(gate_all, "dp", [(i, i ^ reach) for i in range(units)])
        reach *= 2
    count = jnp.sum(gate_all[:, -1, 0])
    normed1 = (field * root_of(field) * gains[0]).astype(low)
    normed1, gate_all = lax.optimization_barrier((normed1, gate_all))
    normed1 = collect(normed1)

    query_part = w_query.reshape(expert_count, depth, local_heads, HEAD).transpose(1, 2, 0, 3)
    out_part = w_out.reshape(expert_count, local_heads, HEAD, depth).transpose(3, 1, 0, 2)
    pair_part = w_keyval.reshape(depth, 2, local_heads, HEAD).transpose(0, 2, 1, 3)
    wide = expert_count * HEAD
    def across(value):
        return lax.ppermute(value, "y", swap_pairs(2))

    def scatter_heads(value):
        lanes = value.shape[2]
        packed = value.reshape(2, depth // 2, local_heads, lanes).transpose(0, 2, 1, 3)
        kept_half = lax.dynamic_index_in_dim(packed, core, 0, keepdims=False)
        sent_half = lax.dynamic_index_in_dim(packed, 1 - core, 0, keepdims=False)
        got_half = lax.ppermute(sent_half, "c", swap_pairs(2))
        return jnp.concatenate(
            [
                jnp.where(core == 0, kept_half, got_half),
                jnp.where(core == 0, got_half, kept_half),
            ],
            axis=0,
        )

    def deal_heads(heads):
        first = lax.ppermute(heads, QUAD, DEAL_FIRST)
        second = lax.ppermute(heads, QUAD, DEAL_SECOND)
        return jnp.stack(
            [jnp.where(plane == 0, first, second), jnp.where(plane == 0, second, first)], axis=1
        ).reshape(width, heads.shape[2])

    def swap_all(value, *later):
        got = lax.all_to_all(value, "dp", 0, 0, tiled=True)
        return lax.optimization_barrier((got, *later))

    def slabs_of(value):
        return value.T.reshape(units, hidden, depth)

    down_own = w_down[0]
    down_far = across(down_own)
    front_heads = scatter_heads(
        jnp.concatenate(
            [
                query_part.reshape(depth, local_heads, wide),
                pair_part.reshape(depth, local_heads, 2 * HEAD),
            ],
            axis=2,
        )
    )
    out_heads = scatter_heads(out_part.reshape(depth, local_heads, wide))
    gate_slabs, up_slabs = slabs_of(w_gate[0]), slabs_of(w_up[0])
    front_heads, out_heads, down_far = swap_all(front_heads, out_heads, down_far)
    out_heads, gate_slabs = swap_all(out_heads, gate_slabs)
    front_weights = deal_heads(front_heads)
    gate_all = (
        gate_all[:, :-1].reshape(units, 2 * expert_count, 2, half)
        .transpose(1, 2, 0, 3)
        .reshape(2 * expert_count, team_rows)
    )
    feed_gate_own = lax.dynamic_index_in_dim(gate_all, expert_count + 2 * plane + core, 0, False)
    feed_gate_far = lax.dynamic_index_in_dim(gate_all, expert_count + 2 * (1 - plane) + core, 0, False)
    counted = lax.dynamic_slice_in_dim(mine(valid), core * half, half, 0).astype(jnp.float32)[:, None]

    normed1, gate_all, feed_gate_own, feed_gate_far, count, gate_slabs = lax.optimization_barrier(
        (normed1, gate_all, feed_gate_own, feed_gate_far, count, gate_slabs)
    )
    gate_slabs, up_slabs = swap_all(gate_slabs, up_slabs)
    gate_own = gate_slabs.transpose(1, 0, 2).reshape(hidden, width)
    gate_far = across(gate_own)
    attn_gate = gate_all[:expert_count].T
    blocks = team_rows // BLOCK
    gate_lines = (
        gate_all[:expert_count].reshape(expert_count, blocks, BLOCK).transpose(1, 0, 2)
    ).reshape(blocks, 1, expert_count * BLOCK)
    index = jnp.arange(team_rows, dtype=jnp.int32)
    places = jnp.where(index < prompt_total, index, prompt_total + index % half)
    cosine, sine = rope_tables(places)
    cosine = jnp.concatenate([cosine, cosine], axis=1)
    sine = jnp.concatenate([-sine, sine], axis=1)

    front = dot(normed1, front_weights)
    front, out_heads = lax.optimization_barrier((front, out_heads))
    out_weights = deal_heads(out_heads)
    mixed_low, query_rot, pair_rot, log_total = attend(
        front, cosine, sine, gate_lines, units, expert_count
    )
    mixed_low, gate_own, up_slabs = lax.optimization_barrier((mixed_low, gate_own, up_slabs))
    up_slabs = lax.all_to_all(up_slabs, "dp", 0, 0, tiled=True)
    up_own = up_slabs.transpose(1, 0, 2).reshape(hidden, width)
    up_far = across(up_own)
    attn_sum = deliver(times_trans(mixed_low, out_weights))
    attn_sum, up_own, gate_far = lax.optimization_barrier((attn_sum, up_own, gate_far))
    hidden1 = field + attn_sum
    normed2 = collect((hidden1 * root_of(hidden1) * gains[1]).astype(low))

    gate_w = jnp.concatenate([gate_own, gate_far], axis=0)
    up_w = jnp.concatenate([up_own, up_far], axis=0)
    down_w = jnp.concatenate([down_own, down_far], axis=0)
    lane = jnp.arange(2 * hidden, dtype=jnp.int32)[None, :]
    share_cols = jnp.where(lane < hidden, feed_gate_own[:, None], feed_gate_far[:, None])
    gate_pre = times_trans(normed2, gate_w)
    up_pre = times_trans(normed2, up_w)
    inner = (jax.nn.silu(gate_pre) * up_pre * share_cols).astype(low)
    feed_part = dot(inner, down_w)
    result = hidden1 + deliver(feed_part)
    layer_out = from_rows(result.astype(low))
    differ = result - goal
    squared = jnp.sum(counted * differ * differ)
    grad_result = counted * differ * (2.0 * (loss_scale / (count * width)))
    grad_rows = collect(grad_result.astype(low))

    grad_inner = times_trans(grad_rows, down_w) * share_cols
    sigma = jax.nn.sigmoid(gate_pre)
    grad_gate = (grad_inner * up_pre * sigma * (1.0 + gate_pre * (1.0 - sigma))).astype(low)
    grad_up = (grad_inner * gate_pre * sigma).astype(low)
    grad_norm2 = deliver(dot(grad_gate, gate_w) + dot(grad_up, up_w))

    def weight_sum(left, right):
        whole = times_rows(left, right)
        return whole[:hidden], whole[hidden:].astype(low)

    gate_near, gate_sent = weight_sum(grad_gate, normed2)
    gate_got = across(gate_sent)
    up_near, up_sent = weight_sum(grad_up, normed2)
    down_near, down_sent = weight_sum(inner, grad_rows)
    grad_norm2, gate_near, gate_got, up_near, up_sent, down_near, down_sent = (
        lax.optimization_barrier(
            (grad_norm2, gate_near, gate_got, up_near, up_sent, down_near, down_sent)
        )
    )
    up_got = across(up_sent)
    grad_hidden_norm, grad_gain2 = norm_back(hidden1, gains[1], grad_norm2)
    grad_hidden1 = grad_result + grad_hidden_norm
    grad_hidden_rows = collect(grad_hidden1.astype(low))

    def rows_for_owners(value):
        return value.astype(low).reshape(hidden, units, depth).transpose(1, 0, 2)

    def own_rows(value):
        return value.reshape(units * hidden, depth).T.astype(jnp.float32)

    gate_slabs = rows_for_owners(gate_near + gate_got.astype(jnp.float32))
    gate_slabs = lax.all_to_all(gate_slabs, "dp", 0, 0, tiled=True)
    grad_hidden_rows, up_got, down_sent, gate_slabs = lax.optimization_barrier(
        (grad_hidden_rows, up_got, down_sent, gate_slabs)
    )
    up_slabs = rows_for_owners(up_near + up_got.astype(jnp.float32))
    up_slabs = lax.all_to_all(up_slabs, "dp", 0, 0, tiled=True)
    down_got = across(down_sent)

    front_back = attend_back(
        dot(grad_hidden_rows, out_weights),
        attn_gate,
        query_rot,
        pair_rot,
        pair_rot[:, :HEAD].T,
        log_total,
        cosine,
        sine,
        units,
        expert_count,
    )
    front_back, up_slabs, down_got = lax.optimization_barrier((front_back, up_slabs, down_got))
    down_sum = down_near + down_got.astype(jnp.float32)
    out_grad = times_rows(grad_hidden_rows, mixed_low)
    grad_norm1 = deliver(times_trans(front_back, front_weights))
    front_grad = times_rows(normed1, front_back)
    grad_field_norm, grad_gain1 = norm_back(field, gains[0], grad_norm1)
    input_grad = from_rows(grad_hidden1 + grad_field_norm)

    def undeal_heads(value):
        halves = value.astype(low).reshape(units, 2, depth // 2, value.shape[1])
        first = lax.dynamic_index_in_dim(halves, plane, 1, keepdims=False)
        second = lax.dynamic_index_in_dim(halves, 1 - plane, 1, keepdims=False)
        both = lax.ppermute(first, QUAD, BACK_FIRST).astype(jnp.float32) + lax.ppermute(
            second, QUAD, BACK_SECOND
        ).astype(jnp.float32)
        return both.astype(low)

    def gather_heads(value):
        got = value.reshape(2, local_heads, depth // 2, value.shape[2])
        own = lax.dynamic_index_in_dim(got, core, 0, keepdims=False)
        swapped = lax.ppermute(
            lax.dynamic_index_in_dim(got, 1 - core, 0, keepdims=False), "c", swap_pairs(2)
        )
        rows = jnp.concatenate(
            [jnp.where(core == 0, own, swapped), jnp.where(core == 0, swapped, own)], axis=1
        )
        return rows.astype(jnp.float32)

    front_heads, out_heads = undeal_heads(front_grad), undeal_heads(out_grad)
    front_heads, out_heads = swap_all(front_heads, out_heads)
    out_heads = lax.all_to_all(out_heads, "dp", 0, 0, tiled=True)
    grad_gate_out, grad_up_out = own_rows(gate_slabs), own_rows(up_slabs)
    front_out, out_back = gather_heads(front_heads), gather_heads(out_heads)
    grad_out = out_back.reshape(local_heads, depth, expert_count, HEAD).transpose(2, 0, 3, 1)
    grad_query_out = front_out[:, :, :wide].reshape(local_heads, depth, expert_count, HEAD).transpose(2, 1, 0, 3)
    grad_pair = front_out[:, :, wide:].reshape(local_heads, depth, 2, HEAD).transpose(1, 2, 0, 3)
    totals = jnp.stack([grad_gain1, grad_gain2, jnp.full((width,), squared)])
    for axis, size in (("c", 2), ("y", 2), ("dp", units)):
        reach = 1
        while reach < size:
            totals = totals + lax.ppermute(totals, axis, [(i, i ^ reach) for i in range(size)])
            reach *= 2
    gain_total, squared_total = totals[:2], totals[2, 0]
    return (
        layer_out,
        squared_total / (count * width),
        input_grad,
        gain_total,
        grad_query_out.reshape(w_query.shape),
        grad_out.reshape(w_out.shape),
        grad_pair.reshape(w_keyval.shape),
        grad_gate_out[None],
        grad_up_out[None],
        down_sum[None],
    )


def solution(mesh):
    units, experts = mesh.shape["dp"], mesh.shape["expert"]

    def specs(quad):
        return (
            (
                P(None, "dp", quad),
                P(None, "dp", quad),
                P(None, "dp"),
                P(None, "dp", None),
                P(None, "dp", None),
                P(None, "dp", None),
                P(None, "dp", None),
                P(),
                P(None, "dp", quad),
                P(None, quad, "dp"),
                P("dp", None, quad),
                P(quad, "dp", None),
                P(quad, "dp", None),
                P(quad, "dp", None),
            ),
            (
                P(None, "dp", quad),
                P(),
                P(None, "dp", quad),
                P(),
                P(None, "dp", quad),
                P(None, quad, "dp"),
                P("dp", None, quad),
                P(quad, "dp", None),
                P(quad, "dp", None),
                P(quad, "dp", None),
            ),
        )

    def step(*arguments):
        tokens_in, w_query = arguments[0], arguments[8]
        team = (
            experts == 4
            and tokens_in.shape[0] == 2
            and w_query.shape[2] // HEAD == 2 * units
            and w_query.shape[0] == 4
            and tokens_in.shape[1] == units * 2 * PROMPT_DEV
            and PROMPT_DEV == CLEN
        )
        if team:
            grid = Mesh(mesh.devices.reshape(units, 2, 2), ("dp", "y", "c"))
            ins, outs = specs(QUAD)
            body = team_device
        else:
            grid = mesh
            ins, outs = specs("expert")
            body = per_device
        return jax.shard_map(body, mesh=grid, in_specs=ins, out_specs=outs, check_vma=False)(*arguments)

    return step
```

```python
import functools

import jax
import jax.numpy as jnp
from jax import lax
from jax.experimental import pallas as pl
from jax.experimental.pallas import tpu as pltpu
from jax.sharding import Mesh
from jax.sharding import PartitionSpec as P

HEAD = 128
PROMPT_DEV = 128
CLEN = 128
CAP = 144


EPS = 1e-06
THETA = 10000.0
TRANS_DIMS = (((1,), (1,)), ((), ()))
ROWS_DIMS = (((0,), (0,)), ((), ()))


def rotate(value, places):
    half = value.shape[-1] // 2
    kind = value.dtype
    ladder = jnp.arange(half).astype(kind) * (2.0 / value.shape[-1])
    freqs = jnp.power(jnp.asarray(THETA, kind), -ladder)
    angle = places.astype(kind)[:, None] * freqs[None, :]
    cosine = jnp.cos(angle)[:, None, :]
    sine = jnp.sin(angle)[:, None, :]
    first = value[..., :half]
    second = value[..., half:]
    return jnp.concatenate(
        [first * cosine - second * sine, second * cosine + first * sine], axis=-1
    )


def rms_scale(field, gain):
    return field * lax.rsqrt(jnp.mean(field * field, axis=-1, keepdims=True) + EPS) * gain


def times_trans(left, right):
    return lax.dot_general(left, right, TRANS_DIMS, preferred_element_type=jnp.float32)


def times_rows(left, right):
    return lax.dot_general(left, right, ROWS_DIMS, preferred_element_type=jnp.float32)


def slot_plan(route, share, expert_id, slots):
    shares = share.astype(jnp.float32)
    weight = shares / jnp.sum(shares, axis=-1, keepdims=True)
    match = route == expert_id
    taken = jnp.any(match, axis=-1)
    gate_row = jnp.sum(jnp.where(match, weight, 0.0), axis=-1)
    order = jnp.cumsum(taken.astype(jnp.int32)) - 1
    placed = (order[None, :] == jnp.arange(slots, dtype=jnp.int32)[:, None]) & taken[None, :]
    row_index = jnp.arange(route.shape[0], dtype=jnp.int32)
    row_ids = jnp.sum(jnp.where(placed, row_index[None, :], 0), axis=1)
    filled = jnp.any(placed, axis=1)
    slot_gate = jnp.where(filled, gate_row[row_ids], 0.0)
    return (row_ids, slot_gate)


def per_device(
    tokens_in,
    teacher,
    valid,
    attn_routes,
    attn_share,
    mlp_routes,
    mlp_share,
    gains,
    w_query,
    w_out,
    w_keyval,
    w_gate,
    w_up,
    w_down,
):
    dp_count = lax.axis_size("dp")
    unit_index = lax.axis_index("dp")
    expert_index = lax.axis_index("expert")
    micro_count, row_count, local_width = tokens_in.shape
    full_width = local_width * lax.axis_size("expert")
    expert_count = w_query.shape[0]
    head_cols = w_query.shape[2]
    local_heads = head_cols // HEAD
    prompt_total = PROMPT_DEV * dp_count
    key_count = prompt_total + CLEN
    loss_scale = full_width * micro_count * row_count * dp_count / 2.0
    scale_root = HEAD ** (-0.5)
    within = jnp.arange(row_count, dtype=jnp.int32)
    places = jnp.where(
        within < PROMPT_DEV, unit_index * PROMPT_DEV + within, prompt_total + within - PROMPT_DEV
    )
    key_index = jnp.arange(key_count, dtype=jnp.int32)
    own_columns = jnp.arange(full_width, dtype=jnp.int32) // local_width == expert_index
    col_start = expert_index * local_width
    count = lax.psum(jnp.sum(valid).astype(jnp.float32), "dp")
    query_full, out_full, keyval_full = (
        lax.all_gather(w_query, "dp", axis=1, tiled=True),
        lax.all_gather(w_out, "dp", axis=2, tiled=True),
        lax.all_gather(w_keyval, "dp", axis=0, tiled=True),
    )
    keyval_flat = keyval_full.reshape(full_width, 2 * head_cols)
    held_query = jnp.zeros(query_full.shape, jnp.float32)
    held_out = jnp.zeros(out_full.shape, jnp.float32)
    held_keyval = jnp.zeros(keyval_full.shape, jnp.float32)
    held_gate = jnp.zeros((full_width, w_gate.shape[2]), jnp.float32)
    held_up = jnp.zeros((full_width, w_up.shape[2]), jnp.float32)
    held_down = jnp.zeros((w_down.shape[1] * dp_count, w_down.shape[2]), jnp.float32)
    gain_sum = jnp.zeros((2, full_width), jnp.float32)
    squared = jnp.zeros((), jnp.float32)
    results = []
    input_grads = []
    for micro_id in range(micro_count):
        field_low = lax.all_gather(tokens_in[micro_id], "expert", axis=1, tiled=True)
        field = field_low.astype(jnp.float32)
        normed1 = rms_scale(field, gains[0]).astype(jnp.bfloat16)
        keyval_pre = jnp.dot(normed1, keyval_flat, preferred_element_type=jnp.float32).reshape(
            row_count, 2, local_heads, HEAD
        )
        keys_here = rotate(keyval_pre[:, 0], places).astype(jnp.bfloat16)
        values_here = keyval_pre[:, 1].astype(jnp.bfloat16)
        pair_here = jnp.stack([keys_here, values_here], axis=1).reshape(row_count, 2, head_cols)
        prompt_pair = lax.all_gather(pair_here[:PROMPT_DEV], "dp", axis=0, tiled=True)
        pair_all = jnp.concatenate([prompt_pair, pair_here[PROMPT_DEV:]], axis=0).reshape(
            key_count, 2, local_heads, HEAD
        )
        keys_all = pair_all[:, 0]
        values_all = pair_all[:, 1]

        def score_block(query_rot, slot_places):
            raw = (
                jnp.einsum("chd,khd->hck", query_rot, keys_all, preferred_element_type=jnp.float32)
                * scale_root
            )
            seen = key_index[None, :] <= slot_places[:, None]
            return jnp.where(seen[None], raw, -1e30)

        attn_part = jnp.zeros((row_count, full_width), jnp.float32)
        kept = []
        for expert_id in range(expert_count):
            row_ids, slot_gate = slot_plan(
                attn_routes[micro_id], attn_share[micro_id], expert_id, CAP
            )
            chosen = jnp.take(normed1, row_ids, axis=0)
            slot_places = places[row_ids]
            query_pre = jnp.dot(
                chosen, query_full[expert_id], preferred_element_type=jnp.float32
            ).reshape(CAP, local_heads, HEAD)
            query_rot = rotate(query_pre, slot_places).astype(jnp.bfloat16)
            scores = score_block(query_rot, slot_places)
            peak = jnp.max(scores, axis=-1, keepdims=True)
            raised = jnp.exp(scores - peak)
            denom_sum = jnp.sum(raised, axis=-1, keepdims=True)
            attend = raised / denom_sum
            log_total = peak + jnp.log(denom_sum)
            mixed = jnp.einsum(
                "hck,khd->chd",
                attend.astype(jnp.bfloat16),
                values_all,
                preferred_element_type=jnp.float32,
            )
            mixed_low = mixed.reshape(CAP, head_cols).astype(jnp.bfloat16)
            project = jnp.dot(mixed_low, out_full[expert_id], preferred_element_type=jnp.float32)
            attn_part = attn_part.at[row_ids].add(project * slot_gate[:, None])
            kept.append(
                (
                    row_ids,
                    slot_gate,
                    chosen,
                    slot_places,
                    query_pre,
                    query_rot,
                    log_total,
                    mixed_low,
                )
            )
        attn_total = lax.psum(attn_part, "expert")
        hidden1 = field + attn_total
        normed2 = rms_scale(hidden1, gains[1]).astype(jnp.bfloat16)
        gate_full, up_full, down_full = (
            lax.all_gather(w_gate[0], "dp", axis=0, tiled=True),
            lax.all_gather(w_up[0], "dp", axis=0, tiled=True),
            lax.all_gather(w_down[0], "dp", axis=0, tiled=True),
        )
        feed_rows, feed_gate = slot_plan(
            mlp_routes[micro_id], mlp_share[micro_id], expert_index, CAP
        )
        feed_in = jnp.take(normed2, feed_rows, axis=0)
        gate_pre = jnp.dot(feed_in, gate_full, preferred_element_type=jnp.float32)
        up_pre = jnp.dot(feed_in, up_full, preferred_element_type=jnp.float32)
        inner = (jax.nn.silu(gate_pre) * up_pre).astype(jnp.bfloat16)
        feed_out = jnp.dot(inner, down_full, preferred_element_type=jnp.float32)
        feed_part = (
            jnp.zeros((row_count, full_width), jnp.float32)
            .at[feed_rows]
            .add(feed_out * feed_gate[:, None])
        )
        feed_shard = lax.psum_scatter(feed_part, "expert", scatter_dimension=1, tiled=True)
        hidden1_shard = lax.dynamic_slice_in_dim(hidden1, col_start, local_width, 1)
        result = hidden1_shard + feed_shard
        results.append(result.astype(jnp.bfloat16))
        differ = result - teacher[micro_id].astype(jnp.float32)
        counted = valid[micro_id].astype(jnp.float32)[:, None]
        squared = squared + jnp.sum(counted * differ * differ)
        grad_result = counted * differ * (2.0 * (loss_scale / (count * full_width)))
        grad_rows = lax.all_gather(grad_result, "expert", axis=1, tiled=True)
        gate_back, up_back, down_back = (
            lax.all_gather(w_gate[0], "dp", axis=0, tiled=True),
            lax.all_gather(w_up[0], "dp", axis=0, tiled=True),
            lax.all_gather(w_down[0], "dp", axis=0, tiled=True),
        )
        grad_feed = (jnp.take(grad_rows, feed_rows, axis=0) * feed_gate[:, None]).astype(
            jnp.bfloat16
        )
        grad_inner = times_trans(grad_feed, down_back)
        _, silu_back = jax.vjp(lambda left, right: jax.nn.silu(left) * right, gate_pre, up_pre)
        grad_gate_pre, grad_up_pre = silu_back(grad_inner)
        grad_gate_low = grad_gate_pre.astype(jnp.bfloat16)
        grad_up_low = grad_up_pre.astype(jnp.bfloat16)
        grad_feed_in = times_trans(grad_gate_low, gate_back) + times_trans(grad_up_low, up_back)
        held_gate = held_gate + times_rows(feed_in, grad_gate_low)
        held_up = held_up + times_rows(feed_in, grad_up_low)
        held_down = held_down + times_rows(inner, grad_feed)
        grad_norm2_part = (
            jnp.zeros((row_count, full_width), jnp.float32).at[feed_rows].add(grad_feed_in)
        )
        grad_norm2 = lax.psum(grad_norm2_part, "expert")
        _, norm2_back = jax.vjp(rms_scale, hidden1, gains[1])
        grad_hidden_norm, grad_gain2 = norm2_back(grad_norm2)
        grad_hidden1 = grad_rows + grad_hidden_norm
        grad_norm1_part = jnp.zeros((row_count, full_width), jnp.float32)
        grad_pair = jnp.zeros((key_count, 2, local_heads, HEAD), jnp.float32)
        term_query = []
        term_out = []
        for expert_id in range(expert_count):
            row_ids, slot_gate, chosen, slot_places, query_pre, query_rot, log_total, mixed_low = (
                kept[expert_id]
            )
            grad_project = (jnp.take(grad_hidden1, row_ids, axis=0) * slot_gate[:, None]).astype(
                jnp.bfloat16
            )
            grad_mixed = times_trans(grad_project, out_full[expert_id]).astype(jnp.bfloat16)
            term_out.append(times_rows(mixed_low, grad_project))
            grad_mixed = grad_mixed.reshape(CAP, local_heads, HEAD)
            scores = score_block(query_rot, slot_places)
            attend = jnp.exp(scores - log_total)
            attend_low = attend.astype(jnp.bfloat16)
            grad_attend = jnp.einsum(
                "chd,khd->hck", grad_mixed, values_all, preferred_element_type=jnp.float32
            )
            inner_sum = jnp.sum(attend * grad_attend, axis=-1, keepdims=True)
            grad_scores = (attend * (grad_attend - inner_sum)).astype(jnp.bfloat16)
            grad_query_rot = (
                jnp.einsum(
                    "hck,khd->chd", grad_scores, keys_all, preferred_element_type=jnp.float32
                )
                * scale_root
            )
            grad_keys = (
                jnp.einsum(
                    "hck,chd->khd", grad_scores, query_rot, preferred_element_type=jnp.float32
                )
                * scale_root
            )
            grad_values = jnp.einsum(
                "hck,chd->khd", attend_low, grad_mixed, preferred_element_type=jnp.float32
            )
            grad_pair = grad_pair + jnp.stack([grad_keys, grad_values], axis=1)
            _, query_back = jax.vjp(lambda value: rotate(value, slot_places), query_pre)
            grad_query_pre = (
                query_back(grad_query_rot)[0].astype(jnp.bfloat16).reshape(CAP, head_cols)
            )
            grad_norm1_part = grad_norm1_part.at[row_ids].add(
                times_trans(grad_query_pre, query_full[expert_id])
            )
            term_query.append(times_rows(chosen, grad_query_pre))
        grad_pair_flat = grad_pair.reshape(key_count, 2, head_cols)
        prompt_grad = lax.psum_scatter(
            grad_pair_flat[:prompt_total], "dp", scatter_dimension=0, tiled=True
        )
        pair_grad = jnp.concatenate([prompt_grad, grad_pair_flat[prompt_total:]], axis=0)
        _, key_back = jax.vjp(lambda value: rotate(value, places), keyval_pre[:, 0])
        grad_key_pre = key_back(pair_grad[:, 0].reshape(row_count, local_heads, HEAD))[0].reshape(
            row_count, head_cols
        )
        grad_pair_low = (
            jnp.stack([grad_key_pre, pair_grad[:, 1]], axis=1)
            .astype(jnp.bfloat16)
            .reshape(row_count, 2 * head_cols)
        )
        grad_norm1_part = grad_norm1_part + times_trans(grad_pair_low, keyval_flat)
        term_keyval = times_rows(normed1, grad_pair_low).reshape(full_width, 2, head_cols)
        grad_norm1 = lax.psum(grad_norm1_part.astype(jnp.bfloat16), "expert").astype(jnp.float32)
        _, norm1_back = jax.vjp(rms_scale, field, gains[0])
        grad_field_norm, grad_gain1 = norm1_back(grad_norm1)
        grad_field = grad_hidden1 + grad_field_norm
        input_grads.append(lax.dynamic_slice_in_dim(grad_field, col_start, local_width, 1))
        gain_sum = gain_sum + jnp.stack(
            [jnp.where(own_columns, grad_gain1, 0.0), jnp.where(own_columns, grad_gain2, 0.0)]
        )
        held_query = held_query + jnp.stack(term_query)
        held_out = held_out + jnp.stack(term_out)
        held_keyval = held_keyval + term_keyval
    grad_query, grad_out, grad_keyval, grad_gate, grad_up, grad_down = (
        lax.psum_scatter(
            held_query.astype(jnp.bfloat16), "dp", scatter_dimension=1, tiled=True
        ).astype(jnp.float32),
        lax.psum_scatter(
            held_out.astype(jnp.bfloat16), "dp", scatter_dimension=2, tiled=True
        ).astype(jnp.float32),
        lax.psum_scatter(
            held_keyval.astype(jnp.bfloat16), "dp", scatter_dimension=0, tiled=True
        ).astype(jnp.float32),
        lax.psum_scatter(
            held_gate.astype(jnp.bfloat16), "dp", scatter_dimension=0, tiled=True
        ).astype(jnp.float32),
        lax.psum_scatter(
            held_up.astype(jnp.bfloat16), "dp", scatter_dimension=0, tiled=True
        ).astype(jnp.float32),
        lax.psum_scatter(
            held_down.astype(jnp.bfloat16), "dp", scatter_dimension=0, tiled=True
        ).astype(jnp.float32),
    )
    gain_total, squared_total = lax.psum((gain_sum, squared), ("dp", "expert"))
    loss = squared_total / (count * full_width)
    return (
        jnp.stack(results),
        loss,
        jnp.stack(input_grads),
        gain_total,
        grad_query,
        grad_out,
        grad_keyval,
        grad_gate[None],
        grad_up[None],
        grad_down[None],
    )


def swap_pairs(size):
    return [(i, i ^ 1) for i in range(size)]


DEAL_FIRST = [(0, 0), (1, 2), (2, 1), (3, 3)]
DEAL_SECOND = [(0, 2), (1, 0), (2, 3), (3, 1)]
BACK_FIRST = [(b, a) for a, b in DEAL_FIRST]
BACK_SECOND = [(b, a) for a, b in DEAL_SECOND]
QUAD = ("y", "c")
TEAM = ("c", "dp")


def rope_tables(places):
    half = HEAD // 2
    ladder = jnp.arange(half).astype(jnp.float32) * (2.0 / HEAD)
    freqs = jnp.power(jnp.asarray(THETA, jnp.float32), -ladder)
    angle = places.astype(jnp.float32)[:, None] * freqs[None, :]
    return jnp.cos(angle), jnp.sin(angle)


def turn(value, cosine, sine):
    half = value.shape[-1] // 2
    first = value[..., :half]
    second = value[..., half:]
    return jnp.concatenate(
        [first * cosine - second * sine, second * cosine + first * sine], axis=-1
    )


def root_of(field):
    return lax.rsqrt(jnp.mean(field * field, axis=-1, keepdims=True) + EPS)


def norm_back(field, gain, grad):
    root = root_of(field)
    scaled = grad * gain
    along = jnp.sum(scaled * field, axis=-1, keepdims=True) / field.shape[-1]
    return root * scaled - field * (root * root * root) * along, jnp.sum(grad * field * root, axis=0)


def gate_rows(route, share, expert_count):
    shares = share.astype(jnp.float32)
    weight = shares / jnp.sum(shares, axis=-1, keepdims=True)
    labels = jnp.arange(expert_count, dtype=jnp.int32)
    match = route[None, :, :] == labels[:, None, None]
    return jnp.sum(jnp.where(match, weight[None], 0.0), axis=-1)


def dot(left, right):
    return jnp.dot(left, right, preferred_element_type=jnp.float32)


BLOCK = 128
MASKED = -1e30
NT_DIMS = (((1,), (1,)), ((), ()))
ROOM = 56 * 1024 * 1024


def nt(left, right):
    return lax.dot_general(left, right, NT_DIMS, preferred_element_type=jnp.float32)


def spin(value, cosine, sine):
    return value * cosine + pltpu.roll(value, HEAD // 2, 1) * sine


def stack_experts(block, count):
    return jnp.concatenate([block[:, e * HEAD : (e + 1) * HEAD] for e in range(count)], axis=0)


def near_mask(columns):
    key_at = lax.broadcasted_iota(jnp.int32, (BLOCK, columns), 0)
    row_at = lax.broadcasted_iota(jnp.int32, (BLOCK, columns), 1) % BLOCK
    return key_at <= row_at


def attend_kernel(
    prompts, experts, front, cosine, sine, gate, mixed, query_out, pair_out, log_out, key_far, value_far
):
    step = pl.program_id(0)
    wide = experts * HEAD
    scale = HEAD ** (-0.5)

    @pl.when(step == 0)
    def _():
        key_far[...] = jnp.zeros_like(key_far)
        value_far[...] = jnp.zeros_like(value_far)

    cos, sin = cosine[...], sine[...]
    key = spin(front[:, wide : wide + HEAD], cos, sin).astype(jnp.bfloat16)
    value_up = front[:, wide + HEAD : wide + 2 * HEAD].T.astype(jnp.bfloat16)
    pair_out[:, :HEAD] = key
    pair_out[:, HEAD:] = front[:, wide + HEAD : wide + 2 * HEAD].astype(jnp.bfloat16)
    for e in range(experts):
        query_out[:, e * HEAD : (e + 1) * HEAD] = spin(
            front[:, e * HEAD : (e + 1) * HEAD], cos, sin
        ).astype(jnp.bfloat16)
    query = stack_experts(query_out[...], experts)
    near = jnp.where(near_mask(wide), nt(key, query) * scale, MASKED)
    far_tiles = jnp.minimum(step, prompts)

    def finish(width):
        far = nt(key_far[:width, :], query) * scale
        key_at = lax.broadcasted_iota(jnp.int32, far.shape, 0)
        far = jnp.where(key_at < far_tiles * BLOCK, far, MASKED)
        peak = jnp.maximum(
            jnp.max(far, axis=0, keepdims=True), jnp.max(near, axis=0, keepdims=True)
        )
        far = jnp.exp(far - peak)
        close = jnp.exp(near - peak)
        total = jnp.sum(far, axis=0, keepdims=True) + jnp.sum(close, axis=0, keepdims=True)
        mix = jnp.dot(
            value_far[:, :width], far.astype(jnp.bfloat16), preferred_element_type=jnp.float32
        ) + jnp.dot(value_up, close.astype(jnp.bfloat16), preferred_element_type=jnp.float32)
        mix = mix * (gate[0] / total)
        log_out[0] = peak + jnp.log(total)
        for e in range(experts):
            mixed[:, e * HEAD : (e + 1) * HEAD] = mix[:, e * BLOCK : (e + 1) * BLOCK].T.astype(
                jnp.bfloat16
            )

    split = prompts // 2

    @pl.when(step <= split)
    def _():
        finish(split * BLOCK)

    @pl.when(step > split)
    def _():
        finish(prompts * BLOCK)

    @pl.when(step < prompts)
    def _():
        at = pl.multiple_of(step * BLOCK, BLOCK)
        key_far[pl.ds(at, BLOCK), :] = key
        value_far[:, pl.ds(at, BLOCK)] = value_up


def attend(front, cosine, sine, gate, prompts, experts):
    rows, lanes = front.shape
    blocks = rows // BLOCK
    wide = experts * HEAD
    at = lambda i: (i, 0)
    line = pl.BlockSpec((1, 1, experts * BLOCK), lambda i: (i, 0, 0))
    return pl.pallas_call(
        functools.partial(attend_kernel, prompts, experts),
        grid=(blocks,),
        in_specs=[
            pl.BlockSpec((BLOCK, lanes), at),
            pl.BlockSpec((BLOCK, HEAD), at),
            pl.BlockSpec((BLOCK, HEAD), at),
            line,
        ],
        out_specs=[
            pl.BlockSpec((BLOCK, wide), at),
            pl.BlockSpec((BLOCK, wide), at),
            pl.BlockSpec((BLOCK, 2 * HEAD), at),
            line,
        ],
        out_shape=[
            jax.ShapeDtypeStruct((rows, wide), jnp.bfloat16),
            jax.ShapeDtypeStruct((rows, wide), jnp.bfloat16),
            jax.ShapeDtypeStruct((rows, 2 * HEAD), jnp.bfloat16),
            jax.ShapeDtypeStruct((blocks, 1, experts * BLOCK), jnp.float32),
        ],
        scratch_shapes=[
            pltpu.VMEM((prompts * BLOCK, HEAD), jnp.bfloat16),
            pltpu.VMEM((HEAD, prompts * BLOCK), jnp.bfloat16),
        ],
        compiler_params=pltpu.CompilerParams(
            dimension_semantics=("arbitrary",), vmem_limit_bytes=ROOM
        ),
        cost_estimate=pl.CostEstimate(
            flops=4 * rows * experts * HEAD * prompts * BLOCK,
            transcendentals=rows * experts * prompts * BLOCK,
            bytes_accessed=rows * lanes * 8,
        ),
        name="attend",
    )(front, cosine, sine, gate)


def attend_back_kernel(
    prompts, experts, pull, gate, query_in, pair, pair_up, log_in, cosine, sine, back, grad_key, grad_value
):
    step = pl.program_id(0)
    wide = experts * HEAD
    scale = HEAD ** (-0.5)

    @pl.when(step == 0)
    def _():
        grad_key[...] = jnp.zeros_like(grad_key)
        grad_value[...] = jnp.zeros_like(grad_value)

    at = pl.multiple_of(step * BLOCK, BLOCK)
    here = pl.ds(at, BLOCK)
    query = stack_experts(query_in[...], experts)
    grads = jnp.concatenate(
        [
            (pull[:, e * HEAD : (e + 1) * HEAD] * gate[:, e : e + 1]).astype(jnp.bfloat16)
            for e in range(experts)
        ],
        axis=0,
    )
    level = log_in[0]
    near = jnp.where(
        near_mask(wide), jnp.exp(nt(pair[here, :HEAD], query) * scale - level), 0.0
    )
    near_pull = nt(pair[here, HEAD:], grads)
    far_tiles = jnp.minimum(step, prompts)

    def finish(width):
        far = jnp.exp(nt(pair[:width, :HEAD], query) * scale - level)
        key_at = lax.broadcasted_iota(jnp.int32, far.shape, 0)
        far = jnp.where(key_at < far_tiles * BLOCK, far, 0.0)
        far_pull = nt(pair[:width, HEAD:], grads)
        along = jnp.sum(far * far_pull, axis=0, keepdims=True) + jnp.sum(
            near * near_pull, axis=0, keepdims=True
        )
        far_ds = (far * (far_pull - along)).astype(jnp.bfloat16)
        near_ds = (near * (near_pull - along)).astype(jnp.bfloat16)
        turned = (
            jnp.dot(pair_up[:, :width], far_ds, preferred_element_type=jnp.float32)
            + jnp.dot(pair_up[:, here], near_ds, preferred_element_type=jnp.float32)
        ) * scale
        cos, sin = cosine[here, :], sine[here, :]
        for e in range(experts):
            back[here, e * HEAD : (e + 1) * HEAD] = spin(
                turned[:, e * BLOCK : (e + 1) * BLOCK].T, cos, -sin
            ).astype(jnp.bfloat16)
        grad_key[:width, :] += jnp.dot(far_ds, query, preferred_element_type=jnp.float32)
        grad_value[:width, :] += jnp.dot(
            far.astype(jnp.bfloat16), grads, preferred_element_type=jnp.float32
        )
        grad_key[here, :] += jnp.dot(near_ds, query, preferred_element_type=jnp.float32)
        grad_value[here, :] += jnp.dot(
            near.astype(jnp.bfloat16), grads, preferred_element_type=jnp.float32
        )

    split = prompts // 2

    @pl.when(step <= split)
    def _():
        finish(split * BLOCK)

    @pl.when(step > split)
    def _():
        finish(prompts * BLOCK)

    @pl.when(step == pl.num_programs(0) - 1)
    def _():
        back[:, wide : wide + HEAD] = spin(
            grad_key[...] * scale, cosine[...], -sine[...]
        ).astype(jnp.bfloat16)
        back[:, wide + HEAD :] = grad_value[...].astype(jnp.bfloat16)


def attend_back(pull, gate, query, pair, pair_up, log_total, cosine, sine, prompts, experts):
    rows, wide = query.shape
    blocks = rows // BLOCK
    at = lambda i: (i, 0)
    still = lambda i: (0, 0)
    line = pl.BlockSpec((1, 1, experts * BLOCK), lambda i: (i, 0, 0))
    return pl.pallas_call(
        functools.partial(attend_back_kernel, prompts, experts),
        grid=(blocks,),
        in_specs=[
            pl.BlockSpec((BLOCK, wide), at),
            pl.BlockSpec((BLOCK, experts), at),
            pl.BlockSpec((BLOCK, wide), at),
            pl.BlockSpec((rows, 2 * HEAD), still),
            pl.BlockSpec((HEAD, rows), still),
            line,
            pl.BlockSpec((rows, HEAD), still),
            pl.BlockSpec((rows, HEAD), still),
        ],
        out_specs=pl.BlockSpec((rows, wide + 2 * HEAD), still),
        out_shape=jax.ShapeDtypeStruct((rows, wide + 2 * HEAD), jnp.bfloat16),
        scratch_shapes=[
            pltpu.VMEM((rows, HEAD), jnp.float32),
            pltpu.VMEM((rows, HEAD), jnp.float32),
        ],
        compiler_params=pltpu.CompilerParams(
            dimension_semantics=("arbitrary",), vmem_limit_bytes=ROOM
        ),
        cost_estimate=pl.CostEstimate(
            flops=10 * rows * experts * HEAD * prompts * BLOCK,
            transcendentals=rows * experts * prompts * BLOCK,
            bytes_accessed=rows * wide * 12,
        ),
        name="attend_back",
    )(pull, gate, query, pair, pair_up, log_total, cosine, sine)


LINE = 4
SIDES = [(i, i ^ 1) for i in range(2 * LINE)]


def hops(moves):
    return [(2 * a + x, 2 * b + x) for a, b in moves for x in (0, 1)]


def hold(*values):
    return lax.optimization_barrier(values)


def to_side(value):
    return lax.ppermute(value, "dp", SIDES)


def to_core(value):
    return lax.ppermute(value, "c", swap_pairs(2))


def scatter_run(make, given, fill=None):
    spot = lax.axis_index("dp") // 2
    low = jnp.bfloat16
    wide = lambda value: value.astype(jnp.float32)

    def rise(value, last):
        return lax.ppermute(value, "dp", hops([(a, a + 1) for a in range(last)]))

    def fall(value, last):
        return lax.ppermute(value, "dp", hops([(LINE - 1 - a, LINE - 2 - a) for a in range(last)]))

    def cut(value):
        middle = value.shape[0] // 2
        return value[:middle], value[middle:]

    here3, there3 = cut(make(3, *given))
    there3, *given = hold(there3, *given)
    got3, part2 = hold(to_core(there3), make(2, *given))
    here2, there2 = cut(part2)
    mine3, other3 = cut(here3 + got3)
    other3, there2, *given = hold(other3, there2, *given)
    side3, both2, part1 = hold(to_side(other3), here2 + to_core(there2), make(1, *given))
    here1, there1 = cut(part1)
    mine2, other2 = cut(both2)
    row3 = wide(mine3) + wide(side3)
    send3, other2, there1, *given = hold(row3.astype(low), other2, there1, *given)
    side2, up, down, both1, part0 = hold(
        to_side(other2), rise(send3, 1), fall(send3, 1), here1 + to_core(there1), make(0, *given)
    )
    here0, there0 = cut(part0)
    mine1, other1 = cut(both1)
    row2 = wide(mine2) + wide(side2)
    send_up = (jnp.where(spot == 0, row2, row3) + wide(up)).astype(low)
    send_down = (jnp.where(spot == LINE - 1, row2, row3) + wide(down)).astype(low)
    send_up, send_down, other1, there0, *given = hold(send_up, send_down, other1, there0, *given)
    side1, up, down, both0 = hold(
        to_side(other1), rise(send_up, 2), fall(send_down, 2), here0 + to_core(there0)
    )
    mine0, other0 = cut(both0)
    row1 = wide(mine1) + wide(side1)
    send_up = (jnp.where(spot == 1, row2, row1) + wide(up)).astype(low)
    send_down = (jnp.where(spot == LINE - 2, row2, row1) + wide(down)).astype(low)
    send_up, send_down, other0, *given = hold(send_up, send_down, other0, *given)
    filled = fill(*given) if fill else ()
    side0, up, down, filled = hold(to_side(other0), rise(send_up, 3), fall(send_down, 3), filled)
    total = wide(mine0) + wide(side0) + wide(up) + wide(down)
    return (total, filled) if fill else total


LANE_STEP = 512


def product_kernel(terms, places, *refs):
    lefts, rights, out = refs[: 4 * terms], refs[4 * terms : 5 * terms], refs[-1]
    total = None
    for term in range(terms):
        rows = jnp.concatenate([lefts[4 * term + j][...] for j in range(4)], axis=0)
        part = jnp.dot(rows, rights[term][...], preferred_element_type=jnp.float32)
        total = part if total is None else total + part
    out[...] = total.astype(out.dtype)


def slot_product(places, lefts, rights):
    width = rights[0].shape[1]
    block = lambda j: (lambda i, places: (places[j], 0))
    return pl.pallas_call(
        functools.partial(product_kernel, len(lefts)),
        grid_spec=pltpu.PrefetchScalarGridSpec(
            num_scalar_prefetch=1,
            grid=(width // LANE_STEP,),
            in_specs=[
                pl.BlockSpec((BLOCK, left.shape[1]), block(j)) for left in lefts for j in range(4)
            ]
            + [
                pl.BlockSpec((right.shape[0], LANE_STEP), lambda i, places: (0, i))
                for right in rights
            ],
            out_specs=pl.BlockSpec((4 * BLOCK, LANE_STEP), lambda i, places: (0, i)),
        ),
        out_shape=jax.ShapeDtypeStruct((4 * BLOCK, width), jnp.bfloat16),
        compiler_params=pltpu.CompilerParams(
            dimension_semantics=("arbitrary",), vmem_limit_bytes=ROOM
        ),
        cost_estimate=pl.CostEstimate(
            flops=sum(8 * BLOCK * right.shape[0] * width for right in rights),
            transcendentals=0,
            bytes_accessed=sum(2 * right.size + 8 * BLOCK * right.shape[0] for right in rights),
        ),
        name="slot_product",
    )(places, *[left for left in lefts for _ in range(4)], *rights)


ROW_STEP = 256


def share_lanes(share, columns):
    lane = lax.broadcasted_iota(jnp.int32, (share.shape[0], columns), 1)
    return jnp.where(lane < columns // 2, share[:, 0:1], share[:, 1:2])


def open_kernel(rows, gate_w, up_w, share, gate_out, up_out, inner_out):
    gate = nt(rows[...], gate_w[...])
    up = nt(rows[...], up_w[...])
    gate_out[...] = gate
    up_out[...] = up
    inner_out[...] = (
        gate / (1.0 + jnp.exp(-gate)) * up * share_lanes(share[...], gate.shape[1])
    ).astype(jnp.bfloat16)


def close_kernel(rows, down_w, share, gate_in, up_in, gate_out, up_out):
    gate = gate_in[...]
    pull = nt(rows[...], down_w[...]) * share_lanes(share[...], gate.shape[1])
    sigma = 1.0 / (1.0 + jnp.exp(-gate))
    gate_out[...] = (pull * up_in[...] * sigma * (1.0 + gate * (1.0 - sigma))).astype(jnp.bfloat16)
    up_out[...] = (pull * gate * sigma).astype(jnp.bfloat16)


def row_call(kernel, rows, weights, others, kinds, name):
    count, width = rows.shape
    columns = weights[0].shape[0]
    tile = lambda lanes: pl.BlockSpec((ROW_STEP, lanes), lambda i: (i, 0))
    return pl.pallas_call(
        kernel,
        grid=(count // ROW_STEP,),
        in_specs=[tile(width)]
        + [
            pl.BlockSpec(weight.shape, lambda i: (0, 0), pipeline_mode=pl.Buffered(1))
            for weight in weights
        ]
        + [tile(other.shape[1]) for other in others],
        out_specs=[tile(columns) for _ in kinds],
        out_shape=[jax.ShapeDtypeStruct((count, columns), kind) for kind in kinds],
        compiler_params=pltpu.CompilerParams(
            dimension_semantics=("arbitrary",), vmem_limit_bytes=ROOM
        ),
        cost_estimate=pl.CostEstimate(
            flops=2 * len(weights) * count * width * columns,
            transcendentals=count * columns,
            bytes_accessed=2 * len(weights) * width * columns + 10 * count * columns,
        ),
        name=name,
    )(rows, *weights, *others)


def team_device(
    tokens_in,
    teacher,
    valid,
    attn_routes,
    attn_share,
    mlp_routes,
    mlp_share,
    gains,
    w_query,
    w_out,
    w_keyval,
    w_gate,
    w_up,
    w_down,
):
    low = jnp.bfloat16
    units = lax.axis_size("dp")
    plane = lax.axis_index("y")
    core = lax.axis_index("c")
    micro_count, row_count, local_width = tokens_in.shape
    half = row_count // 2
    width = local_width * 4
    team_rows = 2 * units * half
    prompt_total = units * half
    expert_count = w_query.shape[0]
    local_heads = w_query.shape[2] // HEAD
    depth = w_query.shape[1]
    hidden = w_down.shape[1]
    loss_scale = width * micro_count * row_count * units / 2.0
    scale_root = HEAD ** (-0.5)

    def exchange(parts):
        spot = 2 * plane + core
        got = [lax.dynamic_index_in_dim(parts, spot, 0, keepdims=False)]
        for step in (1, 2, 3):
            part = lax.dynamic_index_in_dim(parts, spot ^ step, 0, keepdims=False)
            got.append(lax.ppermute(part, QUAD, [(p, p ^ step) for p in range(4)]))
        for step, flag in ((1, core), (2, plane)):
            got = [jnp.where(flag == 0, got[p], got[p ^ step]) for p in range(4)]
        return got

    def to_rows(value):
        return jnp.concatenate(exchange(value.reshape(4, half, local_width)), axis=1)

    def from_rows(value):
        got = exchange(value.reshape(half, 4, local_width).transpose(1, 0, 2))
        return jnp.stack(got).reshape(micro_count, row_count, local_width)

    def collect(value):
        return lax.all_gather(value, TEAM, axis=0, tiled=True)

    def deliver(value):
        return lax.psum_scatter(value.astype(low), TEAM, scatter_dimension=0, tiled=True).astype(
            jnp.float32
        )

    def mine(value):
        return lax.dynamic_index_in_dim(value, plane, 0, keepdims=False)

    field = to_rows(tokens_in).astype(jnp.float32)
    goal = to_rows(teacher).astype(jnp.float32)
    gate_here = jnp.concatenate(
        [
            gate_rows(mine(attn_routes), mine(attn_share), expert_count),
            gate_rows(mine(mlp_routes), mine(mlp_share), expert_count),
        ],
        axis=0,
    )
    tokens_here = jnp.full((1, row_count), jnp.sum(valid).astype(jnp.float32))
    gate_here = jnp.concatenate([gate_here, tokens_here], axis=0)
    slots = jnp.arange(units, dtype=jnp.int32)[:, None, None]
    gate_all = jnp.where(slots == lax.axis_index("dp"), gate_here[None], 0.0)
    for shift in range(1, units):
        got = lax.ppermute(gate_here, "dp", [(i, (i + shift) % units) for i in range(units)])
        gate_all = jnp.where(slots == (lax.axis_index("dp") - shift) % units, got[None], gate_all)
    count = jnp.sum(gate_all[:, -1, 0])
    normed1 = (field * root_of(field) * gains[0]).astype(low)
    normed1 = collect(normed1)

    query_part = w_query.reshape(expert_count, depth, local_heads, HEAD).transpose(1, 2, 0, 3)
    out_part = w_out.reshape(expert_count, local_heads, HEAD, depth).transpose(3, 1, 0, 2)
    pair_part = w_keyval.reshape(depth, 2, local_heads, HEAD).transpose(0, 2, 1, 3)
    wide = expert_count * HEAD
    def across(value):
        return lax.ppermute(value, "y", swap_pairs(2))

    def scatter_heads(value):
        lanes = value.shape[2]
        packed = value.reshape(2, depth // 2, local_heads, lanes).transpose(0, 2, 1, 3)
        kept_half = lax.dynamic_index_in_dim(packed, core, 0, keepdims=False)
        sent_half = lax.dynamic_index_in_dim(packed, 1 - core, 0, keepdims=False)
        got_half = lax.ppermute(sent_half, "c", swap_pairs(2))
        return jnp.concatenate(
            [
                jnp.where(core == 0, kept_half, got_half),
                jnp.where(core == 0, got_half, kept_half),
            ],
            axis=0,
        )

    def deal_heads(heads):
        first = lax.ppermute(heads, QUAD, DEAL_FIRST)
        second = lax.ppermute(heads, QUAD, DEAL_SECOND)
        return jnp.stack(
            [jnp.where(plane == 0, first, second), jnp.where(plane == 0, second, first)], axis=1
        ).reshape(width, heads.shape[2])

    def swap_all(value, *later):
        got = lax.all_to_all(value, "dp", 0, 0, tiled=True)
        return lax.optimization_barrier((got, *later))

    def slabs_of(value):
        return value.T.reshape(units, hidden, depth)

    down_own = w_down[0]
    down_far = across(down_own)
    front_heads = scatter_heads(
        jnp.concatenate(
            [
                query_part.reshape(depth, local_heads, wide),
                pair_part.reshape(depth, local_heads, 2 * HEAD),
            ],
            axis=2,
        )
    )
    out_heads = scatter_heads(out_part.reshape(depth, local_heads, wide))
    gate_slabs, up_slabs = slabs_of(w_gate[0]), slabs_of(w_up[0])
    front_heads, gate_all, count = hold(front_heads, gate_all, count)
    front_heads, out_heads, down_far = swap_all(front_heads, out_heads, down_far)
    out_heads, gate_slabs = swap_all(out_heads, gate_slabs)
    front_weights = deal_heads(front_heads)
    gate_all = (
        gate_all[:, :-1].reshape(units, 2 * expert_count, 2, half)
        .transpose(1, 2, 0, 3)
        .reshape(2 * expert_count, team_rows)
    )
    feed_gate_own = lax.dynamic_index_in_dim(gate_all, expert_count + 2 * plane + core, 0, False)
    feed_gate_far = lax.dynamic_index_in_dim(gate_all, expert_count + 2 * (1 - plane) + core, 0, False)
    counted = lax.dynamic_slice_in_dim(mine(valid), core * half, half, 0).astype(jnp.float32)[:, None]

    normed1, gate_all, feed_gate_own, feed_gate_far, count, gate_slabs = lax.optimization_barrier(
        (normed1, gate_all, feed_gate_own, feed_gate_far, count, gate_slabs)
    )
    gate_slabs, up_slabs = swap_all(gate_slabs, up_slabs)
    gate_own = gate_slabs.transpose(1, 0, 2).reshape(hidden, width)
    gate_far = across(gate_own)
    attn_gate = gate_all[:expert_count].T
    blocks = team_rows // BLOCK
    gate_lines = (
        gate_all[:expert_count].reshape(expert_count, blocks, BLOCK).transpose(1, 0, 2)
    ).reshape(blocks, 1, expert_count * BLOCK)
    index = jnp.arange(team_rows, dtype=jnp.int32)
    places = jnp.where(index < prompt_total, index, prompt_total + index % half)
    cosine, sine = rope_tables(places)
    cosine = jnp.concatenate([cosine, cosine], axis=1)
    sine = jnp.concatenate([-sine, sine], axis=1)

    unit = lax.axis_index("dp")
    order = jnp.asarray([[0, 1, 2, 3], [1, 0, 2, 3], [2, 3, 1, 0], [3, 2, 1, 0]], jnp.int32)
    block = jnp.arange(blocks, dtype=jnp.int32)
    owners = (
        ((block // 2 % 2) ^ core) * units
        + lax.dynamic_index_in_dim(order, unit // 2, 0, False)[block // 4] * 2
        + ((block % 2) ^ (unit % 2))
    )

    front = dot(normed1, front_weights)
    front, out_heads = lax.optimization_barrier((front, out_heads))
    out_weights = deal_heads(out_heads)
    mixed_low, query_rot, pair_rot, log_total = attend(
        front, cosine, sine, gate_lines, units, expert_count
    )
    mixed_low, gate_own, up_slabs = lax.optimization_barrier((mixed_low, gate_own, up_slabs))
    up_slabs = lax.all_to_all(up_slabs, "dp", 0, 0, tiled=True)
    up_own = up_slabs.transpose(1, 0, 2).reshape(hidden, width)
    up_far = across(up_own)
    attn_sum = deliver(times_trans(mixed_low, out_weights))
    attn_sum, up_own, gate_far = lax.optimization_barrier((attn_sum, up_own, gate_far))
    hidden1 = field + attn_sum
    normed2 = collect((hidden1 * root_of(hidden1) * gains[1]).astype(low))

    gate_w = jnp.concatenate([gate_own, gate_far], axis=0)
    up_w = jnp.concatenate([up_own, up_far], axis=0)
    down_w = jnp.concatenate([down_own, down_far], axis=0)
    feed_share = jnp.stack([feed_gate_own, feed_gate_far], axis=1)
    gate_pre, up_pre, inner = row_call(
        open_kernel,
        normed2,
        [gate_w, up_w],
        [feed_share],
        [jnp.float32, jnp.float32, low],
        "open_rows",
    )
    result = hidden1 + scatter_run(
        lambda k, left: slot_product(owners[4 * k : 4 * k + 4], [left], [down_w]), (inner,)
    )
    layer_low = result.astype(low)
    differ = result - goal
    squared = jnp.sum(counted * differ * differ)
    grad_result = counted * differ * (2.0 * (loss_scale / (count * width)))
    grad_rows = collect(grad_result.astype(low))
    grad_rows, layer_low = hold(grad_rows, layer_low)
    layer_out = from_rows(layer_low)

    grad_gate, grad_up = row_call(
        close_kernel, grad_rows, [down_w], [feed_share, gate_pre, up_pre], [low, low], "close_rows"
    )

    def weight_sum(left, right):
        whole = times_rows(left, right)
        return whole[:hidden], whole[hidden:].astype(low)

    grad_norm2, (gate_near, gate_sent) = scatter_run(
        lambda k, one, two: slot_product(owners[4 * k : 4 * k + 4], [one, two], [gate_w, up_w]),
        (grad_gate, grad_up),
        lambda one, two: weight_sum(one, normed2),
    )
    gate_got = across(gate_sent)
    grad_norm2, grad_up, inner = hold(grad_norm2, grad_up, inner)
    up_near, up_sent = weight_sum(grad_up, normed2)
    down_near, down_sent = weight_sum(inner, grad_rows)
    gate_got, up_near, up_sent, down_near, down_sent = hold(
        gate_got, up_near, up_sent, down_near, down_sent
    )
    up_got = across(up_sent)
    grad_hidden_norm, grad_gain2 = norm_back(hidden1, gains[1], grad_norm2)
    grad_hidden1 = grad_result + grad_hidden_norm
    grad_hidden_rows = collect(grad_hidden1.astype(low))

    def rows_for_owners(value):
        return value.astype(low).reshape(hidden, units, depth).transpose(1, 0, 2)

    def own_rows(value):
        return value.reshape(units * hidden, depth).T.astype(jnp.float32)

    gate_slabs = rows_for_owners(gate_near + gate_got.astype(jnp.float32))
    gate_slabs = lax.all_to_all(gate_slabs, "dp", 0, 0, tiled=True)
    front_back = attend_back(
        dot(grad_hidden_rows, out_weights),
        attn_gate,
        query_rot,
        pair_rot,
        pair_rot[:, :HEAD].T,
        log_total,
        cosine,
        sine,
        units,
        expert_count,
    )
    front_back, gate_slabs, up_got = hold(front_back, gate_slabs, up_got)
    up_slabs = rows_for_owners(up_near + up_got.astype(jnp.float32))
    up_slabs = lax.all_to_all(up_slabs, "dp", 0, 0, tiled=True)
    out_grad = times_rows(grad_hidden_rows, mixed_low)
    grad_norm1 = deliver(times_trans(front_back, front_weights))
    front_grad = times_rows(normed1, front_back)
    grad_field_norm, grad_gain1 = norm_back(field, gains[0], grad_norm1)
    grad_field = grad_hidden1 + grad_field_norm

    def undeal_heads(value):
        halves = value.astype(low).reshape(units, 2, depth // 2, value.shape[1])
        first = lax.dynamic_index_in_dim(halves, plane, 1, keepdims=False)
        second = lax.dynamic_index_in_dim(halves, 1 - plane, 1, keepdims=False)
        both = lax.ppermute(first, QUAD, BACK_FIRST).astype(jnp.float32) + lax.ppermute(
            second, QUAD, BACK_SECOND
        ).astype(jnp.float32)
        return both.astype(low)

    def gather_heads(value):
        got = value.reshape(2, local_heads, depth // 2, value.shape[2])
        own = lax.dynamic_index_in_dim(got, core, 0, keepdims=False)
        swapped = lax.ppermute(
            lax.dynamic_index_in_dim(got, 1 - core, 0, keepdims=False), "c", swap_pairs(2)
        )
        rows = jnp.concatenate(
            [jnp.where(core == 0, own, swapped), jnp.where(core == 0, swapped, own)], axis=1
        )
        return rows.astype(jnp.float32)

    front_heads = undeal_heads(front_grad)
    front_heads, out_grad = hold(front_heads, out_grad)
    out_heads = undeal_heads(out_grad)
    out_heads, down_sent = hold(out_heads, down_sent)
    down_sum = down_near + across(down_sent).astype(jnp.float32)
    front_heads, up_slabs = hold(front_heads, up_slabs)
    front_heads, out_heads = swap_all(front_heads, out_heads)
    out_heads, grad_field, grad_gain1 = hold(out_heads, grad_field, grad_gain1)
    input_grad = from_rows(grad_field)
    out_heads = lax.all_to_all(out_heads, "dp", 0, 0, tiled=True)
    grad_gate_out, grad_up_out = own_rows(gate_slabs), own_rows(up_slabs)
    front_out, out_back = gather_heads(front_heads), gather_heads(out_heads)
    grad_out = out_back.reshape(local_heads, depth, expert_count, HEAD).transpose(2, 0, 3, 1)
    grad_query_out = front_out[:, :, :wide].reshape(local_heads, depth, expert_count, HEAD).transpose(2, 1, 0, 3)
    grad_pair = front_out[:, :, wide:].reshape(local_heads, depth, 2, HEAD).transpose(1, 2, 0, 3)
    totals = jnp.stack([grad_gain1, grad_gain2, jnp.full((width,), squared)])
    for axis, size in (("c", 2), ("y", 2), ("dp", units)):
        reach = 1
        while reach < size:
            totals = totals + lax.ppermute(totals, axis, [(i, i ^ reach) for i in range(size)])
            reach *= 2
    gain_total, squared_total = totals[:2], totals[2, 0]
    return (
        layer_out,
        squared_total / (count * width),
        input_grad,
        gain_total,
        grad_query_out.reshape(w_query.shape),
        grad_out.reshape(w_out.shape),
        grad_pair.reshape(w_keyval.shape),
        grad_gate_out[None],
        grad_up_out[None],
        down_sum[None],
    )


def solution(mesh):
    units, experts = mesh.shape["dp"], mesh.shape["expert"]

    def specs(quad):
        return (
            (
                P(None, "dp", quad),
                P(None, "dp", quad),
                P(None, "dp"),
                P(None, "dp", None),
                P(None, "dp", None),
                P(None, "dp", None),
                P(None, "dp", None),
                P(),
                P(None, "dp", quad),
                P(None, quad, "dp"),
                P("dp", None, quad),
                P(quad, "dp", None),
                P(quad, "dp", None),
                P(quad, "dp", None),
            ),
            (
                P(None, "dp", quad),
                P(),
                P(None, "dp", quad),
                P(),
                P(None, "dp", quad),
                P(None, quad, "dp"),
                P("dp", None, quad),
                P(quad, "dp", None),
                P(quad, "dp", None),
                P(quad, "dp", None),
            ),
        )

    def step(*arguments):
        tokens_in, w_query = arguments[0], arguments[8]
        team = (
            experts == 4
            and tokens_in.shape[0] == 2
            and w_query.shape[2] // HEAD == 2 * units
            and w_query.shape[0] == 4
            and tokens_in.shape[1] == units * 2 * PROMPT_DEV
            and PROMPT_DEV == CLEN == BLOCK
            and units == 2 * LINE
        )
        if team:
            grid = Mesh(mesh.devices.reshape(units, 2, 2), ("dp", "y", "c"))
            ins, outs = specs(QUAD)
            body = team_device
        else:
            grid = mesh
            ins, outs = specs("expert")
            body = per_device
        return jax.shard_map(body, mesh=grid, in_specs=ins, out_specs=outs, check_vma=False)(*arguments)

    return step
```

```python
import functools

import jax
import jax.numpy as jnp
from jax import lax
from jax.experimental import pallas as pl
from jax.experimental.pallas import tpu as pltpu
from jax.sharding import Mesh
from jax.sharding import PartitionSpec as P

HEAD = 128
PROMPT_DEV = 128
CLEN = 128
CAP = 144


EPS = 1e-06
THETA = 10000.0
TRANS_DIMS = (((1,), (1,)), ((), ()))
ROWS_DIMS = (((0,), (0,)), ((), ()))


def rotate(value, places):
    half = value.shape[-1] // 2
    kind = value.dtype
    ladder = jnp.arange(half).astype(kind) * (2.0 / value.shape[-1])
    freqs = jnp.power(jnp.asarray(THETA, kind), -ladder)
    angle = places.astype(kind)[:, None] * freqs[None, :]
    cosine = jnp.cos(angle)[:, None, :]
    sine = jnp.sin(angle)[:, None, :]
    first = value[..., :half]
    second = value[..., half:]
    return jnp.concatenate(
        [first * cosine - second * sine, second * cosine + first * sine], axis=-1
    )


def rms_scale(field, gain):
    return field * lax.rsqrt(jnp.mean(field * field, axis=-1, keepdims=True) + EPS) * gain


def times_trans(left, right):
    return lax.dot_general(left, right, TRANS_DIMS, preferred_element_type=jnp.float32)


def times_rows(left, right):
    return lax.dot_general(left, right, ROWS_DIMS, preferred_element_type=jnp.float32)


def slot_plan(route, share, expert_id, slots):
    shares = share.astype(jnp.float32)
    weight = shares / jnp.sum(shares, axis=-1, keepdims=True)
    match = route == expert_id
    taken = jnp.any(match, axis=-1)
    gate_row = jnp.sum(jnp.where(match, weight, 0.0), axis=-1)
    order = jnp.cumsum(taken.astype(jnp.int32)) - 1
    placed = (order[None, :] == jnp.arange(slots, dtype=jnp.int32)[:, None]) & taken[None, :]
    row_index = jnp.arange(route.shape[0], dtype=jnp.int32)
    row_ids = jnp.sum(jnp.where(placed, row_index[None, :], 0), axis=1)
    filled = jnp.any(placed, axis=1)
    slot_gate = jnp.where(filled, gate_row[row_ids], 0.0)
    return (row_ids, slot_gate)


def per_device(
    tokens_in,
    teacher,
    valid,
    attn_routes,
    attn_share,
    mlp_routes,
    mlp_share,
    gains,
    w_query,
    w_out,
    w_keyval,
    w_gate,
    w_up,
    w_down,
):
    dp_count = lax.axis_size("dp")
    unit_index = lax.axis_index("dp")
    expert_index = lax.axis_index("expert")
    micro_count, row_count, local_width = tokens_in.shape
    full_width = local_width * lax.axis_size("expert")
    expert_count = w_query.shape[0]
    head_cols = w_query.shape[2]
    local_heads = head_cols // HEAD
    prompt_total = PROMPT_DEV * dp_count
    key_count = prompt_total + CLEN
    loss_scale = full_width * micro_count * row_count * dp_count / 2.0
    scale_root = HEAD ** (-0.5)
    within = jnp.arange(row_count, dtype=jnp.int32)
    places = jnp.where(
        within < PROMPT_DEV, unit_index * PROMPT_DEV + within, prompt_total + within - PROMPT_DEV
    )
    key_index = jnp.arange(key_count, dtype=jnp.int32)
    own_columns = jnp.arange(full_width, dtype=jnp.int32) // local_width == expert_index
    col_start = expert_index * local_width
    count = lax.psum(jnp.sum(valid).astype(jnp.float32), "dp")
    query_full, out_full, keyval_full = (
        lax.all_gather(w_query, "dp", axis=1, tiled=True),
        lax.all_gather(w_out, "dp", axis=2, tiled=True),
        lax.all_gather(w_keyval, "dp", axis=0, tiled=True),
    )
    keyval_flat = keyval_full.reshape(full_width, 2 * head_cols)
    held_query = jnp.zeros(query_full.shape, jnp.float32)
    held_out = jnp.zeros(out_full.shape, jnp.float32)
    held_keyval = jnp.zeros(keyval_full.shape, jnp.float32)
    held_gate = jnp.zeros((full_width, w_gate.shape[2]), jnp.float32)
    held_up = jnp.zeros((full_width, w_up.shape[2]), jnp.float32)
    held_down = jnp.zeros((w_down.shape[1] * dp_count, w_down.shape[2]), jnp.float32)
    gain_sum = jnp.zeros((2, full_width), jnp.float32)
    squared = jnp.zeros((), jnp.float32)
    results = []
    input_grads = []
    for micro_id in range(micro_count):
        field_low = lax.all_gather(tokens_in[micro_id], "expert", axis=1, tiled=True)
        field = field_low.astype(jnp.float32)
        normed1 = rms_scale(field, gains[0]).astype(jnp.bfloat16)
        keyval_pre = jnp.dot(normed1, keyval_flat, preferred_element_type=jnp.float32).reshape(
            row_count, 2, local_heads, HEAD
        )
        keys_here = rotate(keyval_pre[:, 0], places).astype(jnp.bfloat16)
        values_here = keyval_pre[:, 1].astype(jnp.bfloat16)
        pair_here = jnp.stack([keys_here, values_here], axis=1).reshape(row_count, 2, head_cols)
        prompt_pair = lax.all_gather(pair_here[:PROMPT_DEV], "dp", axis=0, tiled=True)
        pair_all = jnp.concatenate([prompt_pair, pair_here[PROMPT_DEV:]], axis=0).reshape(
            key_count, 2, local_heads, HEAD
        )
        keys_all = pair_all[:, 0]
        values_all = pair_all[:, 1]

        def score_block(query_rot, slot_places):
            raw = (
                jnp.einsum("chd,khd->hck", query_rot, keys_all, preferred_element_type=jnp.float32)
                * scale_root
            )
            seen = key_index[None, :] <= slot_places[:, None]
            return jnp.where(seen[None], raw, -1e30)

        attn_part = jnp.zeros((row_count, full_width), jnp.float32)
        kept = []
        for expert_id in range(expert_count):
            row_ids, slot_gate = slot_plan(
                attn_routes[micro_id], attn_share[micro_id], expert_id, CAP
            )
            chosen = jnp.take(normed1, row_ids, axis=0)
            slot_places = places[row_ids]
            query_pre = jnp.dot(
                chosen, query_full[expert_id], preferred_element_type=jnp.float32
            ).reshape(CAP, local_heads, HEAD)
            query_rot = rotate(query_pre, slot_places).astype(jnp.bfloat16)
            scores = score_block(query_rot, slot_places)
            peak = jnp.max(scores, axis=-1, keepdims=True)
            raised = jnp.exp(scores - peak)
            denom_sum = jnp.sum(raised, axis=-1, keepdims=True)
            attend = raised / denom_sum
            log_total = peak + jnp.log(denom_sum)
            mixed = jnp.einsum(
                "hck,khd->chd",
                attend.astype(jnp.bfloat16),
                values_all,
                preferred_element_type=jnp.float32,
            )
            mixed_low = mixed.reshape(CAP, head_cols).astype(jnp.bfloat16)
            project = jnp.dot(mixed_low, out_full[expert_id], preferred_element_type=jnp.float32)
            attn_part = attn_part.at[row_ids].add(project * slot_gate[:, None])
            kept.append(
                (
                    row_ids,
                    slot_gate,
                    chosen,
                    slot_places,
                    query_pre,
                    query_rot,
                    log_total,
                    mixed_low,
                )
            )
        attn_total = lax.psum(attn_part, "expert")
        hidden1 = field + attn_total
        normed2 = rms_scale(hidden1, gains[1]).astype(jnp.bfloat16)
        gate_full, up_full, down_full = (
            lax.all_gather(w_gate[0], "dp", axis=0, tiled=True),
            lax.all_gather(w_up[0], "dp", axis=0, tiled=True),
            lax.all_gather(w_down[0], "dp", axis=0, tiled=True),
        )
        feed_rows, feed_gate = slot_plan(
            mlp_routes[micro_id], mlp_share[micro_id], expert_index, CAP
        )
        feed_in = jnp.take(normed2, feed_rows, axis=0)
        gate_pre = jnp.dot(feed_in, gate_full, preferred_element_type=jnp.float32)
        up_pre = jnp.dot(feed_in, up_full, preferred_element_type=jnp.float32)
        inner = (jax.nn.silu(gate_pre) * up_pre).astype(jnp.bfloat16)
        feed_out = jnp.dot(inner, down_full, preferred_element_type=jnp.float32)
        feed_part = (
            jnp.zeros((row_count, full_width), jnp.float32)
            .at[feed_rows]
            .add(feed_out * feed_gate[:, None])
        )
        feed_shard = lax.psum_scatter(feed_part, "expert", scatter_dimension=1, tiled=True)
        hidden1_shard = lax.dynamic_slice_in_dim(hidden1, col_start, local_width, 1)
        result = hidden1_shard + feed_shard
        results.append(result.astype(jnp.bfloat16))
        differ = result - teacher[micro_id].astype(jnp.float32)
        counted = valid[micro_id].astype(jnp.float32)[:, None]
        squared = squared + jnp.sum(counted * differ * differ)
        grad_result = counted * differ * (2.0 * (loss_scale / (count * full_width)))
        grad_rows = lax.all_gather(grad_result, "expert", axis=1, tiled=True)
        gate_back, up_back, down_back = (
            lax.all_gather(w_gate[0], "dp", axis=0, tiled=True),
            lax.all_gather(w_up[0], "dp", axis=0, tiled=True),
            lax.all_gather(w_down[0], "dp", axis=0, tiled=True),
        )
        grad_feed = (jnp.take(grad_rows, feed_rows, axis=0) * feed_gate[:, None]).astype(
            jnp.bfloat16
        )
        grad_inner = times_trans(grad_feed, down_back)
        _, silu_back = jax.vjp(lambda left, right: jax.nn.silu(left) * right, gate_pre, up_pre)
        grad_gate_pre, grad_up_pre = silu_back(grad_inner)
        grad_gate_low = grad_gate_pre.astype(jnp.bfloat16)
        grad_up_low = grad_up_pre.astype(jnp.bfloat16)
        grad_feed_in = times_trans(grad_gate_low, gate_back) + times_trans(grad_up_low, up_back)
        held_gate = held_gate + times_rows(feed_in, grad_gate_low)
        held_up = held_up + times_rows(feed_in, grad_up_low)
        held_down = held_down + times_rows(inner, grad_feed)
        grad_norm2_part = (
            jnp.zeros((row_count, full_width), jnp.float32).at[feed_rows].add(grad_feed_in)
        )
        grad_norm2 = lax.psum(grad_norm2_part, "expert")
        _, norm2_back = jax.vjp(rms_scale, hidden1, gains[1])
        grad_hidden_norm, grad_gain2 = norm2_back(grad_norm2)
        grad_hidden1 = grad_rows + grad_hidden_norm
        grad_norm1_part = jnp.zeros((row_count, full_width), jnp.float32)
        grad_pair = jnp.zeros((key_count, 2, local_heads, HEAD), jnp.float32)
        term_query = []
        term_out = []
        for expert_id in range(expert_count):
            row_ids, slot_gate, chosen, slot_places, query_pre, query_rot, log_total, mixed_low = (
                kept[expert_id]
            )
            grad_project = (jnp.take(grad_hidden1, row_ids, axis=0) * slot_gate[:, None]).astype(
                jnp.bfloat16
            )
            grad_mixed = times_trans(grad_project, out_full[expert_id]).astype(jnp.bfloat16)
            term_out.append(times_rows(mixed_low, grad_project))
            grad_mixed = grad_mixed.reshape(CAP, local_heads, HEAD)
            scores = score_block(query_rot, slot_places)
            attend = jnp.exp(scores - log_total)
            attend_low = attend.astype(jnp.bfloat16)
            grad_attend = jnp.einsum(
                "chd,khd->hck", grad_mixed, values_all, preferred_element_type=jnp.float32
            )
            inner_sum = jnp.sum(attend * grad_attend, axis=-1, keepdims=True)
            grad_scores = (attend * (grad_attend - inner_sum)).astype(jnp.bfloat16)
            grad_query_rot = (
                jnp.einsum(
                    "hck,khd->chd", grad_scores, keys_all, preferred_element_type=jnp.float32
                )
                * scale_root
            )
            grad_keys = (
                jnp.einsum(
                    "hck,chd->khd", grad_scores, query_rot, preferred_element_type=jnp.float32
                )
                * scale_root
            )
            grad_values = jnp.einsum(
                "hck,chd->khd", attend_low, grad_mixed, preferred_element_type=jnp.float32
            )
            grad_pair = grad_pair + jnp.stack([grad_keys, grad_values], axis=1)
            _, query_back = jax.vjp(lambda value: rotate(value, slot_places), query_pre)
            grad_query_pre = (
                query_back(grad_query_rot)[0].astype(jnp.bfloat16).reshape(CAP, head_cols)
            )
            grad_norm1_part = grad_norm1_part.at[row_ids].add(
                times_trans(grad_query_pre, query_full[expert_id])
            )
            term_query.append(times_rows(chosen, grad_query_pre))
        grad_pair_flat = grad_pair.reshape(key_count, 2, head_cols)
        prompt_grad = lax.psum_scatter(
            grad_pair_flat[:prompt_total], "dp", scatter_dimension=0, tiled=True
        )
        pair_grad = jnp.concatenate([prompt_grad, grad_pair_flat[prompt_total:]], axis=0)
        _, key_back = jax.vjp(lambda value: rotate(value, places), keyval_pre[:, 0])
        grad_key_pre = key_back(pair_grad[:, 0].reshape(row_count, local_heads, HEAD))[0].reshape(
            row_count, head_cols
        )
        grad_pair_low = (
            jnp.stack([grad_key_pre, pair_grad[:, 1]], axis=1)
            .astype(jnp.bfloat16)
            .reshape(row_count, 2 * head_cols)
        )
        grad_norm1_part = grad_norm1_part + times_trans(grad_pair_low, keyval_flat)
        term_keyval = times_rows(normed1, grad_pair_low).reshape(full_width, 2, head_cols)
        grad_norm1 = lax.psum(grad_norm1_part.astype(jnp.bfloat16), "expert").astype(jnp.float32)
        _, norm1_back = jax.vjp(rms_scale, field, gains[0])
        grad_field_norm, grad_gain1 = norm1_back(grad_norm1)
        grad_field = grad_hidden1 + grad_field_norm
        input_grads.append(lax.dynamic_slice_in_dim(grad_field, col_start, local_width, 1))
        gain_sum = gain_sum + jnp.stack(
            [jnp.where(own_columns, grad_gain1, 0.0), jnp.where(own_columns, grad_gain2, 0.0)]
        )
        held_query = held_query + jnp.stack(term_query)
        held_out = held_out + jnp.stack(term_out)
        held_keyval = held_keyval + term_keyval
    grad_query, grad_out, grad_keyval, grad_gate, grad_up, grad_down = (
        lax.psum_scatter(
            held_query.astype(jnp.bfloat16), "dp", scatter_dimension=1, tiled=True
        ).astype(jnp.float32),
        lax.psum_scatter(
            held_out.astype(jnp.bfloat16), "dp", scatter_dimension=2, tiled=True
        ).astype(jnp.float32),
        lax.psum_scatter(
            held_keyval.astype(jnp.bfloat16), "dp", scatter_dimension=0, tiled=True
        ).astype(jnp.float32),
        lax.psum_scatter(
            held_gate.astype(jnp.bfloat16), "dp", scatter_dimension=0, tiled=True
        ).astype(jnp.float32),
        lax.psum_scatter(
            held_up.astype(jnp.bfloat16), "dp", scatter_dimension=0, tiled=True
        ).astype(jnp.float32),
        lax.psum_scatter(
            held_down.astype(jnp.bfloat16), "dp", scatter_dimension=0, tiled=True
        ).astype(jnp.float32),
    )
    gain_total, squared_total = lax.psum((gain_sum, squared), ("dp", "expert"))
    loss = squared_total / (count * full_width)
    return (
        jnp.stack(results),
        loss,
        jnp.stack(input_grads),
        gain_total,
        grad_query,
        grad_out,
        grad_keyval,
        grad_gate[None],
        grad_up[None],
        grad_down[None],
    )


def swap_pairs(size):
    return [(i, i ^ 1) for i in range(size)]


DEAL_FIRST = [(1, 2), (2, 1)]
DEAL_SECOND = [(0, 2), (1, 0), (2, 3), (3, 1)]
BACK_SECOND = [(b, a) for a, b in DEAL_SECOND]
QUAD = ("y", "c")
TEAM = ("c", "dp")


def rope_tables(places):
    half = HEAD // 2
    ladder = jnp.arange(half).astype(jnp.float32) * (2.0 / HEAD)
    freqs = jnp.power(jnp.asarray(THETA, jnp.float32), -ladder)
    angle = places.astype(jnp.float32)[:, None] * freqs[None, :]
    return jnp.cos(angle), jnp.sin(angle)


def turn(value, cosine, sine):
    half = value.shape[-1] // 2
    first = value[..., :half]
    second = value[..., half:]
    return jnp.concatenate(
        [first * cosine - second * sine, second * cosine + first * sine], axis=-1
    )


def root_of(field):
    return lax.rsqrt(jnp.mean(field * field, axis=-1, keepdims=True) + EPS)


def norm_back(field, gain, grad):
    root = root_of(field)
    scaled = grad * gain
    along = jnp.sum(scaled * field, axis=-1, keepdims=True) / field.shape[-1]
    return root * scaled - field * (root * root * root) * along, jnp.sum(grad * field * root, axis=0)


def gate_rows(route, share, expert_count):
    shares = share.astype(jnp.float32)
    weight = shares / jnp.sum(shares, axis=-1, keepdims=True)
    labels = jnp.arange(expert_count, dtype=jnp.int32)
    match = route[None, :, :] == labels[:, None, None]
    return jnp.sum(jnp.where(match, weight[None], 0.0), axis=-1)


def dot(left, right):
    return jnp.dot(left, right, preferred_element_type=jnp.float32)


BLOCK = 128
MASKED = -1e30
NT_DIMS = (((1,), (1,)), ((), ()))
ROOM = 56 * 1024 * 1024


def nt(left, right):
    return lax.dot_general(left, right, NT_DIMS, preferred_element_type=jnp.float32)


def spin(value, cosine, sine):
    return value * cosine + pltpu.roll(value, HEAD // 2, 1) * sine


def stack_experts(block, count):
    return jnp.concatenate([block[:, e * HEAD : (e + 1) * HEAD] for e in range(count)], axis=0)


def near_mask(columns):
    key_at = lax.broadcasted_iota(jnp.int32, (BLOCK, columns), 0)
    row_at = lax.broadcasted_iota(jnp.int32, (BLOCK, columns), 1) % BLOCK
    return key_at <= row_at


def attend_kernel(
    prompts, experts, front, cosine, sine, gate, mixed, query_out, pair_out, log_out, key_far, value_far
):
    step = pl.program_id(0)
    wide = experts * HEAD
    scale = HEAD ** (-0.5)

    @pl.when(step == 0)
    def _():
        key_far[...] = jnp.zeros_like(key_far)
        value_far[...] = jnp.zeros_like(value_far)

    cos, sin = cosine[...], sine[...]
    key = spin(front[:, wide : wide + HEAD], cos, sin).astype(jnp.bfloat16)
    value_up = front[:, wide + HEAD : wide + 2 * HEAD].T.astype(jnp.bfloat16)
    pair_out[:, :HEAD] = key
    pair_out[:, HEAD:] = front[:, wide + HEAD : wide + 2 * HEAD].astype(jnp.bfloat16)
    for e in range(experts):
        query_out[:, e * HEAD : (e + 1) * HEAD] = spin(
            front[:, e * HEAD : (e + 1) * HEAD], cos, sin
        ).astype(jnp.bfloat16)
    query = stack_experts(query_out[...], experts)
    near = jnp.where(near_mask(wide), nt(key, query) * scale, MASKED)
    far_tiles = jnp.minimum(step, prompts)

    def finish(width):
        far = nt(key_far[:width, :], query) * scale
        key_at = lax.broadcasted_iota(jnp.int32, far.shape, 0)
        far = jnp.where(key_at < far_tiles * BLOCK, far, MASKED)
        peak = jnp.maximum(
            jnp.max(far, axis=0, keepdims=True), jnp.max(near, axis=0, keepdims=True)
        )
        far = jnp.exp(far - peak)
        close = jnp.exp(near - peak)
        total = jnp.sum(far, axis=0, keepdims=True) + jnp.sum(close, axis=0, keepdims=True)
        mix = jnp.dot(
            value_far[:, :width], far.astype(jnp.bfloat16), preferred_element_type=jnp.float32
        ) + jnp.dot(value_up, close.astype(jnp.bfloat16), preferred_element_type=jnp.float32)
        mix = mix * (gate[0] / total)
        log_out[0] = peak + jnp.log(total)
        for e in range(experts):
            mixed[:, e * HEAD : (e + 1) * HEAD] = mix[:, e * BLOCK : (e + 1) * BLOCK].T.astype(
                jnp.bfloat16
            )

    split = prompts // 2

    @pl.when(step <= split)
    def _():
        finish(split * BLOCK)

    @pl.when(step > split)
    def _():
        finish(prompts * BLOCK)

    @pl.when(step < prompts)
    def _():
        at = pl.multiple_of(step * BLOCK, BLOCK)
        key_far[pl.ds(at, BLOCK), :] = key
        value_far[:, pl.ds(at, BLOCK)] = value_up


def attend(front, cosine, sine, gate, prompts, experts):
    rows, lanes = front.shape
    blocks = rows // BLOCK
    wide = experts * HEAD
    at = lambda i: (i, 0)
    line = pl.BlockSpec((1, 1, experts * BLOCK), lambda i: (i, 0, 0))
    return pl.pallas_call(
        functools.partial(attend_kernel, prompts, experts),
        grid=(blocks,),
        in_specs=[
            pl.BlockSpec((BLOCK, lanes), at),
            pl.BlockSpec((BLOCK, HEAD), at),
            pl.BlockSpec((BLOCK, HEAD), at),
            line,
        ],
        out_specs=[
            pl.BlockSpec((BLOCK, wide), at),
            pl.BlockSpec((BLOCK, wide), at),
            pl.BlockSpec((BLOCK, 2 * HEAD), at),
            line,
        ],
        out_shape=[
            jax.ShapeDtypeStruct((rows, wide), jnp.bfloat16),
            jax.ShapeDtypeStruct((rows, wide), jnp.bfloat16),
            jax.ShapeDtypeStruct((rows, 2 * HEAD), jnp.bfloat16),
            jax.ShapeDtypeStruct((blocks, 1, experts * BLOCK), jnp.float32),
        ],
        scratch_shapes=[
            pltpu.VMEM((prompts * BLOCK, HEAD), jnp.bfloat16),
            pltpu.VMEM((HEAD, prompts * BLOCK), jnp.bfloat16),
        ],
        compiler_params=pltpu.CompilerParams(
            dimension_semantics=("arbitrary",), vmem_limit_bytes=ROOM
        ),
        cost_estimate=pl.CostEstimate(
            flops=4 * rows * experts * HEAD * prompts * BLOCK,
            transcendentals=rows * experts * prompts * BLOCK,
            bytes_accessed=rows * lanes * 8,
        ),
        name="attend",
    )(front, cosine, sine, gate)


def attend_back_kernel(
    prompts, experts, pull, gate, query_in, pair, pair_up, log_in, cosine, sine, back, grad_key, grad_value
):
    step = pl.program_id(0)
    wide = experts * HEAD
    scale = HEAD ** (-0.5)

    @pl.when(step == 0)
    def _():
        grad_key[...] = jnp.zeros_like(grad_key)
        grad_value[...] = jnp.zeros_like(grad_value)

    at = pl.multiple_of(step * BLOCK, BLOCK)
    here = pl.ds(at, BLOCK)
    query = stack_experts(query_in[...], experts)
    grads = jnp.concatenate(
        [
            (pull[:, e * HEAD : (e + 1) * HEAD] * gate[:, e : e + 1]).astype(jnp.bfloat16)
            for e in range(experts)
        ],
        axis=0,
    )
    level = log_in[0]
    near = jnp.where(
        near_mask(wide), jnp.exp(nt(pair[here, :HEAD], query) * scale - level), 0.0
    )
    near_pull = nt(pair[here, HEAD:], grads)
    far_tiles = jnp.minimum(step, prompts)

    def finish(width):
        far = jnp.exp(nt(pair[:width, :HEAD], query) * scale - level)
        key_at = lax.broadcasted_iota(jnp.int32, far.shape, 0)
        far = jnp.where(key_at < far_tiles * BLOCK, far, 0.0)
        far_pull = nt(pair[:width, HEAD:], grads)
        along = jnp.sum(far * far_pull, axis=0, keepdims=True) + jnp.sum(
            near * near_pull, axis=0, keepdims=True
        )
        far_ds = (far * (far_pull - along)).astype(jnp.bfloat16)
        near_ds = (near * (near_pull - along)).astype(jnp.bfloat16)
        turned = (
            jnp.dot(pair_up[:, :width], far_ds, preferred_element_type=jnp.float32)
            + jnp.dot(pair_up[:, here], near_ds, preferred_element_type=jnp.float32)
        ) * scale
        cos, sin = cosine[here, :], sine[here, :]
        for e in range(experts):
            back[here, e * HEAD : (e + 1) * HEAD] = spin(
                turned[:, e * BLOCK : (e + 1) * BLOCK].T, cos, -sin
            ).astype(jnp.bfloat16)
        grad_key[:width, :] += jnp.dot(far_ds, query, preferred_element_type=jnp.float32)
        grad_value[:width, :] += jnp.dot(
            far.astype(jnp.bfloat16), grads, preferred_element_type=jnp.float32
        )
        grad_key[here, :] += jnp.dot(near_ds, query, preferred_element_type=jnp.float32)
        grad_value[here, :] += jnp.dot(
            near.astype(jnp.bfloat16), grads, preferred_element_type=jnp.float32
        )

    split = prompts // 2

    @pl.when(step <= split)
    def _():
        finish(split * BLOCK)

    @pl.when(step > split)
    def _():
        finish(prompts * BLOCK)

    @pl.when(step == pl.num_programs(0) - 1)
    def _():
        back[:, wide : wide + HEAD] = spin(
            grad_key[...] * scale, cosine[...], -sine[...]
        ).astype(jnp.bfloat16)
        back[:, wide + HEAD :] = grad_value[...].astype(jnp.bfloat16)


def attend_back(pull, gate, query, pair, pair_up, log_total, cosine, sine, prompts, experts):
    rows, wide = query.shape
    blocks = rows // BLOCK
    at = lambda i: (i, 0)
    still = lambda i: (0, 0)
    line = pl.BlockSpec((1, 1, experts * BLOCK), lambda i: (i, 0, 0))
    return pl.pallas_call(
        functools.partial(attend_back_kernel, prompts, experts),
        grid=(blocks,),
        in_specs=[
            pl.BlockSpec((BLOCK, wide), at),
            pl.BlockSpec((BLOCK, experts), at),
            pl.BlockSpec((BLOCK, wide), at),
            pl.BlockSpec((rows, 2 * HEAD), still),
            pl.BlockSpec((HEAD, rows), still),
            line,
            pl.BlockSpec((rows, HEAD), still),
            pl.BlockSpec((rows, HEAD), still),
        ],
        out_specs=pl.BlockSpec((rows, wide + 2 * HEAD), still),
        out_shape=jax.ShapeDtypeStruct((rows, wide + 2 * HEAD), jnp.bfloat16),
        scratch_shapes=[
            pltpu.VMEM((rows, HEAD), jnp.float32),
            pltpu.VMEM((rows, HEAD), jnp.float32),
        ],
        compiler_params=pltpu.CompilerParams(
            dimension_semantics=("arbitrary",), vmem_limit_bytes=ROOM
        ),
        cost_estimate=pl.CostEstimate(
            flops=10 * rows * experts * HEAD * prompts * BLOCK,
            transcendentals=rows * experts * prompts * BLOCK,
            bytes_accessed=rows * wide * 12,
        ),
        name="attend_back",
    )(pull, gate, query, pair, pair_up, log_total, cosine, sine)


LINE = 4
SIDES = [(i, i ^ 1) for i in range(2 * LINE)]


def hops(moves):
    return [(2 * a + x, 2 * b + x) for a, b in moves for x in (0, 1)]


def hold(*values):
    return lax.optimization_barrier(values)


def to_side(value):
    return lax.ppermute(value, "dp", SIDES)


def to_core(value):
    return lax.ppermute(value, "c", swap_pairs(2))


def scatter_run(make, given, fill=None):
    spot = lax.axis_index("dp") // 2
    low = jnp.bfloat16
    wide = lambda value: value.astype(jnp.float32)

    def rise(value, last):
        return lax.ppermute(value, "dp", hops([(a, a + 1) for a in range(last)]))

    def fall(value, last):
        return lax.ppermute(value, "dp", hops([(LINE - 1 - a, LINE - 2 - a) for a in range(last)]))

    def cut(value):
        middle = value.shape[0] // 2
        return value[:middle], value[middle:]

    here3, there3 = make(3, *given)
    there3, *given = hold(there3, *given)
    got3, (here2, there2) = hold(to_core(there3), make(2, *given))
    mine3, other3 = cut(here3 + got3)
    other3, there2, *given = hold(other3, there2, *given)
    side3, both2, (here1, there1) = hold(
        to_side(other3), here2 + to_core(there2), make(1, *given)
    )
    mine2, other2 = cut(both2)
    other2, there1, *given = hold(other2, there1, *given)
    row3 = wide(mine3) + wide(side3)
    send3 = row3.astype(low)
    side2, up, down, both1, (here0, there0) = hold(
        to_side(other2), rise(send3, 1), fall(send3, 1), here1 + to_core(there1), make(0, *given)
    )
    mine1, other1 = cut(both1)
    other1, there0, *given = hold(other1, there0, *given)
    row2 = wide(mine2) + wide(side2)
    send_up = (jnp.where(spot == 0, row2, row3) + wide(up)).astype(low)
    send_down = (jnp.where(spot == LINE - 1, row2, row3) + wide(down)).astype(low)
    side1, up, down, both0 = hold(
        to_side(other1), rise(send_up, 2), fall(send_down, 2), here0 + to_core(there0)
    )
    mine0, other0 = cut(both0)
    other0, *given = hold(other0, *given)
    row1 = wide(mine1) + wide(side1)
    send_up = (jnp.where(spot == 1, row2, row1) + wide(up)).astype(low)
    send_down = (jnp.where(spot == LINE - 2, row2, row1) + wide(down)).astype(low)
    filled = fill(*given) if fill else ()
    side0, up, down, filled = hold(to_side(other0), rise(send_up, 3), fall(send_down, 3), filled)
    total = wide(mine0) + wide(side0) + wide(up) + wide(down)
    return (total, filled) if fill else total


LANE_STEP = 512


def product_kernel(terms, places, *refs):
    lefts, rights, out = refs[: 4 * terms], refs[4 * terms : 5 * terms], refs[-2]
    far_out = refs[-1]
    total = None
    for term in range(terms):
        rows = jnp.concatenate([lefts[4 * term + j][...] for j in range(4)], axis=0)
        part = jnp.dot(rows, rights[term][...], preferred_element_type=jnp.float32)
        total = part if total is None else total + part
    middle = out.shape[0]
    out[...] = total[:middle].astype(out.dtype)
    far_out[...] = total[middle:].astype(out.dtype)


def slot_product(places, lefts, rights):
    width = rights[0].shape[1]
    block = lambda j: (lambda i, places: (places[j], 0))
    return pl.pallas_call(
        functools.partial(product_kernel, len(lefts)),
        grid_spec=pltpu.PrefetchScalarGridSpec(
            num_scalar_prefetch=1,
            grid=(width // LANE_STEP,),
            in_specs=[
                pl.BlockSpec((BLOCK, left.shape[1]), block(j)) for left in lefts for j in range(4)
            ]
            + [
                pl.BlockSpec((right.shape[0], LANE_STEP), lambda i, places: (0, i))
                for right in rights
            ],
            out_specs=[pl.BlockSpec((2 * BLOCK, LANE_STEP), lambda i, places: (0, i))] * 2,
        ),
        out_shape=[jax.ShapeDtypeStruct((2 * BLOCK, width), jnp.bfloat16)] * 2,
        compiler_params=pltpu.CompilerParams(
            dimension_semantics=("arbitrary",), vmem_limit_bytes=ROOM
        ),
        cost_estimate=pl.CostEstimate(
            flops=sum(8 * BLOCK * right.shape[0] * width for right in rights),
            transcendentals=0,
            bytes_accessed=sum(2 * right.size + 8 * BLOCK * right.shape[0] for right in rights),
        ),
        name="slot_product",
    )(places, *[left for left in lefts for _ in range(4)], *rights)


ROW_STEP = 256


def share_lanes(share, columns):
    lane = lax.broadcasted_iota(jnp.int32, (share.shape[0], columns), 1)
    return jnp.where(lane < columns // 2, share[:, 0:1], share[:, 1:2])


def open_kernel(rows, gate_w, up_w, share, gate_out, up_out, inner_out):
    gate = nt(rows[...], gate_w[...])
    up = nt(rows[...], up_w[...])
    gate_out[...] = gate
    up_out[...] = up
    inner_out[...] = (
        gate / (1.0 + jnp.exp(-gate)) * up * share_lanes(share[...], gate.shape[1])
    ).astype(jnp.bfloat16)


def close_kernel(rows, down_w, share, gate_in, up_in, gate_out, up_out):
    gate = gate_in[...]
    pull = nt(rows[...], down_w[...]) * share_lanes(share[...], gate.shape[1])
    sigma = 1.0 / (1.0 + jnp.exp(-gate))
    gate_out[...] = (pull * up_in[...] * sigma * (1.0 + gate * (1.0 - sigma))).astype(jnp.bfloat16)
    up_out[...] = (pull * gate * sigma).astype(jnp.bfloat16)


def row_call(kernel, rows, weights, others, kinds, name):
    count, width = rows.shape
    columns = weights[0].shape[0]
    tile = lambda lanes: pl.BlockSpec((ROW_STEP, lanes), lambda i: (i, 0))
    return pl.pallas_call(
        kernel,
        grid=(count // ROW_STEP,),
        in_specs=[tile(width)]
        + [
            pl.BlockSpec(weight.shape, lambda i: (0, 0), pipeline_mode=pl.Buffered(1))
            for weight in weights
        ]
        + [tile(other.shape[1]) for other in others],
        out_specs=[tile(columns) for _ in kinds],
        out_shape=[jax.ShapeDtypeStruct((count, columns), kind) for kind in kinds],
        compiler_params=pltpu.CompilerParams(
            dimension_semantics=("arbitrary",), vmem_limit_bytes=ROOM
        ),
        cost_estimate=pl.CostEstimate(
            flops=2 * len(weights) * count * width * columns,
            transcendentals=count * columns,
            bytes_accessed=2 * len(weights) * width * columns + 10 * count * columns,
        ),
        name=name,
    )(rows, *weights, *others)


def team_device(
    tokens_in,
    teacher,
    valid,
    attn_routes,
    attn_share,
    mlp_routes,
    mlp_share,
    gains,
    w_query,
    w_out,
    w_keyval,
    w_gate,
    w_up,
    w_down,
):
    low = jnp.bfloat16
    units = lax.axis_size("dp")
    plane = lax.axis_index("y")
    core = lax.axis_index("c")
    micro_count, row_count, local_width = tokens_in.shape
    half = row_count // 2
    width = local_width * 4
    team_rows = 2 * units * half
    prompt_total = units * half
    expert_count = w_query.shape[0]
    local_heads = w_query.shape[2] // HEAD
    depth = w_query.shape[1]
    hidden = w_down.shape[1]
    loss_scale = width * micro_count * row_count * units / 2.0
    scale_root = HEAD ** (-0.5)

    def exchange(parts):
        spot = 2 * plane + core
        got = [lax.dynamic_index_in_dim(parts, spot, 0, keepdims=False)]
        for step in (1, 2, 3):
            part = lax.dynamic_index_in_dim(parts, spot ^ step, 0, keepdims=False)
            got.append(lax.ppermute(part, QUAD, [(p, p ^ step) for p in range(4)]))
        for step, flag in ((1, core), (2, plane)):
            got = [jnp.where(flag == 0, got[p], got[p ^ step]) for p in range(4)]
        return got

    def to_rows(value):
        return jnp.concatenate(exchange(value.reshape(4, half, local_width)), axis=1)

    def from_rows(value):
        got = exchange(value.reshape(half, 4, local_width).transpose(1, 0, 2))
        return jnp.stack(got).reshape(micro_count, row_count, local_width)

    def collect(value):
        return lax.all_gather(value, TEAM, axis=0, tiled=True)

    def deliver(value):
        return lax.psum_scatter(value.astype(low), TEAM, scatter_dimension=0, tiled=True).astype(
            jnp.float32
        )

    def mine(value):
        return lax.dynamic_index_in_dim(value, plane, 0, keepdims=False)

    field = to_rows(tokens_in).astype(jnp.float32)
    goal = to_rows(teacher).astype(jnp.float32)
    gate_here = jnp.concatenate(
        [
            gate_rows(mine(attn_routes), mine(attn_share), expert_count),
            gate_rows(mine(mlp_routes), mine(mlp_share), expert_count),
        ],
        axis=0,
    )
    tokens_here = jnp.full((1, row_count), jnp.sum(valid).astype(jnp.float32))
    gate_here = jnp.concatenate([gate_here, tokens_here], axis=0)
    slots = jnp.arange(units, dtype=jnp.int32)[:, None, None]
    gate_all = jnp.where(slots == lax.axis_index("dp"), gate_here[None], 0.0)
    for shift in range(1, units):
        got = lax.ppermute(gate_here, "dp", [(i, (i + shift) % units) for i in range(units)])
        gate_all = jnp.where(slots == (lax.axis_index("dp") - shift) % units, got[None], gate_all)
    count = jnp.sum(gate_all[:, -1, 0])
    normed1 = (field * root_of(field) * gains[0]).astype(low)
    normed1 = collect(normed1)

    query_part = w_query.reshape(expert_count, depth, local_heads, HEAD).transpose(1, 2, 0, 3)
    out_part = w_out.reshape(expert_count, local_heads, HEAD, depth).transpose(3, 1, 0, 2)
    pair_part = w_keyval.reshape(depth, 2, local_heads, HEAD).transpose(0, 2, 1, 3)
    wide = expert_count * HEAD
    def across(value):
        return lax.ppermute(value, "y", swap_pairs(2))

    def scatter_heads(value):
        lanes = value.shape[2]
        packed = value.reshape(2, depth // 2, local_heads, lanes).transpose(0, 2, 1, 3)
        kept_half = lax.dynamic_index_in_dim(packed, core, 0, keepdims=False)
        sent_half = lax.dynamic_index_in_dim(packed, 1 - core, 0, keepdims=False)
        got_half = lax.ppermute(sent_half, "c", swap_pairs(2))
        return jnp.concatenate(
            [
                jnp.where(core == 0, kept_half, got_half),
                jnp.where(core == 0, got_half, kept_half),
            ],
            axis=0,
        )

    def deal_heads(heads):
        first = jnp.where(plane == core, heads, lax.ppermute(heads, QUAD, DEAL_FIRST))
        second = lax.ppermute(heads, QUAD, DEAL_SECOND)
        return jnp.stack(
            [jnp.where(plane == 0, first, second), jnp.where(plane == 0, second, first)], axis=1
        ).reshape(width, heads.shape[2])

    def swap_all(value, *later):
        got = lax.all_to_all(value, "dp", 0, 0, tiled=True)
        return lax.optimization_barrier((got, *later))

    def slabs_of(value):
        return value.T.reshape(units, hidden, depth)

    down_own = w_down[0]
    down_far = across(down_own)
    front_heads = scatter_heads(
        jnp.concatenate(
            [
                query_part.reshape(depth, local_heads, wide),
                pair_part.reshape(depth, local_heads, 2 * HEAD),
            ],
            axis=2,
        )
    )
    out_heads = scatter_heads(out_part.reshape(depth, local_heads, wide))
    gate_slabs, up_slabs = slabs_of(w_gate[0]), slabs_of(w_up[0])
    front_heads, gate_all, count = hold(front_heads, gate_all, count)
    front_heads, out_heads, down_far, gate_slabs, up_slabs = swap_all(
        front_heads, out_heads, down_far, gate_slabs, up_slabs
    )
    out_heads, gate_slabs = swap_all(out_heads, gate_slabs)
    front_weights = deal_heads(front_heads)
    gate_all = (
        gate_all[:, :-1].reshape(units, 2 * expert_count, 2, half)
        .transpose(1, 2, 0, 3)
        .reshape(2 * expert_count, team_rows)
    )
    feed_gate_own = lax.dynamic_index_in_dim(gate_all, expert_count + 2 * plane + core, 0, False)
    feed_gate_far = lax.dynamic_index_in_dim(gate_all, expert_count + 2 * (1 - plane) + core, 0, False)
    counted = lax.dynamic_slice_in_dim(mine(valid), core * half, half, 0).astype(jnp.float32)[:, None]

    normed1, gate_all, feed_gate_own, feed_gate_far, count, gate_slabs = lax.optimization_barrier(
        (normed1, gate_all, feed_gate_own, feed_gate_far, count, gate_slabs)
    )
    gate_slabs, up_slabs = swap_all(gate_slabs, up_slabs)
    gate_own = gate_slabs.transpose(1, 0, 2).reshape(hidden, width)
    gate_far = across(gate_own)
    attn_gate = gate_all[:expert_count].T
    blocks = team_rows // BLOCK
    gate_lines = (
        gate_all[:expert_count].reshape(expert_count, blocks, BLOCK).transpose(1, 0, 2)
    ).reshape(blocks, 1, expert_count * BLOCK)
    index = jnp.arange(team_rows, dtype=jnp.int32)
    places = jnp.where(index < prompt_total, index, prompt_total + index % half)
    cosine, sine = rope_tables(places)
    cosine = jnp.concatenate([cosine, cosine], axis=1)
    sine = jnp.concatenate([-sine, sine], axis=1)

    unit = lax.axis_index("dp")
    order = jnp.asarray([[0, 1, 2, 3], [1, 0, 2, 3], [2, 3, 1, 0], [3, 2, 1, 0]], jnp.int32)
    block = jnp.arange(blocks, dtype=jnp.int32)
    owners = (
        ((block // 2 % 2) ^ core) * units
        + lax.dynamic_index_in_dim(order, unit // 2, 0, False)[block // 4] * 2
        + ((block % 2) ^ (unit % 2))
    )

    front = dot(normed1, front_weights)
    front, out_heads = lax.optimization_barrier((front, out_heads))
    out_weights = deal_heads(out_heads)
    mixed_low, query_rot, pair_rot, log_total = attend(
        front, cosine, sine, gate_lines, units, expert_count
    )
    mixed_low, gate_own, up_slabs = lax.optimization_barrier((mixed_low, gate_own, up_slabs))
    up_slabs = lax.all_to_all(up_slabs, "dp", 0, 0, tiled=True)
    up_own = up_slabs.transpose(1, 0, 2).reshape(hidden, width)
    up_far = across(up_own)
    attn_sum = deliver(times_trans(mixed_low, out_weights))
    attn_sum, up_own, gate_far = lax.optimization_barrier((attn_sum, up_own, gate_far))
    hidden1 = field + attn_sum
    normed2 = collect((hidden1 * root_of(hidden1) * gains[1]).astype(low))

    gate_w = jnp.concatenate([gate_own, gate_far], axis=0)
    up_w = jnp.concatenate([up_own, up_far], axis=0)
    down_w = jnp.concatenate([down_own, down_far], axis=0)
    feed_share = jnp.stack([feed_gate_own, feed_gate_far], axis=1)
    gate_pre, up_pre, inner = row_call(
        open_kernel,
        normed2,
        [gate_w, up_w],
        [feed_share],
        [jnp.float32, jnp.float32, low],
        "open_rows",
    )
    result = hidden1 + scatter_run(
        lambda k, left: slot_product(owners[4 * k : 4 * k + 4], [left], [down_w]), (inner,)
    )
    layer_low = result.astype(low)
    differ = result - goal
    squared = jnp.sum(counted * differ * differ)
    grad_result = counted * differ * (2.0 * (loss_scale / (count * width)))
    grad_rows = collect(grad_result.astype(low))
    grad_rows, layer_low = hold(grad_rows, layer_low)
    layer_out = from_rows(layer_low)

    grad_gate, grad_up = row_call(
        close_kernel, grad_rows, [down_w], [feed_share, gate_pre, up_pre], [low, low], "close_rows"
    )

    def weight_sum(left, right):
        whole = times_rows(left, right)
        return whole[:hidden], whole[hidden:].astype(low)

    grad_norm2, (gate_near, gate_sent) = scatter_run(
        lambda k, one, two: slot_product(owners[4 * k : 4 * k + 4], [one, two], [gate_w, up_w]),
        (grad_gate, grad_up),
        lambda one, two: weight_sum(one, normed2),
    )
    gate_got = across(gate_sent)
    grad_norm2, grad_up, inner = hold(grad_norm2, grad_up, inner)
    up_near, up_sent = weight_sum(grad_up, normed2)
    down_near, down_sent = weight_sum(inner, grad_rows)
    gate_got, up_near, up_sent, down_near, down_sent = hold(
        gate_got, up_near, up_sent, down_near, down_sent
    )
    up_got = across(up_sent)
    grad_hidden_norm, grad_gain2 = norm_back(hidden1, gains[1], grad_norm2)
    grad_hidden1 = grad_result + grad_hidden_norm
    grad_hidden_rows = collect(grad_hidden1.astype(low))

    def rows_for_owners(value):
        return value.astype(low).reshape(hidden, units, depth).transpose(1, 0, 2)

    def own_rows(value):
        return value.reshape(units * hidden, depth).T.astype(jnp.float32)

    gate_slabs = rows_for_owners(gate_near + gate_got.astype(jnp.float32))
    gate_slabs = lax.all_to_all(gate_slabs, "dp", 0, 0, tiled=True)
    front_back = attend_back(
        dot(grad_hidden_rows, out_weights),
        attn_gate,
        query_rot,
        pair_rot,
        pair_rot[:, :HEAD].T,
        log_total,
        cosine,
        sine,
        units,
        expert_count,
    )
    front_back, gate_slabs, up_got = hold(front_back, gate_slabs, up_got)
    up_slabs = rows_for_owners(up_near + up_got.astype(jnp.float32))
    up_slabs = lax.all_to_all(up_slabs, "dp", 0, 0, tiled=True)
    out_grad = times_rows(grad_hidden_rows, mixed_low)
    grad_norm1 = deliver(times_trans(front_back, front_weights))
    front_grad = times_rows(normed1, front_back)
    grad_field_norm, grad_gain1 = norm_back(field, gains[0], grad_norm1)
    grad_field = grad_hidden1 + grad_field_norm

    def undeal_heads(value):
        halves = value.astype(low).reshape(units, 2, depth // 2, value.shape[1])
        first = lax.dynamic_index_in_dim(halves, plane, 1, keepdims=False)
        second = lax.dynamic_index_in_dim(halves, 1 - plane, 1, keepdims=False)
        first = jnp.where(plane == core, first, lax.ppermute(first, QUAD, DEAL_FIRST))
        both = first.astype(jnp.float32) + lax.ppermute(second, QUAD, BACK_SECOND).astype(
            jnp.float32
        )
        return both.astype(low)

    def gather_heads(value):
        got = value.reshape(2, local_heads, depth // 2, value.shape[2])
        own = lax.dynamic_index_in_dim(got, core, 0, keepdims=False)
        swapped = lax.ppermute(
            lax.dynamic_index_in_dim(got, 1 - core, 0, keepdims=False), "c", swap_pairs(2)
        )
        rows = jnp.concatenate(
            [jnp.where(core == 0, own, swapped), jnp.where(core == 0, swapped, own)], axis=1
        )
        return rows.astype(jnp.float32)

    front_heads = undeal_heads(front_grad)
    front_heads, out_grad = hold(front_heads, out_grad)
    out_heads = undeal_heads(out_grad)
    out_heads, down_sent = hold(out_heads, down_sent)
    down_sum = down_near + across(down_sent).astype(jnp.float32)
    front_heads, up_slabs = hold(front_heads, up_slabs)
    front_heads, out_heads = swap_all(front_heads, out_heads)
    out_heads, grad_field, grad_gain1 = hold(out_heads, grad_field, grad_gain1)
    input_grad = from_rows(grad_field)
    out_heads = lax.all_to_all(out_heads, "dp", 0, 0, tiled=True)
    grad_gate_out, grad_up_out = own_rows(gate_slabs), own_rows(up_slabs)
    front_out, out_back = gather_heads(front_heads), gather_heads(out_heads)
    grad_out = out_back.reshape(local_heads, depth, expert_count, HEAD).transpose(2, 0, 3, 1)
    grad_query_out = front_out[:, :, :wide].reshape(local_heads, depth, expert_count, HEAD).transpose(2, 1, 0, 3)
    grad_pair = front_out[:, :, wide:].reshape(local_heads, depth, 2, HEAD).transpose(1, 2, 0, 3)
    totals = jnp.stack([grad_gain1, grad_gain2, jnp.full((width,), squared)])
    for axis, size in (("c", 2), ("y", 2), ("dp", units)):
        reach = 1
        while reach < size:
            totals = totals + lax.ppermute(totals, axis, [(i, i ^ reach) for i in range(size)])
            reach *= 2
    gain_total, squared_total = totals[:2], totals[2, 0]
    return (
        layer_out,
        squared_total / (count * width),
        input_grad,
        gain_total,
        grad_query_out.reshape(w_query.shape),
        grad_out.reshape(w_out.shape),
        grad_pair.reshape(w_keyval.shape),
        grad_gate_out[None],
        grad_up_out[None],
        down_sum[None],
    )


def solution(mesh):
    units, experts = mesh.shape["dp"], mesh.shape["expert"]

    def specs(quad):
        return (
            (
                P(None, "dp", quad),
                P(None, "dp", quad),
                P(None, "dp"),
                P(None, "dp", None),
                P(None, "dp", None),
                P(None, "dp", None),
                P(None, "dp", None),
                P(),
                P(None, "dp", quad),
                P(None, quad, "dp"),
                P("dp", None, quad),
                P(quad, "dp", None),
                P(quad, "dp", None),
                P(quad, "dp", None),
            ),
            (
                P(None, "dp", quad),
                P(),
                P(None, "dp", quad),
                P(),
                P(None, "dp", quad),
                P(None, quad, "dp"),
                P("dp", None, quad),
                P(quad, "dp", None),
                P(quad, "dp", None),
                P(quad, "dp", None),
            ),
        )

    def step(*arguments):
        tokens_in, w_query = arguments[0], arguments[8]
        team = (
            experts == 4
            and tokens_in.shape[0] == 2
            and w_query.shape[2] // HEAD == 2 * units
            and w_query.shape[0] == 4
            and tokens_in.shape[1] == units * 2 * PROMPT_DEV
            and PROMPT_DEV == CLEN == BLOCK
            and units == 2 * LINE
        )
        if team:
            grid = Mesh(mesh.devices.reshape(units, 2, 2), ("dp", "y", "c"))
            ins, outs = specs(QUAD)
            body = team_device
        else:
            grid = mesh
            ins, outs = specs("expert")
            body = per_device
        return jax.shard_map(body, mesh=grid, in_specs=ins, out_specs=outs, check_vma=False)(*arguments)

    return step
```

```python
import functools

import jax
import jax.numpy as jnp
from jax import lax
from jax.experimental import pallas as pl
from jax.experimental.pallas import tpu as pltpu
from jax.sharding import Mesh
from jax.sharding import PartitionSpec as P

HEAD = 128
PROMPT_DEV = 128
CLEN = 128
CAP = 144


EPS = 1e-06
THETA = 10000.0
TRANS_DIMS = (((1,), (1,)), ((), ()))
ROWS_DIMS = (((0,), (0,)), ((), ()))


def rotate(value, places):
    half = value.shape[-1] // 2
    kind = value.dtype
    ladder = jnp.arange(half).astype(kind) * (2.0 / value.shape[-1])
    freqs = jnp.power(jnp.asarray(THETA, kind), -ladder)
    angle = places.astype(kind)[:, None] * freqs[None, :]
    cosine = jnp.cos(angle)[:, None, :]
    sine = jnp.sin(angle)[:, None, :]
    first = value[..., :half]
    second = value[..., half:]
    return jnp.concatenate(
        [first * cosine - second * sine, second * cosine + first * sine], axis=-1
    )


def rms_scale(field, gain):
    return field * lax.rsqrt(jnp.mean(field * field, axis=-1, keepdims=True) + EPS) * gain


def times_trans(left, right):
    return lax.dot_general(left, right, TRANS_DIMS, preferred_element_type=jnp.float32)


def times_rows(left, right):
    return lax.dot_general(left, right, ROWS_DIMS, preferred_element_type=jnp.float32)


def slot_plan(route, share, expert_id, slots):
    shares = share.astype(jnp.float32)
    weight = shares / jnp.sum(shares, axis=-1, keepdims=True)
    match = route == expert_id
    taken = jnp.any(match, axis=-1)
    gate_row = jnp.sum(jnp.where(match, weight, 0.0), axis=-1)
    order = jnp.cumsum(taken.astype(jnp.int32)) - 1
    placed = (order[None, :] == jnp.arange(slots, dtype=jnp.int32)[:, None]) & taken[None, :]
    row_index = jnp.arange(route.shape[0], dtype=jnp.int32)
    row_ids = jnp.sum(jnp.where(placed, row_index[None, :], 0), axis=1)
    filled = jnp.any(placed, axis=1)
    slot_gate = jnp.where(filled, gate_row[row_ids], 0.0)
    return (row_ids, slot_gate)


def per_device(
    tokens_in,
    teacher,
    valid,
    attn_routes,
    attn_share,
    mlp_routes,
    mlp_share,
    gains,
    w_query,
    w_out,
    w_keyval,
    w_gate,
    w_up,
    w_down,
):
    dp_count = lax.axis_size("dp")
    unit_index = lax.axis_index("dp")
    expert_index = lax.axis_index("expert")
    micro_count, row_count, local_width = tokens_in.shape
    full_width = local_width * lax.axis_size("expert")
    expert_count = w_query.shape[0]
    head_cols = w_query.shape[2]
    local_heads = head_cols // HEAD
    prompt_total = PROMPT_DEV * dp_count
    key_count = prompt_total + CLEN
    loss_scale = full_width * micro_count * row_count * dp_count / 2.0
    scale_root = HEAD ** (-0.5)
    within = jnp.arange(row_count, dtype=jnp.int32)
    places = jnp.where(
        within < PROMPT_DEV, unit_index * PROMPT_DEV + within, prompt_total + within - PROMPT_DEV
    )
    key_index = jnp.arange(key_count, dtype=jnp.int32)
    own_columns = jnp.arange(full_width, dtype=jnp.int32) // local_width == expert_index
    col_start = expert_index * local_width
    count = lax.psum(jnp.sum(valid).astype(jnp.float32), "dp")
    query_full, out_full, keyval_full = (
        lax.all_gather(w_query, "dp", axis=1, tiled=True),
        lax.all_gather(w_out, "dp", axis=2, tiled=True),
        lax.all_gather(w_keyval, "dp", axis=0, tiled=True),
    )
    keyval_flat = keyval_full.reshape(full_width, 2 * head_cols)
    held_query = jnp.zeros(query_full.shape, jnp.float32)
    held_out = jnp.zeros(out_full.shape, jnp.float32)
    held_keyval = jnp.zeros(keyval_full.shape, jnp.float32)
    held_gate = jnp.zeros((full_width, w_gate.shape[2]), jnp.float32)
    held_up = jnp.zeros((full_width, w_up.shape[2]), jnp.float32)
    held_down = jnp.zeros((w_down.shape[1] * dp_count, w_down.shape[2]), jnp.float32)
    gain_sum = jnp.zeros((2, full_width), jnp.float32)
    squared = jnp.zeros((), jnp.float32)
    results = []
    input_grads = []
    for micro_id in range(micro_count):
        field_low = lax.all_gather(tokens_in[micro_id], "expert", axis=1, tiled=True)
        field = field_low.astype(jnp.float32)
        normed1 = rms_scale(field, gains[0]).astype(jnp.bfloat16)
        keyval_pre = jnp.dot(normed1, keyval_flat, preferred_element_type=jnp.float32).reshape(
            row_count, 2, local_heads, HEAD
        )
        keys_here = rotate(keyval_pre[:, 0], places).astype(jnp.bfloat16)
        values_here = keyval_pre[:, 1].astype(jnp.bfloat16)
        pair_here = jnp.stack([keys_here, values_here], axis=1).reshape(row_count, 2, head_cols)
        prompt_pair = lax.all_gather(pair_here[:PROMPT_DEV], "dp", axis=0, tiled=True)
        pair_all = jnp.concatenate([prompt_pair, pair_here[PROMPT_DEV:]], axis=0).reshape(
            key_count, 2, local_heads, HEAD
        )
        keys_all = pair_all[:, 0]
        values_all = pair_all[:, 1]

        def score_block(query_rot, slot_places):
            raw = (
                jnp.einsum("chd,khd->hck", query_rot, keys_all, preferred_element_type=jnp.float32)
                * scale_root
            )
            seen = key_index[None, :] <= slot_places[:, None]
            return jnp.where(seen[None], raw, -1e30)

        attn_part = jnp.zeros((row_count, full_width), jnp.float32)
        kept = []
        for expert_id in range(expert_count):
            row_ids, slot_gate = slot_plan(
                attn_routes[micro_id], attn_share[micro_id], expert_id, CAP
            )
            chosen = jnp.take(normed1, row_ids, axis=0)
            slot_places = places[row_ids]
            query_pre = jnp.dot(
                chosen, query_full[expert_id], preferred_element_type=jnp.float32
            ).reshape(CAP, local_heads, HEAD)
            query_rot = rotate(query_pre, slot_places).astype(jnp.bfloat16)
            scores = score_block(query_rot, slot_places)
            peak = jnp.max(scores, axis=-1, keepdims=True)
            raised = jnp.exp(scores - peak)
            denom_sum = jnp.sum(raised, axis=-1, keepdims=True)
            attend = raised / denom_sum
            log_total = peak + jnp.log(denom_sum)
            mixed = jnp.einsum(
                "hck,khd->chd",
                attend.astype(jnp.bfloat16),
                values_all,
                preferred_element_type=jnp.float32,
            )
            mixed_low = mixed.reshape(CAP, head_cols).astype(jnp.bfloat16)
            project = jnp.dot(mixed_low, out_full[expert_id], preferred_element_type=jnp.float32)
            attn_part = attn_part.at[row_ids].add(project * slot_gate[:, None])
            kept.append(
                (
                    row_ids,
                    slot_gate,
                    chosen,
                    slot_places,
                    query_pre,
                    query_rot,
                    log_total,
                    mixed_low,
                )
            )
        attn_total = lax.psum(attn_part, "expert")
        hidden1 = field + attn_total
        normed2 = rms_scale(hidden1, gains[1]).astype(jnp.bfloat16)
        gate_full, up_full, down_full = (
            lax.all_gather(w_gate[0], "dp", axis=0, tiled=True),
            lax.all_gather(w_up[0], "dp", axis=0, tiled=True),
            lax.all_gather(w_down[0], "dp", axis=0, tiled=True),
        )
        feed_rows, feed_gate = slot_plan(
            mlp_routes[micro_id], mlp_share[micro_id], expert_index, CAP
        )
        feed_in = jnp.take(normed2, feed_rows, axis=0)
        gate_pre = jnp.dot(feed_in, gate_full, preferred_element_type=jnp.float32)
        up_pre = jnp.dot(feed_in, up_full, preferred_element_type=jnp.float32)
        inner = (jax.nn.silu(gate_pre) * up_pre).astype(jnp.bfloat16)
        feed_out = jnp.dot(inner, down_full, preferred_element_type=jnp.float32)
        feed_part = (
            jnp.zeros((row_count, full_width), jnp.float32)
            .at[feed_rows]
            .add(feed_out * feed_gate[:, None])
        )
        feed_shard = lax.psum_scatter(feed_part, "expert", scatter_dimension=1, tiled=True)
        hidden1_shard = lax.dynamic_slice_in_dim(hidden1, col_start, local_width, 1)
        result = hidden1_shard + feed_shard
        results.append(result.astype(jnp.bfloat16))
        differ = result - teacher[micro_id].astype(jnp.float32)
        counted = valid[micro_id].astype(jnp.float32)[:, None]
        squared = squared + jnp.sum(counted * differ * differ)
        grad_result = counted * differ * (2.0 * (loss_scale / (count * full_width)))
        grad_rows = lax.all_gather(grad_result, "expert", axis=1, tiled=True)
        gate_back, up_back, down_back = (
            lax.all_gather(w_gate[0], "dp", axis=0, tiled=True),
            lax.all_gather(w_up[0], "dp", axis=0, tiled=True),
            lax.all_gather(w_down[0], "dp", axis=0, tiled=True),
        )
        grad_feed = (jnp.take(grad_rows, feed_rows, axis=0) * feed_gate[:, None]).astype(
            jnp.bfloat16
        )
        grad_inner = times_trans(grad_feed, down_back)
        _, silu_back = jax.vjp(lambda left, right: jax.nn.silu(left) * right, gate_pre, up_pre)
        grad_gate_pre, grad_up_pre = silu_back(grad_inner)
        grad_gate_low = grad_gate_pre.astype(jnp.bfloat16)
        grad_up_low = grad_up_pre.astype(jnp.bfloat16)
        grad_feed_in = times_trans(grad_gate_low, gate_back) + times_trans(grad_up_low, up_back)
        held_gate = held_gate + times_rows(feed_in, grad_gate_low)
        held_up = held_up + times_rows(feed_in, grad_up_low)
        held_down = held_down + times_rows(inner, grad_feed)
        grad_norm2_part = (
            jnp.zeros((row_count, full_width), jnp.float32).at[feed_rows].add(grad_feed_in)
        )
        grad_norm2 = lax.psum(grad_norm2_part, "expert")
        _, norm2_back = jax.vjp(rms_scale, hidden1, gains[1])
        grad_hidden_norm, grad_gain2 = norm2_back(grad_norm2)
        grad_hidden1 = grad_rows + grad_hidden_norm
        grad_norm1_part = jnp.zeros((row_count, full_width), jnp.float32)
        grad_pair = jnp.zeros((key_count, 2, local_heads, HEAD), jnp.float32)
        term_query = []
        term_out = []
        for expert_id in range(expert_count):
            row_ids, slot_gate, chosen, slot_places, query_pre, query_rot, log_total, mixed_low = (
                kept[expert_id]
            )
            grad_project = (jnp.take(grad_hidden1, row_ids, axis=0) * slot_gate[:, None]).astype(
                jnp.bfloat16
            )
            grad_mixed = times_trans(grad_project, out_full[expert_id]).astype(jnp.bfloat16)
            term_out.append(times_rows(mixed_low, grad_project))
            grad_mixed = grad_mixed.reshape(CAP, local_heads, HEAD)
            scores = score_block(query_rot, slot_places)
            attend = jnp.exp(scores - log_total)
            attend_low = attend.astype(jnp.bfloat16)
            grad_attend = jnp.einsum(
                "chd,khd->hck", grad_mixed, values_all, preferred_element_type=jnp.float32
            )
            inner_sum = jnp.sum(attend * grad_attend, axis=-1, keepdims=True)
            grad_scores = (attend * (grad_attend - inner_sum)).astype(jnp.bfloat16)
            grad_query_rot = (
                jnp.einsum(
                    "hck,khd->chd", grad_scores, keys_all, preferred_element_type=jnp.float32
                )
                * scale_root
            )
            grad_keys = (
                jnp.einsum(
                    "hck,chd->khd", grad_scores, query_rot, preferred_element_type=jnp.float32
                )
                * scale_root
            )
            grad_values = jnp.einsum(
                "hck,chd->khd", attend_low, grad_mixed, preferred_element_type=jnp.float32
            )
            grad_pair = grad_pair + jnp.stack([grad_keys, grad_values], axis=1)
            _, query_back = jax.vjp(lambda value: rotate(value, slot_places), query_pre)
            grad_query_pre = (
                query_back(grad_query_rot)[0].astype(jnp.bfloat16).reshape(CAP, head_cols)
            )
            grad_norm1_part = grad_norm1_part.at[row_ids].add(
                times_trans(grad_query_pre, query_full[expert_id])
            )
            term_query.append(times_rows(chosen, grad_query_pre))
        grad_pair_flat = grad_pair.reshape(key_count, 2, head_cols)
        prompt_grad = lax.psum_scatter(
            grad_pair_flat[:prompt_total], "dp", scatter_dimension=0, tiled=True
        )
        pair_grad = jnp.concatenate([prompt_grad, grad_pair_flat[prompt_total:]], axis=0)
        _, key_back = jax.vjp(lambda value: rotate(value, places), keyval_pre[:, 0])
        grad_key_pre = key_back(pair_grad[:, 0].reshape(row_count, local_heads, HEAD))[0].reshape(
            row_count, head_cols
        )
        grad_pair_low = (
            jnp.stack([grad_key_pre, pair_grad[:, 1]], axis=1)
            .astype(jnp.bfloat16)
            .reshape(row_count, 2 * head_cols)
        )
        grad_norm1_part = grad_norm1_part + times_trans(grad_pair_low, keyval_flat)
        term_keyval = times_rows(normed1, grad_pair_low).reshape(full_width, 2, head_cols)
        grad_norm1 = lax.psum(grad_norm1_part.astype(jnp.bfloat16), "expert").astype(jnp.float32)
        _, norm1_back = jax.vjp(rms_scale, field, gains[0])
        grad_field_norm, grad_gain1 = norm1_back(grad_norm1)
        grad_field = grad_hidden1 + grad_field_norm
        input_grads.append(lax.dynamic_slice_in_dim(grad_field, col_start, local_width, 1))
        gain_sum = gain_sum + jnp.stack(
            [jnp.where(own_columns, grad_gain1, 0.0), jnp.where(own_columns, grad_gain2, 0.0)]
        )
        held_query = held_query + jnp.stack(term_query)
        held_out = held_out + jnp.stack(term_out)
        held_keyval = held_keyval + term_keyval
    grad_query, grad_out, grad_keyval, grad_gate, grad_up, grad_down = (
        lax.psum_scatter(
            held_query.astype(jnp.bfloat16), "dp", scatter_dimension=1, tiled=True
        ).astype(jnp.float32),
        lax.psum_scatter(
            held_out.astype(jnp.bfloat16), "dp", scatter_dimension=2, tiled=True
        ).astype(jnp.float32),
        lax.psum_scatter(
            held_keyval.astype(jnp.bfloat16), "dp", scatter_dimension=0, tiled=True
        ).astype(jnp.float32),
        lax.psum_scatter(
            held_gate.astype(jnp.bfloat16), "dp", scatter_dimension=0, tiled=True
        ).astype(jnp.float32),
        lax.psum_scatter(
            held_up.astype(jnp.bfloat16), "dp", scatter_dimension=0, tiled=True
        ).astype(jnp.float32),
        lax.psum_scatter(
            held_down.astype(jnp.bfloat16), "dp", scatter_dimension=0, tiled=True
        ).astype(jnp.float32),
    )
    gain_total, squared_total = lax.psum((gain_sum, squared), ("dp", "expert"))
    loss = squared_total / (count * full_width)
    return (
        jnp.stack(results),
        loss,
        jnp.stack(input_grads),
        gain_total,
        grad_query,
        grad_out,
        grad_keyval,
        grad_gate[None],
        grad_up[None],
        grad_down[None],
    )


def swap_pairs(size):
    return [(i, i ^ 1) for i in range(size)]


DEAL_FIRST = [(1, 2), (2, 1)]
DEAL_SECOND = [(0, 2), (1, 0), (2, 3), (3, 1)]
BACK_SECOND = [(b, a) for a, b in DEAL_SECOND]
QUAD = ("y", "c")
TEAM = ("c", "dp")


def rope_tables(places):
    half = HEAD // 2
    ladder = jnp.arange(half).astype(jnp.float32) * (2.0 / HEAD)
    freqs = jnp.power(jnp.asarray(THETA, jnp.float32), -ladder)
    angle = places.astype(jnp.float32)[:, None] * freqs[None, :]
    return jnp.cos(angle), jnp.sin(angle)


def turn(value, cosine, sine):
    half = value.shape[-1] // 2
    first = value[..., :half]
    second = value[..., half:]
    return jnp.concatenate(
        [first * cosine - second * sine, second * cosine + first * sine], axis=-1
    )


def root_of(field):
    return lax.rsqrt(jnp.mean(field * field, axis=-1, keepdims=True) + EPS)


def norm_back(field, gain, grad):
    root = root_of(field)
    scaled = grad * gain
    along = jnp.sum(scaled * field, axis=-1, keepdims=True) / field.shape[-1]
    return root * scaled - field * (root * root * root) * along, jnp.sum(grad * field * root, axis=0)


def gate_rows(route, share, expert_count):
    shares = share.astype(jnp.float32)
    weight = shares / jnp.sum(shares, axis=-1, keepdims=True)
    labels = jnp.arange(expert_count, dtype=jnp.int32)
    match = route[None, :, :] == labels[:, None, None]
    return jnp.sum(jnp.where(match, weight[None], 0.0), axis=-1)


def dot(left, right):
    return jnp.dot(left, right, preferred_element_type=jnp.float32)


BLOCK = 128
MASKED = -1e30
NT_DIMS = (((1,), (1,)), ((), ()))
ROOM = 56 * 1024 * 1024


def nt(left, right):
    return lax.dot_general(left, right, NT_DIMS, preferred_element_type=jnp.float32)


def spin(value, cosine, sine):
    return value * cosine + pltpu.roll(value, HEAD // 2, 1) * sine


def stack_experts(block, count):
    return jnp.concatenate([block[:, e * HEAD : (e + 1) * HEAD] for e in range(count)], axis=0)


def near_mask(columns):
    key_at = lax.broadcasted_iota(jnp.int32, (BLOCK, columns), 0)
    row_at = lax.broadcasted_iota(jnp.int32, (BLOCK, columns), 1) % BLOCK
    return key_at <= row_at


def attend_kernel(
    prompts, experts, front, cosine, sine, gate, mixed, query_out, pair_out, log_out, key_far, value_far
):
    step = pl.program_id(0)
    wide = experts * HEAD
    scale = HEAD ** (-0.5)

    @pl.when(step == 0)
    def _():
        key_far[...] = jnp.zeros_like(key_far)
        value_far[...] = jnp.zeros_like(value_far)

    cos, sin = cosine[...], sine[...]
    key = spin(front[:, wide : wide + HEAD], cos, sin).astype(jnp.bfloat16)
    value_up = front[:, wide + HEAD : wide + 2 * HEAD].T.astype(jnp.bfloat16)
    pair_out[:, :HEAD] = key
    pair_out[:, HEAD:] = front[:, wide + HEAD : wide + 2 * HEAD].astype(jnp.bfloat16)
    for e in range(experts):
        query_out[:, e * HEAD : (e + 1) * HEAD] = spin(
            front[:, e * HEAD : (e + 1) * HEAD], cos, sin
        ).astype(jnp.bfloat16)
    query = stack_experts(query_out[...], experts)
    near = jnp.where(near_mask(wide), nt(key, query) * scale, MASKED)
    far_tiles = jnp.minimum(step, prompts)

    def finish(width):
        far = nt(key_far[:width, :], query) * scale
        key_at = lax.broadcasted_iota(jnp.int32, far.shape, 0)
        far = jnp.where(key_at < far_tiles * BLOCK, far, MASKED)
        peak = jnp.maximum(
            jnp.max(far, axis=0, keepdims=True), jnp.max(near, axis=0, keepdims=True)
        )
        far = jnp.exp(far - peak)
        close = jnp.exp(near - peak)
        total = jnp.sum(far, axis=0, keepdims=True) + jnp.sum(close, axis=0, keepdims=True)
        mix = jnp.dot(
            value_far[:, :width], far.astype(jnp.bfloat16), preferred_element_type=jnp.float32
        ) + jnp.dot(value_up, close.astype(jnp.bfloat16), preferred_element_type=jnp.float32)
        mix = mix * (gate[0] / total)
        log_out[0] = peak + jnp.log(total)
        for e in range(experts):
            mixed[:, e * HEAD : (e + 1) * HEAD] = mix[:, e * BLOCK : (e + 1) * BLOCK].T.astype(
                jnp.bfloat16
            )

    split = prompts // 2

    @pl.when(step <= split)
    def _():
        finish(split * BLOCK)

    @pl.when(step > split)
    def _():
        finish(prompts * BLOCK)

    @pl.when(step < prompts)
    def _():
        at = pl.multiple_of(step * BLOCK, BLOCK)
        key_far[pl.ds(at, BLOCK), :] = key
        value_far[:, pl.ds(at, BLOCK)] = value_up


def attend(front, cosine, sine, gate, prompts, experts):
    rows, lanes = front.shape
    blocks = rows // BLOCK
    wide = experts * HEAD
    at = lambda i: (i, 0)
    line = pl.BlockSpec((1, 1, experts * BLOCK), lambda i: (i, 0, 0))
    return pl.pallas_call(
        functools.partial(attend_kernel, prompts, experts),
        grid=(blocks,),
        in_specs=[
            pl.BlockSpec((BLOCK, lanes), at),
            pl.BlockSpec((BLOCK, HEAD), at),
            pl.BlockSpec((BLOCK, HEAD), at),
            line,
        ],
        out_specs=[
            pl.BlockSpec((BLOCK, wide), at),
            pl.BlockSpec((BLOCK, wide), at),
            pl.BlockSpec((BLOCK, 2 * HEAD), at),
            line,
        ],
        out_shape=[
            jax.ShapeDtypeStruct((rows, wide), jnp.bfloat16),
            jax.ShapeDtypeStruct((rows, wide), jnp.bfloat16),
            jax.ShapeDtypeStruct((rows, 2 * HEAD), jnp.bfloat16),
            jax.ShapeDtypeStruct((blocks, 1, experts * BLOCK), jnp.float32),
        ],
        scratch_shapes=[
            pltpu.VMEM((prompts * BLOCK, HEAD), jnp.bfloat16),
            pltpu.VMEM((HEAD, prompts * BLOCK), jnp.bfloat16),
        ],
        compiler_params=pltpu.CompilerParams(
            dimension_semantics=("arbitrary",), vmem_limit_bytes=ROOM
        ),
        cost_estimate=pl.CostEstimate(
            flops=4 * rows * experts * HEAD * prompts * BLOCK,
            transcendentals=rows * experts * prompts * BLOCK,
            bytes_accessed=rows * lanes * 8,
        ),
        name="attend",
    )(front, cosine, sine, gate)


def attend_back_kernel(
    prompts, experts, pull, gate, query_in, pair, pair_up, log_in, cosine, sine, back, grad_key, grad_value
):
    step = pl.program_id(0)
    wide = experts * HEAD
    scale = HEAD ** (-0.5)

    @pl.when(step == 0)
    def _():
        grad_key[...] = jnp.zeros_like(grad_key)
        grad_value[...] = jnp.zeros_like(grad_value)

    at = pl.multiple_of(step * BLOCK, BLOCK)
    here = pl.ds(at, BLOCK)
    query = stack_experts(query_in[...], experts)
    grads = jnp.concatenate(
        [
            (pull[:, e * HEAD : (e + 1) * HEAD] * gate[:, e : e + 1]).astype(jnp.bfloat16)
            for e in range(experts)
        ],
        axis=0,
    )
    level = log_in[0]
    near = jnp.where(
        near_mask(wide), jnp.exp(nt(pair[here, :HEAD], query) * scale - level), 0.0
    )
    near_pull = nt(pair[here, HEAD:], grads)
    far_tiles = jnp.minimum(step, prompts)

    def finish(width):
        far = jnp.exp(nt(pair[:width, :HEAD], query) * scale - level)
        key_at = lax.broadcasted_iota(jnp.int32, far.shape, 0)
        far = jnp.where(key_at < far_tiles * BLOCK, far, 0.0)
        far_pull = nt(pair[:width, HEAD:], grads)
        along = jnp.sum(far * far_pull, axis=0, keepdims=True) + jnp.sum(
            near * near_pull, axis=0, keepdims=True
        )
        far_ds = (far * (far_pull - along)).astype(jnp.bfloat16)
        near_ds = (near * (near_pull - along)).astype(jnp.bfloat16)
        turned = (
            jnp.dot(pair_up[:, :width], far_ds, preferred_element_type=jnp.float32)
            + jnp.dot(pair_up[:, here], near_ds, preferred_element_type=jnp.float32)
        ) * scale
        cos, sin = cosine[here, :], sine[here, :]
        for e in range(experts):
            back[here, e * HEAD : (e + 1) * HEAD] = spin(
                turned[:, e * BLOCK : (e + 1) * BLOCK].T, cos, -sin
            ).astype(jnp.bfloat16)
        grad_key[:width, :] += jnp.dot(far_ds, query, preferred_element_type=jnp.float32)
        grad_value[:width, :] += jnp.dot(
            far.astype(jnp.bfloat16), grads, preferred_element_type=jnp.float32
        )
        grad_key[here, :] += jnp.dot(near_ds, query, preferred_element_type=jnp.float32)
        grad_value[here, :] += jnp.dot(
            near.astype(jnp.bfloat16), grads, preferred_element_type=jnp.float32
        )

    split = prompts // 2

    @pl.when(step <= split)
    def _():
        finish(split * BLOCK)

    @pl.when(step > split)
    def _():
        finish(prompts * BLOCK)

    @pl.when(step == pl.num_programs(0) - 1)
    def _():
        back[:, wide : wide + HEAD] = spin(
            grad_key[...] * scale, cosine[...], -sine[...]
        ).astype(jnp.bfloat16)
        back[:, wide + HEAD :] = grad_value[...].astype(jnp.bfloat16)


def attend_back(pull, gate, query, pair, pair_up, log_total, cosine, sine, prompts, experts):
    rows, wide = query.shape
    blocks = rows // BLOCK
    at = lambda i: (i, 0)
    still = lambda i: (0, 0)
    line = pl.BlockSpec((1, 1, experts * BLOCK), lambda i: (i, 0, 0))
    return pl.pallas_call(
        functools.partial(attend_back_kernel, prompts, experts),
        grid=(blocks,),
        in_specs=[
            pl.BlockSpec((BLOCK, wide), at),
            pl.BlockSpec((BLOCK, experts), at),
            pl.BlockSpec((BLOCK, wide), at),
            pl.BlockSpec((rows, 2 * HEAD), still),
            pl.BlockSpec((HEAD, rows), still),
            line,
            pl.BlockSpec((rows, HEAD), still),
            pl.BlockSpec((rows, HEAD), still),
        ],
        out_specs=pl.BlockSpec((rows, wide + 2 * HEAD), still),
        out_shape=jax.ShapeDtypeStruct((rows, wide + 2 * HEAD), jnp.bfloat16),
        scratch_shapes=[
            pltpu.VMEM((rows, HEAD), jnp.float32),
            pltpu.VMEM((rows, HEAD), jnp.float32),
        ],
        compiler_params=pltpu.CompilerParams(
            dimension_semantics=("arbitrary",), vmem_limit_bytes=ROOM
        ),
        cost_estimate=pl.CostEstimate(
            flops=10 * rows * experts * HEAD * prompts * BLOCK,
            transcendentals=rows * experts * prompts * BLOCK,
            bytes_accessed=rows * wide * 12,
        ),
        name="attend_back",
    )(pull, gate, query, pair, pair_up, log_total, cosine, sine)


LINE = 4
SIDES = [(i, i ^ 1) for i in range(2 * LINE)]


def hops(moves):
    return [(2 * a + x, 2 * b + x) for a, b in moves for x in (0, 1)]


def hold(*values):
    return lax.optimization_barrier(values)


def to_side(value):
    return lax.ppermute(value, "dp", SIDES)


def to_core(value):
    return lax.ppermute(value, "c", swap_pairs(2))


def scatter_run(make, given, fill=None):
    spot = lax.axis_index("dp") // 2
    low = jnp.bfloat16
    wide = lambda value: value.astype(jnp.float32)

    def rise(value, last):
        return lax.ppermute(value, "dp", hops([(a, a + 1) for a in range(last)]))

    def fall(value, last):
        return lax.ppermute(value, "dp", hops([(LINE - 1 - a, LINE - 2 - a) for a in range(last)]))

    def cut(value):
        middle = value.shape[0] // 2
        return value[:middle], value[middle:]

    here3, there3 = make(3, *given)
    there3, *given = hold(there3, *given)
    got3, (here2, there2) = hold(to_core(there3), make(2, *given))
    mine3, other3 = cut(here3 + got3)
    other3, there2, *given = hold(other3, there2, *given)
    side3, both2, (here1, there1) = hold(
        to_side(other3), here2 + to_core(there2), make(1, *given)
    )
    mine2, other2 = cut(both2)
    other2, there1, *given = hold(other2, there1, *given)
    row3 = wide(mine3) + wide(side3)
    send3 = row3.astype(low)
    side2, up, down, both1, (here0, there0) = hold(
        to_side(other2), rise(send3, 1), fall(send3, 1), here1 + to_core(there1), make(0, *given)
    )
    mine1, other1 = cut(both1)
    other1, there0, *given = hold(other1, there0, *given)
    row2 = wide(mine2) + wide(side2)
    send_up = (jnp.where(spot == 0, row2, row3) + wide(up)).astype(low)
    send_down = (jnp.where(spot == LINE - 1, row2, row3) + wide(down)).astype(low)
    side1, up, down, both0 = hold(
        to_side(other1), rise(send_up, 2), fall(send_down, 2), here0 + to_core(there0)
    )
    mine0, other0 = cut(both0)
    other0, *given = hold(other0, *given)
    row1 = wide(mine1) + wide(side1)
    send_up = (jnp.where(spot == 1, row2, row1) + wide(up)).astype(low)
    send_down = (jnp.where(spot == LINE - 2, row2, row1) + wide(down)).astype(low)
    filled = fill(*given) if fill else ()
    side0, up, down, filled = hold(to_side(other0), rise(send_up, 3), fall(send_down, 3), filled)
    total = wide(mine0) + wide(side0) + wide(up) + wide(down)
    return (total, filled) if fill else total


LANE_STEP = 512


def product_kernel(terms, places, *refs):
    lefts, rights, out = refs[: 4 * terms], refs[4 * terms : 5 * terms], refs[-2]
    far_out = refs[-1]
    total = None
    for term in range(terms):
        rows = jnp.concatenate([lefts[4 * term + j][...] for j in range(4)], axis=0)
        part = jnp.dot(rows, rights[term][...], preferred_element_type=jnp.float32)
        total = part if total is None else total + part
    middle = out.shape[0]
    out[...] = total[:middle].astype(out.dtype)
    far_out[...] = total[middle:].astype(out.dtype)


def slot_product(places, lefts, rights):
    width = rights[0].shape[1]
    block = lambda j: (lambda i, places: (places[j], 0))
    return pl.pallas_call(
        functools.partial(product_kernel, len(lefts)),
        grid_spec=pltpu.PrefetchScalarGridSpec(
            num_scalar_prefetch=1,
            grid=(width // LANE_STEP,),
            in_specs=[
                pl.BlockSpec((BLOCK, left.shape[1]), block(j)) for left in lefts for j in range(4)
            ]
            + [
                pl.BlockSpec((right.shape[0], LANE_STEP), lambda i, places: (0, i))
                for right in rights
            ],
            out_specs=[pl.BlockSpec((2 * BLOCK, LANE_STEP), lambda i, places: (0, i))] * 2,
        ),
        out_shape=[jax.ShapeDtypeStruct((2 * BLOCK, width), jnp.bfloat16)] * 2,
        compiler_params=pltpu.CompilerParams(
            dimension_semantics=("arbitrary",), vmem_limit_bytes=ROOM
        ),
        cost_estimate=pl.CostEstimate(
            flops=sum(8 * BLOCK * right.shape[0] * width for right in rights),
            transcendentals=0,
            bytes_accessed=sum(2 * right.size + 8 * BLOCK * right.shape[0] for right in rights),
        ),
        name="slot_product",
    )(places, *[left for left in lefts for _ in range(4)], *rights)


ROW_STEP = 256


def share_lanes(share, columns):
    lane = lax.broadcasted_iota(jnp.int32, (share.shape[0], columns), 1)
    return jnp.where(lane < columns // 2, share[:, 0:1], share[:, 1:2])


def open_kernel(rows, gate_w, up_w, share, gate_out, up_out, inner_out):
    gate = nt(rows[...], gate_w[...])
    up = nt(rows[...], up_w[...])
    gate_out[...] = gate.astype(gate_out.dtype)
    up_out[...] = up.astype(up_out.dtype)
    inner_out[...] = (
        gate / (1.0 + jnp.exp(-gate)) * up * share_lanes(share[...], gate.shape[1])
    ).astype(jnp.bfloat16)


def close_kernel(rows, down_w, share, gate_in, up_in, gate_out, up_out):
    gate = gate_in[...].astype(jnp.float32)
    up = up_in[...].astype(jnp.float32)
    pull = nt(rows[...], down_w[...]) * share_lanes(share[...], gate.shape[1])
    sigma = 1.0 / (1.0 + jnp.exp(-gate))
    gate_out[...] = (pull * up * sigma * (1.0 + gate * (1.0 - sigma))).astype(jnp.bfloat16)
    up_out[...] = (pull * gate * sigma).astype(jnp.bfloat16)


def row_call(kernel, rows, weights, others, kinds, name):
    count, width = rows.shape
    columns = weights[0].shape[0]
    tile = lambda lanes: pl.BlockSpec((ROW_STEP, lanes), lambda i: (i, 0))
    return pl.pallas_call(
        kernel,
        grid=(count // ROW_STEP,),
        in_specs=[tile(width)]
        + [
            pl.BlockSpec(weight.shape, lambda i: (0, 0), pipeline_mode=pl.Buffered(1))
            for weight in weights
        ]
        + [tile(other.shape[1]) for other in others],
        out_specs=[tile(columns) for _ in kinds],
        out_shape=[jax.ShapeDtypeStruct((count, columns), kind) for kind in kinds],
        compiler_params=pltpu.CompilerParams(
            dimension_semantics=("arbitrary",), vmem_limit_bytes=ROOM
        ),
        cost_estimate=pl.CostEstimate(
            flops=2 * len(weights) * count * width * columns,
            transcendentals=count * columns,
            bytes_accessed=2 * len(weights) * width * columns + 10 * count * columns,
        ),
        name=name,
    )(rows, *weights, *others)


def team_device(
    tokens_in,
    teacher,
    valid,
    attn_routes,
    attn_share,
    mlp_routes,
    mlp_share,
    gains,
    w_query,
    w_out,
    w_keyval,
    w_gate,
    w_up,
    w_down,
):
    low = jnp.bfloat16
    units = lax.axis_size("dp")
    plane = lax.axis_index("y")
    core = lax.axis_index("c")
    micro_count, row_count, local_width = tokens_in.shape
    half = row_count // 2
    width = local_width * 4
    team_rows = 2 * units * half
    prompt_total = units * half
    expert_count = w_query.shape[0]
    local_heads = w_query.shape[2] // HEAD
    depth = w_query.shape[1]
    hidden = w_down.shape[1]
    loss_scale = width * micro_count * row_count * units / 2.0
    scale_root = HEAD ** (-0.5)

    def exchange(parts):
        spot = 2 * plane + core
        got = [lax.dynamic_index_in_dim(parts, spot, 0, keepdims=False)]
        for step in (1, 2, 3):
            part = lax.dynamic_index_in_dim(parts, spot ^ step, 0, keepdims=False)
            got.append(lax.ppermute(part, QUAD, [(p, p ^ step) for p in range(4)]))
        for step, flag in ((1, core), (2, plane)):
            got = [jnp.where(flag == 0, got[p], got[p ^ step]) for p in range(4)]
        return got

    def to_rows(value):
        return jnp.concatenate(exchange(value.reshape(4, half, local_width)), axis=1)

    def from_rows(value):
        got = exchange(value.reshape(half, 4, local_width).transpose(1, 0, 2))
        return jnp.stack(got).reshape(micro_count, row_count, local_width)

    def collect(value):
        return lax.all_gather(value, TEAM, axis=0, tiled=True)

    def deliver(value):
        return lax.psum_scatter(value.astype(low), TEAM, scatter_dimension=0, tiled=True).astype(
            jnp.float32
        )

    def mine(value):
        return lax.dynamic_index_in_dim(value, plane, 0, keepdims=False)

    field = to_rows(tokens_in).astype(jnp.float32)
    goal = to_rows(teacher).astype(jnp.float32)
    gate_here = jnp.concatenate(
        [
            gate_rows(mine(attn_routes), mine(attn_share), expert_count),
            gate_rows(mine(mlp_routes), mine(mlp_share), expert_count),
        ],
        axis=0,
    )
    tokens_here = jnp.full((1, row_count), jnp.sum(valid).astype(jnp.float32))
    gate_here = jnp.concatenate([gate_here, tokens_here], axis=0)
    slots = jnp.arange(units, dtype=jnp.int32)[:, None, None]
    gate_all = jnp.where(slots == lax.axis_index("dp"), gate_here[None], 0.0)
    for shift in range(1, units):
        got = lax.ppermute(gate_here, "dp", [(i, (i + shift) % units) for i in range(units)])
        gate_all = jnp.where(slots == (lax.axis_index("dp") - shift) % units, got[None], gate_all)
    count = jnp.sum(gate_all[:, -1, 0])
    normed1 = (field * root_of(field) * gains[0]).astype(low)
    normed1 = collect(normed1)

    query_part = w_query.reshape(expert_count, depth, local_heads, HEAD).transpose(1, 2, 0, 3)
    out_part = w_out.reshape(expert_count, local_heads, HEAD, depth).transpose(3, 1, 0, 2)
    pair_part = w_keyval.reshape(depth, 2, local_heads, HEAD).transpose(0, 2, 1, 3)
    wide = expert_count * HEAD
    def across(value):
        return lax.ppermute(value, "y", swap_pairs(2))

    def scatter_heads(value):
        lanes = value.shape[2]
        packed = value.reshape(2, depth // 2, local_heads, lanes).transpose(0, 2, 1, 3)
        kept_half = lax.dynamic_index_in_dim(packed, core, 0, keepdims=False)
        sent_half = lax.dynamic_index_in_dim(packed, 1 - core, 0, keepdims=False)
        got_half = lax.ppermute(sent_half, "c", swap_pairs(2))
        return jnp.concatenate(
            [
                jnp.where(core == 0, kept_half, got_half),
                jnp.where(core == 0, got_half, kept_half),
            ],
            axis=0,
        )

    def deal_heads(heads):
        first = jnp.where(plane == core, heads, lax.ppermute(heads, QUAD, DEAL_FIRST))
        second = lax.ppermute(heads, QUAD, DEAL_SECOND)
        return jnp.stack(
            [jnp.where(plane == 0, first, second), jnp.where(plane == 0, second, first)], axis=1
        ).reshape(width, heads.shape[2])

    def swap_all(value, *later):
        got = lax.all_to_all(value, "dp", 0, 0, tiled=True)
        return lax.optimization_barrier((got, *later))

    def slabs_of(value):
        return value.T.reshape(units, hidden, depth)

    down_own = w_down[0]
    down_far = across(down_own)
    front_heads = scatter_heads(
        jnp.concatenate(
            [
                query_part.reshape(depth, local_heads, wide),
                pair_part.reshape(depth, local_heads, 2 * HEAD),
            ],
            axis=2,
        )
    )
    out_heads = scatter_heads(out_part.reshape(depth, local_heads, wide))
    gate_slabs, up_slabs = slabs_of(w_gate[0]), slabs_of(w_up[0])
    front_heads, gate_all, count = hold(front_heads, gate_all, count)
    front_heads, out_heads, down_far, gate_slabs, up_slabs = swap_all(
        front_heads, out_heads, down_far, gate_slabs, up_slabs
    )
    out_heads, gate_slabs = swap_all(out_heads, gate_slabs)
    front_weights = deal_heads(front_heads)
    gate_all = (
        gate_all[:, :-1].reshape(units, 2 * expert_count, 2, half)
        .transpose(1, 2, 0, 3)
        .reshape(2 * expert_count, team_rows)
    )
    feed_gate_own = lax.dynamic_index_in_dim(gate_all, expert_count + 2 * plane + core, 0, False)
    feed_gate_far = lax.dynamic_index_in_dim(gate_all, expert_count + 2 * (1 - plane) + core, 0, False)
    counted = lax.dynamic_slice_in_dim(mine(valid), core * half, half, 0).astype(jnp.float32)[:, None]

    normed1, gate_all, feed_gate_own, feed_gate_far, count, gate_slabs = lax.optimization_barrier(
        (normed1, gate_all, feed_gate_own, feed_gate_far, count, gate_slabs)
    )
    gate_slabs, up_slabs = swap_all(gate_slabs, up_slabs)
    gate_own = gate_slabs.transpose(1, 0, 2).reshape(hidden, width)
    gate_far = across(gate_own)
    attn_gate = gate_all[:expert_count].T
    blocks = team_rows // BLOCK
    gate_lines = (
        gate_all[:expert_count].reshape(expert_count, blocks, BLOCK).transpose(1, 0, 2)
    ).reshape(blocks, 1, expert_count * BLOCK)
    index = jnp.arange(team_rows, dtype=jnp.int32)
    places = jnp.where(index < prompt_total, index, prompt_total + index % half)
    cosine, sine = rope_tables(places)
    cosine = jnp.concatenate([cosine, cosine], axis=1)
    sine = jnp.concatenate([-sine, sine], axis=1)

    unit = lax.axis_index("dp")
    order = jnp.asarray([[0, 1, 2, 3], [1, 0, 2, 3], [2, 3, 1, 0], [3, 2, 1, 0]], jnp.int32)
    block = jnp.arange(blocks, dtype=jnp.int32)
    owners = (
        ((block // 2 % 2) ^ core) * units
        + lax.dynamic_index_in_dim(order, unit // 2, 0, False)[block // 4] * 2
        + ((block % 2) ^ (unit % 2))
    )

    front = dot(normed1, front_weights)
    front, out_heads = lax.optimization_barrier((front, out_heads))
    out_weights = deal_heads(out_heads)
    mixed_low, query_rot, pair_rot, log_total = attend(
        front, cosine, sine, gate_lines, units, expert_count
    )
    mixed_low, gate_own, up_slabs = lax.optimization_barrier((mixed_low, gate_own, up_slabs))
    up_slabs = lax.all_to_all(up_slabs, "dp", 0, 0, tiled=True)
    up_own = up_slabs.transpose(1, 0, 2).reshape(hidden, width)
    up_far = across(up_own)
    attn_sum = deliver(times_trans(mixed_low, out_weights))
    attn_sum, up_own, gate_far = lax.optimization_barrier((attn_sum, up_own, gate_far))
    hidden1 = field + attn_sum
    normed2 = collect((hidden1 * root_of(hidden1) * gains[1]).astype(low))

    gate_w = jnp.concatenate([gate_own, gate_far], axis=0)
    up_w = jnp.concatenate([up_own, up_far], axis=0)
    down_w = jnp.concatenate([down_own, down_far], axis=0)
    feed_share = jnp.stack([feed_gate_own, feed_gate_far], axis=1)
    gate_pre, up_pre, inner = row_call(
        open_kernel,
        normed2,
        [gate_w, up_w],
        [feed_share],
        [low, low, low],
        "open_rows",
    )
    result = hidden1 + scatter_run(
        lambda k, left: slot_product(owners[4 * k : 4 * k + 4], [left], [down_w]), (inner,)
    )
    layer_low = result.astype(low)
    differ = result - goal
    squared = jnp.sum(counted * differ * differ)
    grad_result = counted * differ * (2.0 * (loss_scale / (count * width)))
    grad_rows = collect(grad_result.astype(low))
    grad_rows, layer_low = hold(grad_rows, layer_low)
    layer_out = from_rows(layer_low)

    grad_gate, grad_up = row_call(
        close_kernel, grad_rows, [down_w], [feed_share, gate_pre, up_pre], [low, low], "close_rows"
    )

    def weight_sum(left, right):
        whole = times_rows(left, right)
        return whole[:hidden], whole[hidden:].astype(low)

    grad_norm2, (gate_near, gate_sent) = scatter_run(
        lambda k, one, two: slot_product(owners[4 * k : 4 * k + 4], [one, two], [gate_w, up_w]),
        (grad_gate, grad_up),
        lambda one, two: weight_sum(one, normed2),
    )
    gate_got = across(gate_sent)
    grad_norm2, grad_up, inner = hold(grad_norm2, grad_up, inner)
    up_near, up_sent = weight_sum(grad_up, normed2)
    down_near, down_sent = weight_sum(inner, grad_rows)
    gate_got, up_near, up_sent, down_near, down_sent = hold(
        gate_got, up_near, up_sent, down_near, down_sent
    )
    up_got = across(up_sent)
    grad_hidden_norm, grad_gain2 = norm_back(hidden1, gains[1], grad_norm2)
    grad_hidden1 = grad_result + grad_hidden_norm
    grad_hidden_rows = collect(grad_hidden1.astype(low))

    def rows_for_owners(value):
        return value.astype(low).reshape(hidden, units, depth).transpose(1, 0, 2)

    def own_rows(value):
        return value.reshape(units * hidden, depth).T.astype(jnp.float32)

    gate_slabs = rows_for_owners(gate_near + gate_got.astype(jnp.float32))
    gate_slabs = lax.all_to_all(gate_slabs, "dp", 0, 0, tiled=True)
    front_back = attend_back(
        dot(grad_hidden_rows, out_weights),
        attn_gate,
        query_rot,
        pair_rot,
        pair_rot[:, :HEAD].T,
        log_total,
        cosine,
        sine,
        units,
        expert_count,
    )
    front_back, gate_slabs = hold(front_back, gate_slabs)
    up_slabs = rows_for_owners(up_near + up_got.astype(jnp.float32))
    up_slabs = lax.all_to_all(up_slabs, "dp", 0, 0, tiled=True)
    out_grad = times_rows(grad_hidden_rows, mixed_low)
    grad_norm1 = deliver(times_trans(front_back, front_weights))
    front_grad = times_rows(normed1, front_back)
    grad_field_norm, grad_gain1 = norm_back(field, gains[0], grad_norm1)
    grad_field = grad_hidden1 + grad_field_norm

    def undeal_heads(value):
        halves = value.astype(low).reshape(units, 2, depth // 2, value.shape[1])
        first = lax.dynamic_index_in_dim(halves, plane, 1, keepdims=False)
        second = lax.dynamic_index_in_dim(halves, 1 - plane, 1, keepdims=False)
        first = jnp.where(plane == core, first, lax.ppermute(first, QUAD, DEAL_FIRST))
        both = first.astype(jnp.float32) + lax.ppermute(second, QUAD, BACK_SECOND).astype(
            jnp.float32
        )
        return both.astype(low)

    def gather_heads(value):
        got = value.reshape(2, local_heads, depth // 2, value.shape[2])
        own = lax.dynamic_index_in_dim(got, core, 0, keepdims=False)
        swapped = lax.ppermute(
            lax.dynamic_index_in_dim(got, 1 - core, 0, keepdims=False), "c", swap_pairs(2)
        )
        rows = jnp.concatenate(
            [jnp.where(core == 0, own, swapped), jnp.where(core == 0, swapped, own)], axis=1
        )
        return rows.astype(jnp.float32)

    middle = hidden // 2
    front_heads = undeal_heads(front_grad)
    front_heads, out_grad, down_sent = hold(front_heads, out_grad, down_sent)
    down_first = across(down_sent[:middle])
    front_heads, up_slabs, down_first = hold(front_heads, up_slabs, down_first)
    out_heads = undeal_heads(out_grad)
    out_heads, down_sent = hold(out_heads, down_sent)
    down_second = across(down_sent[middle:])
    front_heads, out_heads = swap_all(front_heads, out_heads)
    out_heads, grad_field, grad_gain1, down_second = hold(
        out_heads, grad_field, grad_gain1, down_second
    )
    input_grad = from_rows(grad_field)
    out_heads = lax.all_to_all(out_heads, "dp", 0, 0, tiled=True)
    down_got = jnp.concatenate([down_first, down_second], axis=0)
    down_sum = down_near + down_got.astype(jnp.float32)
    grad_gate_out, grad_up_out = own_rows(gate_slabs), own_rows(up_slabs)
    front_out, out_back = gather_heads(front_heads), gather_heads(out_heads)
    grad_out = out_back.reshape(local_heads, depth, expert_count, HEAD).transpose(2, 0, 3, 1)
    grad_query_out = front_out[:, :, :wide].reshape(local_heads, depth, expert_count, HEAD).transpose(2, 1, 0, 3)
    grad_pair = front_out[:, :, wide:].reshape(local_heads, depth, 2, HEAD).transpose(1, 2, 0, 3)
    totals = jnp.stack([grad_gain1, grad_gain2, jnp.full((width,), squared)])
    for axis, size in (("c", 2), ("y", 2), ("dp", units)):
        reach = 1
        while reach < size:
            totals = totals + lax.ppermute(totals, axis, [(i, i ^ reach) for i in range(size)])
            reach *= 2
    gain_total, squared_total = totals[:2], totals[2, 0]
    return (
        layer_out,
        squared_total / (count * width),
        input_grad,
        gain_total,
        grad_query_out.reshape(w_query.shape),
        grad_out.reshape(w_out.shape),
        grad_pair.reshape(w_keyval.shape),
        grad_gate_out[None],
        grad_up_out[None],
        down_sum[None],
    )


def solution(mesh):
    units, experts = mesh.shape["dp"], mesh.shape["expert"]

    def specs(quad):
        return (
            (
                P(None, "dp", quad),
                P(None, "dp", quad),
                P(None, "dp"),
                P(None, "dp", None),
                P(None, "dp", None),
                P(None, "dp", None),
                P(None, "dp", None),
                P(),
                P(None, "dp", quad),
                P(None, quad, "dp"),
                P("dp", None, quad),
                P(quad, "dp", None),
                P(quad, "dp", None),
                P(quad, "dp", None),
            ),
            (
                P(None, "dp", quad),
                P(),
                P(None, "dp", quad),
                P(),
                P(None, "dp", quad),
                P(None, quad, "dp"),
                P("dp", None, quad),
                P(quad, "dp", None),
                P(quad, "dp", None),
                P(quad, "dp", None),
            ),
        )

    def step(*arguments):
        tokens_in, w_query = arguments[0], arguments[8]
        team = (
            experts == 4
            and tokens_in.shape[0] == 2
            and w_query.shape[2] // HEAD == 2 * units
            and w_query.shape[0] == 4
            and tokens_in.shape[1] == units * 2 * PROMPT_DEV
            and PROMPT_DEV == CLEN == BLOCK
            and units == 2 * LINE
        )
        if team:
            grid = Mesh(mesh.devices.reshape(units, 2, 2), ("dp", "y", "c"))
            ins, outs = specs(QUAD)
            body = team_device
        else:
            grid = mesh
            ins, outs = specs("expert")
            body = per_device
        return jax.shard_map(body, mesh=grid, in_specs=ins, out_specs=outs, check_vma=False)(*arguments)

    return step
```

```python
import functools

import jax
import jax.numpy as jnp
from jax import lax
from jax.experimental import pallas as pl
from jax.experimental.pallas import tpu as pltpu
from jax.sharding import Mesh
from jax.sharding import PartitionSpec as P

HEAD = 128
PROMPT_DEV = 128
CLEN = 128
CAP = 144


EPS = 1e-06
THETA = 10000.0
TRANS_DIMS = (((1,), (1,)), ((), ()))
ROWS_DIMS = (((0,), (0,)), ((), ()))


def rotate(value, places):
    half = value.shape[-1] // 2
    kind = value.dtype
    ladder = jnp.arange(half).astype(kind) * (2.0 / value.shape[-1])
    freqs = jnp.power(jnp.asarray(THETA, kind), -ladder)
    angle = places.astype(kind)[:, None] * freqs[None, :]
    cosine = jnp.cos(angle)[:, None, :]
    sine = jnp.sin(angle)[:, None, :]
    first = value[..., :half]
    second = value[..., half:]
    return jnp.concatenate(
        [first * cosine - second * sine, second * cosine + first * sine], axis=-1
    )


def rms_scale(field, gain):
    return field * lax.rsqrt(jnp.mean(field * field, axis=-1, keepdims=True) + EPS) * gain


def times_trans(left, right):
    return lax.dot_general(left, right, TRANS_DIMS, preferred_element_type=jnp.float32)


def times_rows(left, right):
    return lax.dot_general(left, right, ROWS_DIMS, preferred_element_type=jnp.float32)


def slot_plan(route, share, expert_id, slots):
    shares = share.astype(jnp.float32)
    weight = shares / jnp.sum(shares, axis=-1, keepdims=True)
    match = route == expert_id
    taken = jnp.any(match, axis=-1)
    gate_row = jnp.sum(jnp.where(match, weight, 0.0), axis=-1)
    order = jnp.cumsum(taken.astype(jnp.int32)) - 1
    placed = (order[None, :] == jnp.arange(slots, dtype=jnp.int32)[:, None]) & taken[None, :]
    row_index = jnp.arange(route.shape[0], dtype=jnp.int32)
    row_ids = jnp.sum(jnp.where(placed, row_index[None, :], 0), axis=1)
    filled = jnp.any(placed, axis=1)
    slot_gate = jnp.where(filled, gate_row[row_ids], 0.0)
    return (row_ids, slot_gate)


def per_device(
    tokens_in,
    teacher,
    valid,
    attn_routes,
    attn_share,
    mlp_routes,
    mlp_share,
    gains,
    w_query,
    w_out,
    w_keyval,
    w_gate,
    w_up,
    w_down,
):
    dp_count = lax.axis_size("dp")
    unit_index = lax.axis_index("dp")
    expert_index = lax.axis_index("expert")
    micro_count, row_count, local_width = tokens_in.shape
    full_width = local_width * lax.axis_size("expert")
    expert_count = w_query.shape[0]
    head_cols = w_query.shape[2]
    local_heads = head_cols // HEAD
    prompt_total = PROMPT_DEV * dp_count
    key_count = prompt_total + CLEN
    loss_scale = full_width * micro_count * row_count * dp_count / 2.0
    scale_root = HEAD ** (-0.5)
    within = jnp.arange(row_count, dtype=jnp.int32)
    places = jnp.where(
        within < PROMPT_DEV, unit_index * PROMPT_DEV + within, prompt_total + within - PROMPT_DEV
    )
    key_index = jnp.arange(key_count, dtype=jnp.int32)
    own_columns = jnp.arange(full_width, dtype=jnp.int32) // local_width == expert_index
    col_start = expert_index * local_width
    count = lax.psum(jnp.sum(valid).astype(jnp.float32), "dp")
    query_full, out_full, keyval_full = (
        lax.all_gather(w_query, "dp", axis=1, tiled=True),
        lax.all_gather(w_out, "dp", axis=2, tiled=True),
        lax.all_gather(w_keyval, "dp", axis=0, tiled=True),
    )
    keyval_flat = keyval_full.reshape(full_width, 2 * head_cols)
    held_query = jnp.zeros(query_full.shape, jnp.float32)
    held_out = jnp.zeros(out_full.shape, jnp.float32)
    held_keyval = jnp.zeros(keyval_full.shape, jnp.float32)
    held_gate = jnp.zeros((full_width, w_gate.shape[2]), jnp.float32)
    held_up = jnp.zeros((full_width, w_up.shape[2]), jnp.float32)
    held_down = jnp.zeros((w_down.shape[1] * dp_count, w_down.shape[2]), jnp.float32)
    gain_sum = jnp.zeros((2, full_width), jnp.float32)
    squared = jnp.zeros((), jnp.float32)
    results = []
    input_grads = []
    for micro_id in range(micro_count):
        field_low = lax.all_gather(tokens_in[micro_id], "expert", axis=1, tiled=True)
        field = field_low.astype(jnp.float32)
        normed1 = rms_scale(field, gains[0]).astype(jnp.bfloat16)
        keyval_pre = jnp.dot(normed1, keyval_flat, preferred_element_type=jnp.float32).reshape(
            row_count, 2, local_heads, HEAD
        )
        keys_here = rotate(keyval_pre[:, 0], places).astype(jnp.bfloat16)
        values_here = keyval_pre[:, 1].astype(jnp.bfloat16)
        pair_here = jnp.stack([keys_here, values_here], axis=1).reshape(row_count, 2, head_cols)
        prompt_pair = lax.all_gather(pair_here[:PROMPT_DEV], "dp", axis=0, tiled=True)
        pair_all = jnp.concatenate([prompt_pair, pair_here[PROMPT_DEV:]], axis=0).reshape(
            key_count, 2, local_heads, HEAD
        )
        keys_all = pair_all[:, 0]
        values_all = pair_all[:, 1]

        def score_block(query_rot, slot_places):
            raw = (
                jnp.einsum("chd,khd->hck", query_rot, keys_all, preferred_element_type=jnp.float32)
                * scale_root
            )
            seen = key_index[None, :] <= slot_places[:, None]
            return jnp.where(seen[None], raw, -1e30)

        attn_part = jnp.zeros((row_count, full_width), jnp.float32)
        kept = []
        for expert_id in range(expert_count):
            row_ids, slot_gate = slot_plan(
                attn_routes[micro_id], attn_share[micro_id], expert_id, CAP
            )
            chosen = jnp.take(normed1, row_ids, axis=0)
            slot_places = places[row_ids]
            query_pre = jnp.dot(
                chosen, query_full[expert_id], preferred_element_type=jnp.float32
            ).reshape(CAP, local_heads, HEAD)
            query_rot = rotate(query_pre, slot_places).astype(jnp.bfloat16)
            scores = score_block(query_rot, slot_places)
            peak = jnp.max(scores, axis=-1, keepdims=True)
            raised = jnp.exp(scores - peak)
            denom_sum = jnp.sum(raised, axis=-1, keepdims=True)
            attend = raised / denom_sum
            log_total = peak + jnp.log(denom_sum)
            mixed = jnp.einsum(
                "hck,khd->chd",
                attend.astype(jnp.bfloat16),
                values_all,
                preferred_element_type=jnp.float32,
            )
            mixed_low = mixed.reshape(CAP, head_cols).astype(jnp.bfloat16)
            project = jnp.dot(mixed_low, out_full[expert_id], preferred_element_type=jnp.float32)
            attn_part = attn_part.at[row_ids].add(project * slot_gate[:, None])
            kept.append(
                (
                    row_ids,
                    slot_gate,
                    chosen,
                    slot_places,
                    query_pre,
                    query_rot,
                    log_total,
                    mixed_low,
                )
            )
        attn_total = lax.psum(attn_part, "expert")
        hidden1 = field + attn_total
        normed2 = rms_scale(hidden1, gains[1]).astype(jnp.bfloat16)
        gate_full, up_full, down_full = (
            lax.all_gather(w_gate[0], "dp", axis=0, tiled=True),
            lax.all_gather(w_up[0], "dp", axis=0, tiled=True),
            lax.all_gather(w_down[0], "dp", axis=0, tiled=True),
        )
        feed_rows, feed_gate = slot_plan(
            mlp_routes[micro_id], mlp_share[micro_id], expert_index, CAP
        )
        feed_in = jnp.take(normed2, feed_rows, axis=0)
        gate_pre = jnp.dot(feed_in, gate_full, preferred_element_type=jnp.float32)
        up_pre = jnp.dot(feed_in, up_full, preferred_element_type=jnp.float32)
        inner = (jax.nn.silu(gate_pre) * up_pre).astype(jnp.bfloat16)
        feed_out = jnp.dot(inner, down_full, preferred_element_type=jnp.float32)
        feed_part = (
            jnp.zeros((row_count, full_width), jnp.float32)
            .at[feed_rows]
            .add(feed_out * feed_gate[:, None])
        )
        feed_shard = lax.psum_scatter(feed_part, "expert", scatter_dimension=1, tiled=True)
        hidden1_shard = lax.dynamic_slice_in_dim(hidden1, col_start, local_width, 1)
        result = hidden1_shard + feed_shard
        results.append(result.astype(jnp.bfloat16))
        differ = result - teacher[micro_id].astype(jnp.float32)
        counted = valid[micro_id].astype(jnp.float32)[:, None]
        squared = squared + jnp.sum(counted * differ * differ)
        grad_result = counted * differ * (2.0 * (loss_scale / (count * full_width)))
        grad_rows = lax.all_gather(grad_result, "expert", axis=1, tiled=True)
        gate_back, up_back, down_back = (
            lax.all_gather(w_gate[0], "dp", axis=0, tiled=True),
            lax.all_gather(w_up[0], "dp", axis=0, tiled=True),
            lax.all_gather(w_down[0], "dp", axis=0, tiled=True),
        )
        grad_feed = (jnp.take(grad_rows, feed_rows, axis=0) * feed_gate[:, None]).astype(
            jnp.bfloat16
        )
        grad_inner = times_trans(grad_feed, down_back)
        _, silu_back = jax.vjp(lambda left, right: jax.nn.silu(left) * right, gate_pre, up_pre)
        grad_gate_pre, grad_up_pre = silu_back(grad_inner)
        grad_gate_low = grad_gate_pre.astype(jnp.bfloat16)
        grad_up_low = grad_up_pre.astype(jnp.bfloat16)
        grad_feed_in = times_trans(grad_gate_low, gate_back) + times_trans(grad_up_low, up_back)
        held_gate = held_gate + times_rows(feed_in, grad_gate_low)
        held_up = held_up + times_rows(feed_in, grad_up_low)
        held_down = held_down + times_rows(inner, grad_feed)
        grad_norm2_part = (
            jnp.zeros((row_count, full_width), jnp.float32).at[feed_rows].add(grad_feed_in)
        )
        grad_norm2 = lax.psum(grad_norm2_part, "expert")
        _, norm2_back = jax.vjp(rms_scale, hidden1, gains[1])
        grad_hidden_norm, grad_gain2 = norm2_back(grad_norm2)
        grad_hidden1 = grad_rows + grad_hidden_norm
        grad_norm1_part = jnp.zeros((row_count, full_width), jnp.float32)
        grad_pair = jnp.zeros((key_count, 2, local_heads, HEAD), jnp.float32)
        term_query = []
        term_out = []
        for expert_id in range(expert_count):
            row_ids, slot_gate, chosen, slot_places, query_pre, query_rot, log_total, mixed_low = (
                kept[expert_id]
            )
            grad_project = (jnp.take(grad_hidden1, row_ids, axis=0) * slot_gate[:, None]).astype(
                jnp.bfloat16
            )
            grad_mixed = times_trans(grad_project, out_full[expert_id]).astype(jnp.bfloat16)
            term_out.append(times_rows(mixed_low, grad_project))
            grad_mixed = grad_mixed.reshape(CAP, local_heads, HEAD)
            scores = score_block(query_rot, slot_places)
            attend = jnp.exp(scores - log_total)
            attend_low = attend.astype(jnp.bfloat16)
            grad_attend = jnp.einsum(
                "chd,khd->hck", grad_mixed, values_all, preferred_element_type=jnp.float32
            )
            inner_sum = jnp.sum(attend * grad_attend, axis=-1, keepdims=True)
            grad_scores = (attend * (grad_attend - inner_sum)).astype(jnp.bfloat16)
            grad_query_rot = (
                jnp.einsum(
                    "hck,khd->chd", grad_scores, keys_all, preferred_element_type=jnp.float32
                )
                * scale_root
            )
            grad_keys = (
                jnp.einsum(
                    "hck,chd->khd", grad_scores, query_rot, preferred_element_type=jnp.float32
                )
                * scale_root
            )
            grad_values = jnp.einsum(
                "hck,chd->khd", attend_low, grad_mixed, preferred_element_type=jnp.float32
            )
            grad_pair = grad_pair + jnp.stack([grad_keys, grad_values], axis=1)
            _, query_back = jax.vjp(lambda value: rotate(value, slot_places), query_pre)
            grad_query_pre = (
                query_back(grad_query_rot)[0].astype(jnp.bfloat16).reshape(CAP, head_cols)
            )
            grad_norm1_part = grad_norm1_part.at[row_ids].add(
                times_trans(grad_query_pre, query_full[expert_id])
            )
            term_query.append(times_rows(chosen, grad_query_pre))
        grad_pair_flat = grad_pair.reshape(key_count, 2, head_cols)
        prompt_grad = lax.psum_scatter(
            grad_pair_flat[:prompt_total], "dp", scatter_dimension=0, tiled=True
        )
        pair_grad = jnp.concatenate([prompt_grad, grad_pair_flat[prompt_total:]], axis=0)
        _, key_back = jax.vjp(lambda value: rotate(value, places), keyval_pre[:, 0])
        grad_key_pre = key_back(pair_grad[:, 0].reshape(row_count, local_heads, HEAD))[0].reshape(
            row_count, head_cols
        )
        grad_pair_low = (
            jnp.stack([grad_key_pre, pair_grad[:, 1]], axis=1)
            .astype(jnp.bfloat16)
            .reshape(row_count, 2 * head_cols)
        )
        grad_norm1_part = grad_norm1_part + times_trans(grad_pair_low, keyval_flat)
        term_keyval = times_rows(normed1, grad_pair_low).reshape(full_width, 2, head_cols)
        grad_norm1 = lax.psum(grad_norm1_part.astype(jnp.bfloat16), "expert").astype(jnp.float32)
        _, norm1_back = jax.vjp(rms_scale, field, gains[0])
        grad_field_norm, grad_gain1 = norm1_back(grad_norm1)
        grad_field = grad_hidden1 + grad_field_norm
        input_grads.append(lax.dynamic_slice_in_dim(grad_field, col_start, local_width, 1))
        gain_sum = gain_sum + jnp.stack(
            [jnp.where(own_columns, grad_gain1, 0.0), jnp.where(own_columns, grad_gain2, 0.0)]
        )
        held_query = held_query + jnp.stack(term_query)
        held_out = held_out + jnp.stack(term_out)
        held_keyval = held_keyval + term_keyval
    grad_query, grad_out, grad_keyval, grad_gate, grad_up, grad_down = (
        lax.psum_scatter(
            held_query.astype(jnp.bfloat16), "dp", scatter_dimension=1, tiled=True
        ).astype(jnp.float32),
        lax.psum_scatter(
            held_out.astype(jnp.bfloat16), "dp", scatter_dimension=2, tiled=True
        ).astype(jnp.float32),
        lax.psum_scatter(
            held_keyval.astype(jnp.bfloat16), "dp", scatter_dimension=0, tiled=True
        ).astype(jnp.float32),
        lax.psum_scatter(
            held_gate.astype(jnp.bfloat16), "dp", scatter_dimension=0, tiled=True
        ).astype(jnp.float32),
        lax.psum_scatter(
            held_up.astype(jnp.bfloat16), "dp", scatter_dimension=0, tiled=True
        ).astype(jnp.float32),
        lax.psum_scatter(
            held_down.astype(jnp.bfloat16), "dp", scatter_dimension=0, tiled=True
        ).astype(jnp.float32),
    )
    gain_total, squared_total = lax.psum((gain_sum, squared), ("dp", "expert"))
    loss = squared_total / (count * full_width)
    return (
        jnp.stack(results),
        loss,
        jnp.stack(input_grads),
        gain_total,
        grad_query,
        grad_out,
        grad_keyval,
        grad_gate[None],
        grad_up[None],
        grad_down[None],
    )


def swap_pairs(size):
    return [(i, i ^ 1) for i in range(size)]


DEAL_FIRST = [(1, 2), (2, 1)]
DEAL_SECOND = [(0, 2), (1, 0), (2, 3), (3, 1)]
BACK_SECOND = [(b, a) for a, b in DEAL_SECOND]
QUAD = ("y", "c")
TEAM = ("c", "dp")


def rope_tables(places):
    half = HEAD // 2
    ladder = jnp.arange(half).astype(jnp.float32) * (2.0 / HEAD)
    freqs = jnp.power(jnp.asarray(THETA, jnp.float32), -ladder)
    angle = places.astype(jnp.float32)[:, None] * freqs[None, :]
    return jnp.cos(angle), jnp.sin(angle)


def turn(value, cosine, sine):
    half = value.shape[-1] // 2
    first = value[..., :half]
    second = value[..., half:]
    return jnp.concatenate(
        [first * cosine - second * sine, second * cosine + first * sine], axis=-1
    )


def root_of(field):
    return lax.rsqrt(jnp.mean(field * field, axis=-1, keepdims=True) + EPS)


def norm_back(field, gain, grad):
    root = root_of(field)
    scaled = grad * gain
    along = jnp.sum(scaled * field, axis=-1, keepdims=True) / field.shape[-1]
    return root * scaled - field * (root * root * root) * along, jnp.sum(grad * field * root, axis=0)


def gate_rows(route, share, expert_count):
    shares = share.astype(jnp.float32)
    weight = shares / jnp.sum(shares, axis=-1, keepdims=True)
    labels = jnp.arange(expert_count, dtype=jnp.int32)
    match = route[None, :, :] == labels[:, None, None]
    return jnp.sum(jnp.where(match, weight[None], 0.0), axis=-1)


def dot(left, right):
    return jnp.dot(left, right, preferred_element_type=jnp.float32)


BLOCK = 128
MASKED = -1e30
NT_DIMS = (((1,), (1,)), ((), ()))
ROOM = 56 * 1024 * 1024


def nt(left, right):
    return lax.dot_general(left, right, NT_DIMS, preferred_element_type=jnp.float32)


def spin(value, cosine, sine):
    return value * cosine + pltpu.roll(value, HEAD // 2, 1) * sine


def stack_experts(block, count):
    return jnp.concatenate([block[:, e * HEAD : (e + 1) * HEAD] for e in range(count)], axis=0)


def near_mask(columns):
    key_at = lax.broadcasted_iota(jnp.int32, (BLOCK, columns), 0)
    row_at = lax.broadcasted_iota(jnp.int32, (BLOCK, columns), 1) % BLOCK
    return key_at <= row_at


def attend_kernel(
    prompts, experts, front, cosine, sine, gate, mixed, query_out, pair_out, log_out, key_far, value_far
):
    step = pl.program_id(0)
    wide = experts * HEAD
    scale = HEAD ** (-0.5)

    @pl.when(step == 0)
    def _():
        key_far[...] = jnp.zeros_like(key_far)
        value_far[...] = jnp.zeros_like(value_far)

    cos, sin = cosine[...], sine[...]
    key = spin(front[:, wide : wide + HEAD], cos, sin).astype(jnp.bfloat16)
    value_up = front[:, wide + HEAD : wide + 2 * HEAD].T.astype(jnp.bfloat16)
    pair_out[:, :HEAD] = key
    pair_out[:, HEAD:] = front[:, wide + HEAD : wide + 2 * HEAD].astype(jnp.bfloat16)
    for e in range(experts):
        query_out[:, e * HEAD : (e + 1) * HEAD] = spin(
            front[:, e * HEAD : (e + 1) * HEAD], cos, sin
        ).astype(jnp.bfloat16)
    query = stack_experts(query_out[...], experts)
    near = jnp.where(near_mask(wide), nt(key, query) * scale, MASKED)
    far_tiles = jnp.minimum(step, prompts)

    def finish(width):
        far = nt(key_far[:width, :], query) * scale
        key_at = lax.broadcasted_iota(jnp.int32, far.shape, 0)
        far = jnp.where(key_at < far_tiles * BLOCK, far, MASKED)
        peak = jnp.maximum(
            jnp.max(far, axis=0, keepdims=True), jnp.max(near, axis=0, keepdims=True)
        )
        far = jnp.exp(far - peak)
        close = jnp.exp(near - peak)
        total = jnp.sum(far, axis=0, keepdims=True) + jnp.sum(close, axis=0, keepdims=True)
        mix = jnp.dot(
            value_far[:, :width], far.astype(jnp.bfloat16), preferred_element_type=jnp.float32
        ) + jnp.dot(value_up, close.astype(jnp.bfloat16), preferred_element_type=jnp.float32)
        mix = mix * (gate[0] / total)
        log_out[0] = peak + jnp.log(total)
        for e in range(experts):
            mixed[:, e * HEAD : (e + 1) * HEAD] = mix[:, e * BLOCK : (e + 1) * BLOCK].T.astype(
                jnp.bfloat16
            )

    split = prompts // 2

    @pl.when(step <= split)
    def _():
        finish(split * BLOCK)

    @pl.when(step > split)
    def _():
        finish(prompts * BLOCK)

    @pl.when(step < prompts)
    def _():
        at = pl.multiple_of(step * BLOCK, BLOCK)
        key_far[pl.ds(at, BLOCK), :] = key
        value_far[:, pl.ds(at, BLOCK)] = value_up


def attend(front, cosine, sine, gate, prompts, experts):
    rows, lanes = front.shape
    blocks = rows // BLOCK
    wide = experts * HEAD
    at = lambda i: (i, 0)
    line = pl.BlockSpec((1, 1, experts * BLOCK), lambda i: (i, 0, 0))
    return pl.pallas_call(
        functools.partial(attend_kernel, prompts, experts),
        grid=(blocks,),
        in_specs=[
            pl.BlockSpec((BLOCK, lanes), at),
            pl.BlockSpec((BLOCK, HEAD), at),
            pl.BlockSpec((BLOCK, HEAD), at),
            line,
        ],
        out_specs=[
            pl.BlockSpec((BLOCK, wide), at),
            pl.BlockSpec((BLOCK, wide), at),
            pl.BlockSpec((BLOCK, 2 * HEAD), at),
            line,
        ],
        out_shape=[
            jax.ShapeDtypeStruct((rows, wide), jnp.bfloat16),
            jax.ShapeDtypeStruct((rows, wide), jnp.bfloat16),
            jax.ShapeDtypeStruct((rows, 2 * HEAD), jnp.bfloat16),
            jax.ShapeDtypeStruct((blocks, 1, experts * BLOCK), jnp.float32),
        ],
        scratch_shapes=[
            pltpu.VMEM((prompts * BLOCK, HEAD), jnp.bfloat16),
            pltpu.VMEM((HEAD, prompts * BLOCK), jnp.bfloat16),
        ],
        compiler_params=pltpu.CompilerParams(
            dimension_semantics=("arbitrary",), vmem_limit_bytes=ROOM
        ),
        cost_estimate=pl.CostEstimate(
            flops=4 * rows * experts * HEAD * prompts * BLOCK,
            transcendentals=rows * experts * prompts * BLOCK,
            bytes_accessed=rows * lanes * 8,
        ),
        name="attend",
    )(front, cosine, sine, gate)


def attend_back_kernel(
    prompts, experts, pull, gate, query_in, pair, pair_up, log_in, cosine, sine, back, grad_key, grad_value
):
    step = pl.program_id(0)
    wide = experts * HEAD
    scale = HEAD ** (-0.5)

    @pl.when(step == 0)
    def _():
        grad_key[...] = jnp.zeros_like(grad_key)
        grad_value[...] = jnp.zeros_like(grad_value)

    at = pl.multiple_of(step * BLOCK, BLOCK)
    here = pl.ds(at, BLOCK)
    query = stack_experts(query_in[...], experts)
    grads = jnp.concatenate(
        [
            (pull[:, e * HEAD : (e + 1) * HEAD] * gate[:, e : e + 1]).astype(jnp.bfloat16)
            for e in range(experts)
        ],
        axis=0,
    )
    level = log_in[0]
    near = jnp.where(
        near_mask(wide), jnp.exp(nt(pair[here, :HEAD], query) * scale - level), 0.0
    )
    near_pull = nt(pair[here, HEAD:], grads)
    far_tiles = jnp.minimum(step, prompts)

    def finish(width):
        far = jnp.exp(nt(pair[:width, :HEAD], query) * scale - level)
        key_at = lax.broadcasted_iota(jnp.int32, far.shape, 0)
        far = jnp.where(key_at < far_tiles * BLOCK, far, 0.0)
        far_pull = nt(pair[:width, HEAD:], grads)
        along = jnp.sum(far * far_pull, axis=0, keepdims=True) + jnp.sum(
            near * near_pull, axis=0, keepdims=True
        )
        far_ds = (far * (far_pull - along)).astype(jnp.bfloat16)
        near_ds = (near * (near_pull - along)).astype(jnp.bfloat16)
        turned = (
            jnp.dot(pair_up[:, :width], far_ds, preferred_element_type=jnp.float32)
            + jnp.dot(pair_up[:, here], near_ds, preferred_element_type=jnp.float32)
        ) * scale
        cos, sin = cosine[here, :], sine[here, :]
        for e in range(experts):
            back[here, e * HEAD : (e + 1) * HEAD] = spin(
                turned[:, e * BLOCK : (e + 1) * BLOCK].T, cos, -sin
            ).astype(jnp.bfloat16)
        grad_key[:width, :] += jnp.dot(far_ds, query, preferred_element_type=jnp.float32)
        grad_value[:width, :] += jnp.dot(
            far.astype(jnp.bfloat16), grads, preferred_element_type=jnp.float32
        )
        grad_key[here, :] += jnp.dot(near_ds, query, preferred_element_type=jnp.float32)
        grad_value[here, :] += jnp.dot(
            near.astype(jnp.bfloat16), grads, preferred_element_type=jnp.float32
        )

    split = prompts // 2

    @pl.when(step <= split)
    def _():
        finish(split * BLOCK)

    @pl.when(step > split)
    def _():
        finish(prompts * BLOCK)

    @pl.when(step == pl.num_programs(0) - 1)
    def _():
        back[:, wide : wide + HEAD] = spin(
            grad_key[...] * scale, cosine[...], -sine[...]
        ).astype(jnp.bfloat16)
        back[:, wide + HEAD :] = grad_value[...].astype(jnp.bfloat16)


def attend_back(pull, gate, query, pair, pair_up, log_total, cosine, sine, prompts, experts):
    rows, wide = query.shape
    blocks = rows // BLOCK
    at = lambda i: (i, 0)
    still = lambda i: (0, 0)
    line = pl.BlockSpec((1, 1, experts * BLOCK), lambda i: (i, 0, 0))
    return pl.pallas_call(
        functools.partial(attend_back_kernel, prompts, experts),
        grid=(blocks,),
        in_specs=[
            pl.BlockSpec((BLOCK, wide), at),
            pl.BlockSpec((BLOCK, experts), at),
            pl.BlockSpec((BLOCK, wide), at),
            pl.BlockSpec((rows, 2 * HEAD), still),
            pl.BlockSpec((HEAD, rows), still),
            line,
            pl.BlockSpec((rows, HEAD), still),
            pl.BlockSpec((rows, HEAD), still),
        ],
        out_specs=pl.BlockSpec((rows, wide + 2 * HEAD), still),
        out_shape=jax.ShapeDtypeStruct((rows, wide + 2 * HEAD), jnp.bfloat16),
        scratch_shapes=[
            pltpu.VMEM((rows, HEAD), jnp.float32),
            pltpu.VMEM((rows, HEAD), jnp.float32),
        ],
        compiler_params=pltpu.CompilerParams(
            dimension_semantics=("arbitrary",), vmem_limit_bytes=ROOM
        ),
        cost_estimate=pl.CostEstimate(
            flops=10 * rows * experts * HEAD * prompts * BLOCK,
            transcendentals=rows * experts * prompts * BLOCK,
            bytes_accessed=rows * wide * 12,
        ),
        name="attend_back",
    )(pull, gate, query, pair, pair_up, log_total, cosine, sine)


LINE = 4
SIDES = [(i, i ^ 1) for i in range(2 * LINE)]


def hops(moves):
    return [(2 * a + x, 2 * b + x) for a, b in moves for x in (0, 1)]


def hold(*values):
    return lax.optimization_barrier(values)


def to_side(value):
    return lax.ppermute(value, "dp", SIDES)


def to_core(value):
    return lax.ppermute(value, "c", swap_pairs(2))


def scatter_run(make, given, fill=None):
    spot = lax.axis_index("dp") // 2
    low = jnp.bfloat16
    wide = lambda value: value.astype(jnp.float32)

    def rise(value, last):
        return lax.ppermute(value, "dp", hops([(a, a + 1) for a in range(last)]))

    def fall(value, last):
        return lax.ppermute(value, "dp", hops([(LINE - 1 - a, LINE - 2 - a) for a in range(last)]))

    def cut(value):
        middle = value.shape[0] // 2
        return value[:middle], value[middle:]

    here3, there3 = make(3, *given)
    there3, *given = hold(there3, *given)
    got3, (here2, there2) = hold(to_core(there3), make(2, *given))
    mine3, other3 = cut(here3 + got3)
    other3, there2, *given = hold(other3, there2, *given)
    side3, both2, (here1, there1) = hold(
        to_side(other3), here2 + to_core(there2), make(1, *given)
    )
    mine2, other2 = cut(both2)
    other2, there1, *given = hold(other2, there1, *given)
    row3 = wide(mine3) + wide(side3)
    send3 = row3.astype(low)
    side2, up, down, both1, (here0, there0) = hold(
        to_side(other2), rise(send3, 1), fall(send3, 1), here1 + to_core(there1), make(0, *given)
    )
    mine1, other1 = cut(both1)
    other1, there0, *given = hold(other1, there0, *given)
    row2 = wide(mine2) + wide(side2)
    send_up = (jnp.where(spot == 0, row2, row3) + wide(up)).astype(low)
    send_down = (jnp.where(spot == LINE - 1, row2, row3) + wide(down)).astype(low)
    side1, up, down, both0 = hold(
        to_side(other1), rise(send_up, 2), fall(send_down, 2), here0 + to_core(there0)
    )
    mine0, other0 = cut(both0)
    other0, *given = hold(other0, *given)
    row1 = wide(mine1) + wide(side1)
    send_up = (jnp.where(spot == 1, row2, row1) + wide(up)).astype(low)
    send_down = (jnp.where(spot == LINE - 2, row2, row1) + wide(down)).astype(low)
    filled = fill(*given) if fill else ()
    side0, up, down, filled = hold(to_side(other0), rise(send_up, 3), fall(send_down, 3), filled)
    total = wide(mine0) + wide(side0) + wide(up) + wide(down)
    return (total, filled) if fill else total


LANE_STEP = 512


def product_kernel(terms, places, *refs):
    lefts, rights, out = refs[: 4 * terms], refs[4 * terms : 5 * terms], refs[-2]
    far_out = refs[-1]
    total = None
    for term in range(terms):
        rows = jnp.concatenate([lefts[4 * term + j][...] for j in range(4)], axis=0)
        part = jnp.dot(rows, rights[term][...], preferred_element_type=jnp.float32)
        total = part if total is None else total + part
    middle = out.shape[0]
    out[...] = total[:middle].astype(out.dtype)
    far_out[...] = total[middle:].astype(out.dtype)


def slot_product(places, lefts, rights):
    width = rights[0].shape[1]
    block = lambda j: (lambda i, places: (places[j], 0))
    return pl.pallas_call(
        functools.partial(product_kernel, len(lefts)),
        grid_spec=pltpu.PrefetchScalarGridSpec(
            num_scalar_prefetch=1,
            grid=(width // LANE_STEP,),
            in_specs=[
                pl.BlockSpec((BLOCK, left.shape[1]), block(j)) for left in lefts for j in range(4)
            ]
            + [
                pl.BlockSpec((right.shape[0], LANE_STEP), lambda i, places: (0, i))
                for right in rights
            ],
            out_specs=[pl.BlockSpec((2 * BLOCK, LANE_STEP), lambda i, places: (0, i))] * 2,
        ),
        out_shape=[jax.ShapeDtypeStruct((2 * BLOCK, width), jnp.bfloat16)] * 2,
        compiler_params=pltpu.CompilerParams(
            dimension_semantics=("arbitrary",), vmem_limit_bytes=ROOM
        ),
        cost_estimate=pl.CostEstimate(
            flops=sum(8 * BLOCK * right.shape[0] * width for right in rights),
            transcendentals=0,
            bytes_accessed=sum(2 * right.size + 8 * BLOCK * right.shape[0] for right in rights),
        ),
        name="slot_product",
    )(places, *[left for left in lefts for _ in range(4)], *rights)


ROW_STEP = 256


def share_lanes(share, columns):
    lane = lax.broadcasted_iota(jnp.int32, (share.shape[0], columns), 1)
    return jnp.where(lane < columns // 2, share[:, 0:1], share[:, 1:2])


def open_kernel(rows, gate_w, up_w, share, gate_out, up_out, inner_out):
    gate = nt(rows[...], gate_w[...])
    up = nt(rows[...], up_w[...])
    gate_out[...] = gate.astype(gate_out.dtype)
    up_out[...] = up.astype(up_out.dtype)
    inner_out[...] = (
        gate / (1.0 + jnp.exp(-gate)) * up * share_lanes(share[...], gate.shape[1])
    ).astype(jnp.bfloat16)


def close_kernel(rows, down_w, share, gate_in, up_in, gate_out, up_out):
    gate = gate_in[...].astype(jnp.float32)
    up = up_in[...].astype(jnp.float32)
    pull = nt(rows[...], down_w[...]) * share_lanes(share[...], gate.shape[1])
    sigma = 1.0 / (1.0 + jnp.exp(-gate))
    gate_out[...] = (pull * up * sigma * (1.0 + gate * (1.0 - sigma))).astype(jnp.bfloat16)
    up_out[...] = (pull * gate * sigma).astype(jnp.bfloat16)


def row_call(kernel, rows, weights, others, kinds, name):
    count, width = rows.shape
    columns = weights[0].shape[0]
    tile = lambda lanes: pl.BlockSpec((ROW_STEP, lanes), lambda i: (i, 0))
    return pl.pallas_call(
        kernel,
        grid=(count // ROW_STEP,),
        in_specs=[tile(width)]
        + [
            pl.BlockSpec(weight.shape, lambda i: (0, 0), pipeline_mode=pl.Buffered(1))
            for weight in weights
        ]
        + [tile(other.shape[1]) for other in others],
        out_specs=[tile(columns) for _ in kinds],
        out_shape=[jax.ShapeDtypeStruct((count, columns), kind) for kind in kinds],
        compiler_params=pltpu.CompilerParams(
            dimension_semantics=("arbitrary",), vmem_limit_bytes=ROOM
        ),
        cost_estimate=pl.CostEstimate(
            flops=2 * len(weights) * count * width * columns,
            transcendentals=count * columns,
            bytes_accessed=2 * len(weights) * width * columns + 10 * count * columns,
        ),
        name=name,
    )(rows, *weights, *others)


def team_device(
    tokens_in,
    teacher,
    valid,
    attn_routes,
    attn_share,
    mlp_routes,
    mlp_share,
    gains,
    w_query,
    w_out,
    w_keyval,
    w_gate,
    w_up,
    w_down,
):
    low = jnp.bfloat16
    units = lax.axis_size("dp")
    plane = lax.axis_index("y")
    core = lax.axis_index("c")
    micro_count, row_count, local_width = tokens_in.shape
    half = row_count // 2
    width = local_width * 4
    team_rows = 2 * units * half
    prompt_total = units * half
    expert_count = w_query.shape[0]
    local_heads = w_query.shape[2] // HEAD
    depth = w_query.shape[1]
    hidden = w_down.shape[1]
    loss_scale = width * micro_count * row_count * units / 2.0
    scale_root = HEAD ** (-0.5)

    def exchange(parts):
        spot = 2 * plane + core
        got = [lax.dynamic_index_in_dim(parts, spot, 0, keepdims=False)]
        for step in (1, 2, 3):
            part = lax.dynamic_index_in_dim(parts, spot ^ step, 0, keepdims=False)
            got.append(lax.ppermute(part, QUAD, [(p, p ^ step) for p in range(4)]))
        for step, flag in ((1, core), (2, plane)):
            got = [jnp.where(flag == 0, got[p], got[p ^ step]) for p in range(4)]
        return got

    def to_rows(value):
        return jnp.concatenate(exchange(value.reshape(4, half, local_width)), axis=1)

    def from_rows(value):
        got = exchange(value.reshape(half, 4, local_width).transpose(1, 0, 2))
        return jnp.stack(got).reshape(micro_count, row_count, local_width)

    def collect(value):
        return lax.all_gather(value, TEAM, axis=0, tiled=True)

    def deliver(value):
        return lax.psum_scatter(value.astype(low), TEAM, scatter_dimension=0, tiled=True).astype(
            jnp.float32
        )

    def mine(value):
        return lax.dynamic_index_in_dim(value, plane, 0, keepdims=False)

    field = to_rows(tokens_in).astype(jnp.float32)
    goal = to_rows(teacher).astype(jnp.float32)
    gate_here = jnp.concatenate(
        [
            gate_rows(mine(attn_routes), mine(attn_share), expert_count),
            gate_rows(mine(mlp_routes), mine(mlp_share), expert_count),
        ],
        axis=0,
    )
    tokens_here = jnp.full((1, row_count), jnp.sum(valid).astype(jnp.float32))
    gate_here = jnp.concatenate([gate_here, tokens_here], axis=0)
    slots = jnp.arange(units, dtype=jnp.int32)[:, None, None]
    gate_all = jnp.where(slots == lax.axis_index("dp"), gate_here[None], 0.0)
    for shift in range(1, units):
        got = lax.ppermute(gate_here, "dp", [(i, (i + shift) % units) for i in range(units)])
        gate_all = jnp.where(slots == (lax.axis_index("dp") - shift) % units, got[None], gate_all)
    count = jnp.sum(gate_all[:, -1, 0])
    normed1 = (field * root_of(field) * gains[0]).astype(low)
    normed1 = collect(normed1)

    query_part = w_query.reshape(expert_count, depth, local_heads, HEAD).transpose(1, 2, 0, 3)
    out_part = w_out.reshape(expert_count, local_heads, HEAD, depth).transpose(3, 1, 0, 2)
    pair_part = w_keyval.reshape(depth, 2, local_heads, HEAD).transpose(0, 2, 1, 3)
    wide = expert_count * HEAD
    def across(value):
        return lax.ppermute(value, "y", swap_pairs(2))

    def scatter_heads(value):
        lanes = value.shape[2]
        packed = value.reshape(2, depth // 2, local_heads, lanes).transpose(0, 2, 1, 3)
        kept_half = lax.dynamic_index_in_dim(packed, core, 0, keepdims=False)
        sent_half = lax.dynamic_index_in_dim(packed, 1 - core, 0, keepdims=False)
        got_half = lax.ppermute(sent_half, "c", swap_pairs(2))
        return jnp.concatenate(
            [
                jnp.where(core == 0, kept_half, got_half),
                jnp.where(core == 0, got_half, kept_half),
            ],
            axis=0,
        )

    def deal_heads(heads):
        first = jnp.where(plane == core, heads, lax.ppermute(heads, QUAD, DEAL_FIRST))
        second = lax.ppermute(heads, QUAD, DEAL_SECOND)
        return jnp.stack(
            [jnp.where(plane == 0, first, second), jnp.where(plane == 0, second, first)], axis=1
        ).reshape(width, heads.shape[2])

    def swap_all(value, *later):
        got = lax.all_to_all(value, "dp", 0, 0, tiled=True)
        return lax.optimization_barrier((got, *later))

    def slabs_of(value):
        return value.T.reshape(units, hidden, depth)

    down_own = w_down[0]
    down_far = across(down_own)
    front_heads = scatter_heads(
        jnp.concatenate(
            [
                query_part.reshape(depth, local_heads, wide),
                pair_part.reshape(depth, local_heads, 2 * HEAD),
            ],
            axis=2,
        )
    )
    out_heads = scatter_heads(out_part.reshape(depth, local_heads, wide))
    gate_slabs, up_slabs = slabs_of(w_gate[0]), slabs_of(w_up[0])
    front_heads, gate_all, count = hold(front_heads, gate_all, count)
    front_heads, out_heads, down_far, gate_slabs, up_slabs = swap_all(
        front_heads, out_heads, down_far, gate_slabs, up_slabs
    )
    out_heads, gate_slabs = swap_all(out_heads, gate_slabs)
    front_weights = deal_heads(front_heads)
    gate_all = (
        gate_all[:, :-1].reshape(units, 2 * expert_count, 2, half)
        .transpose(1, 2, 0, 3)
        .reshape(2 * expert_count, team_rows)
    )
    feed_gate_own = lax.dynamic_index_in_dim(gate_all, expert_count + 2 * plane + core, 0, False)
    feed_gate_far = lax.dynamic_index_in_dim(gate_all, expert_count + 2 * (1 - plane) + core, 0, False)
    counted = lax.dynamic_slice_in_dim(mine(valid), core * half, half, 0).astype(jnp.float32)[:, None]

    normed1, gate_all, feed_gate_own, feed_gate_far, count, gate_slabs = lax.optimization_barrier(
        (normed1, gate_all, feed_gate_own, feed_gate_far, count, gate_slabs)
    )
    gate_slabs, up_slabs = swap_all(gate_slabs, up_slabs)
    gate_own = gate_slabs.transpose(1, 0, 2).reshape(hidden, width)
    gate_far = across(gate_own)
    attn_gate = gate_all[:expert_count].T
    blocks = team_rows // BLOCK
    gate_lines = (
        gate_all[:expert_count].reshape(expert_count, blocks, BLOCK).transpose(1, 0, 2)
    ).reshape(blocks, 1, expert_count * BLOCK)
    index = jnp.arange(team_rows, dtype=jnp.int32)
    places = jnp.where(index < prompt_total, index, prompt_total + index % half)
    cosine, sine = rope_tables(places)
    cosine = jnp.concatenate([cosine, cosine], axis=1)
    sine = jnp.concatenate([-sine, sine], axis=1)

    unit = lax.axis_index("dp")
    order = jnp.asarray([[0, 1, 2, 3], [1, 0, 2, 3], [2, 3, 1, 0], [3, 2, 1, 0]], jnp.int32)
    block = jnp.arange(blocks, dtype=jnp.int32)
    owners = (
        ((block // 2 % 2) ^ core) * units
        + lax.dynamic_index_in_dim(order, unit // 2, 0, False)[block // 4] * 2
        + ((block % 2) ^ (unit % 2))
    )

    front = dot(normed1, front_weights)
    front, out_heads = lax.optimization_barrier((front, out_heads))
    out_weights = deal_heads(out_heads)
    mixed_low, query_rot, pair_rot, log_total = attend(
        front, cosine, sine, gate_lines, units, expert_count
    )
    mixed_low, gate_own, up_slabs = lax.optimization_barrier((mixed_low, gate_own, up_slabs))
    up_slabs = lax.all_to_all(up_slabs, "dp", 0, 0, tiled=True)
    up_own = up_slabs.transpose(1, 0, 2).reshape(hidden, width)
    up_far = across(up_own)
    attn_sum = deliver(times_trans(mixed_low, out_weights))
    attn_sum, up_own, gate_far = lax.optimization_barrier((attn_sum, up_own, gate_far))
    hidden1 = field + attn_sum
    normed2 = collect((hidden1 * root_of(hidden1) * gains[1]).astype(low))

    gate_w = jnp.concatenate([gate_own, gate_far], axis=0)
    up_w = jnp.concatenate([up_own, up_far], axis=0)
    down_w = jnp.concatenate([down_own, down_far], axis=0)
    feed_share = jnp.stack([feed_gate_own, feed_gate_far], axis=1)
    gate_pre, up_pre, inner = row_call(
        open_kernel,
        normed2,
        [gate_w, up_w],
        [feed_share],
        [low, low, low],
        "open_rows",
    )
    result = hidden1 + scatter_run(
        lambda k, left: slot_product(owners[4 * k : 4 * k + 4], [left], [down_w]), (inner,)
    )
    layer_low = result.astype(low)
    differ = result - goal
    squared = jnp.sum(counted * differ * differ)
    grad_result = counted * differ * (2.0 * (loss_scale / (count * width)))
    grad_rows = collect(grad_result.astype(low))
    grad_rows, layer_low = hold(grad_rows, layer_low)
    layer_out = from_rows(layer_low)

    grad_gate, grad_up = row_call(
        close_kernel, grad_rows, [down_w], [feed_share, gate_pre, up_pre], [low, low], "close_rows"
    )

    def weight_sum(left, right):
        whole = times_rows(left, right)
        return whole[:hidden], whole[hidden:].astype(low)

    grad_norm2, (gate_near, gate_sent) = scatter_run(
        lambda k, one, two: slot_product(owners[4 * k : 4 * k + 4], [one, two], [gate_w, up_w]),
        (grad_gate, grad_up),
        lambda one, two: weight_sum(one, normed2),
    )
    gate_got = across(gate_sent)
    grad_norm2, grad_up, inner = hold(grad_norm2, grad_up, inner)
    up_near, up_sent = weight_sum(grad_up, normed2)
    down_near, down_sent = weight_sum(inner, grad_rows)
    gate_got, up_near, up_sent, down_near, down_sent = hold(
        gate_got, up_near, up_sent, down_near, down_sent
    )
    up_got = across(up_sent)
    grad_hidden_norm, grad_gain2 = norm_back(hidden1, gains[1], grad_norm2)
    grad_hidden1 = grad_result + grad_hidden_norm
    grad_hidden_rows = collect(grad_hidden1.astype(low))

    def rows_for_owners(value):
        return value.astype(low).reshape(hidden, units, depth).transpose(1, 0, 2)

    def own_rows(value):
        return value.reshape(units * hidden, depth).T.astype(jnp.float32)

    gate_slabs = rows_for_owners(gate_near + gate_got.astype(jnp.float32))
    gate_slabs = lax.all_to_all(gate_slabs, "dp", 0, 0, tiled=True)
    front_back = attend_back(
        dot(grad_hidden_rows, out_weights),
        attn_gate,
        query_rot,
        pair_rot,
        pair_rot[:, :HEAD].T,
        log_total,
        cosine,
        sine,
        units,
        expert_count,
    )
    front_back, gate_slabs = hold(front_back, gate_slabs)
    up_slabs = rows_for_owners(up_near + up_got.astype(jnp.float32))
    up_slabs = lax.all_to_all(up_slabs, "dp", 0, 0, tiled=True)
    out_grad = times_rows(grad_hidden_rows, mixed_low)
    grad_norm1 = deliver(times_trans(front_back, front_weights))
    front_grad = times_rows(normed1, front_back)
    grad_field_norm, grad_gain1 = norm_back(field, gains[0], grad_norm1)
    grad_field = grad_hidden1 + grad_field_norm

    def undeal_heads(value):
        halves = value.astype(low).reshape(units, 2, depth // 2, value.shape[1])
        first = lax.dynamic_index_in_dim(halves, plane, 1, keepdims=False)
        second = lax.dynamic_index_in_dim(halves, 1 - plane, 1, keepdims=False)
        first = jnp.where(plane == core, first, lax.ppermute(first, QUAD, DEAL_FIRST))
        both = first.astype(jnp.float32) + lax.ppermute(second, QUAD, BACK_SECOND).astype(
            jnp.float32
        )
        return both.astype(low)

    def gather_heads(value):
        got = value.reshape(2, local_heads, depth // 2, value.shape[2])
        own = lax.dynamic_index_in_dim(got, core, 0, keepdims=False)
        swapped = lax.ppermute(
            lax.dynamic_index_in_dim(got, 1 - core, 0, keepdims=False), "c", swap_pairs(2)
        )
        rows = jnp.concatenate(
            [jnp.where(core == 0, own, swapped), jnp.where(core == 0, swapped, own)], axis=1
        )
        return rows

    middle = hidden // 2
    front_heads = undeal_heads(front_grad)
    front_heads, out_grad, down_sent = hold(front_heads, out_grad, down_sent)
    down_first = across(down_sent[:middle])
    front_heads, up_slabs, down_first = hold(front_heads, up_slabs, down_first)
    out_heads = undeal_heads(out_grad)
    out_heads, down_sent = hold(out_heads, down_sent)
    down_second = across(down_sent[middle:])
    front_heads, out_heads = swap_all(front_heads, out_heads)
    out_heads, grad_field, grad_gain1, down_second = hold(
        out_heads, grad_field, grad_gain1, down_second
    )
    input_grad = from_rows(grad_field)
    out_heads = lax.all_to_all(out_heads, "dp", 0, 0, tiled=True)
    down_got = jnp.concatenate([down_first, down_second], axis=0)
    down_sum = down_near + down_got.astype(jnp.float32)
    grad_gate_out, grad_up_out = own_rows(gate_slabs), own_rows(up_slabs)
    front_out, out_back = gather_heads(front_heads), gather_heads(out_heads)
    grad_out = out_back.reshape(local_heads, depth, expert_count, HEAD).transpose(2, 0, 3, 1)
    grad_query_out = front_out[:, :, :wide].reshape(local_heads, depth, expert_count, HEAD).transpose(2, 1, 0, 3)
    grad_pair = front_out[:, :, wide:].reshape(local_heads, depth, 2, HEAD).transpose(1, 2, 0, 3)
    grad_out, grad_query_out, grad_pair = (
        hold(value)[0].astype(jnp.float32)
        for value in (
            grad_out.reshape(w_out.shape),
            grad_query_out.reshape(w_query.shape),
            grad_pair.reshape(w_keyval.shape),
        )
    )
    totals = jnp.stack([grad_gain1, grad_gain2, jnp.full((width,), squared)])
    for axis, size in (("c", 2), ("y", 2), ("dp", units)):
        reach = 1
        while reach < size:
            totals = totals + lax.ppermute(totals, axis, [(i, i ^ reach) for i in range(size)])
            reach *= 2
    gain_total, squared_total = totals[:2], totals[2, 0]
    return (
        layer_out,
        squared_total / (count * width),
        input_grad,
        gain_total,
        grad_query_out.reshape(w_query.shape),
        grad_out.reshape(w_out.shape),
        grad_pair.reshape(w_keyval.shape),
        grad_gate_out[None],
        grad_up_out[None],
        down_sum[None],
    )


def solution(mesh):
    units, experts = mesh.shape["dp"], mesh.shape["expert"]

    def specs(quad):
        return (
            (
                P(None, "dp", quad),
                P(None, "dp", quad),
                P(None, "dp"),
                P(None, "dp", None),
                P(None, "dp", None),
                P(None, "dp", None),
                P(None, "dp", None),
                P(),
                P(None, "dp", quad),
                P(None, quad, "dp"),
                P("dp", None, quad),
                P(quad, "dp", None),
                P(quad, "dp", None),
                P(quad, "dp", None),
            ),
            (
                P(None, "dp", quad),
                P(),
                P(None, "dp", quad),
                P(),
                P(None, "dp", quad),
                P(None, quad, "dp"),
                P("dp", None, quad),
                P(quad, "dp", None),
                P(quad, "dp", None),
                P(quad, "dp", None),
            ),
        )

    def step(*arguments):
        tokens_in, w_query = arguments[0], arguments[8]
        team = (
            experts == 4
            and tokens_in.shape[0] == 2
            and w_query.shape[2] // HEAD == 2 * units
            and w_query.shape[0] == 4
            and tokens_in.shape[1] == units * 2 * PROMPT_DEV
            and PROMPT_DEV == CLEN == BLOCK
            and units == 2 * LINE
        )
        if team:
            grid = Mesh(mesh.devices.reshape(units, 2, 2), ("dp", "y", "c"))
            ins, outs = specs(QUAD)
            body = team_device
        else:
            grid = mesh
            ins, outs = specs("expert")
            body = per_device
        return jax.shard_map(body, mesh=grid, in_specs=ins, out_specs=outs, check_vma=False)(*arguments)

    return step
```
